256 devices in a mesh: seq: 32 (over z, y_hi, core), tp: 8 (over x, y_lo).
Axes of the slice: x: 4, y: 4 (y_hi: 2, y_lo: 2; y = y_hi * 2 + y_lo), z: 8, core: 2. Of those that a mesh axis runs over, the one named last changes fastest.
Arguments:
- stream: bfloat16 [8192, 2048], P('seq', 'tp'), may hold values from -16 to 16
- frames: int32 [8192], P('seq'), may hold values from 0 to 63, never falling along the last dimension, each value on 1 to 256 neighbouring positions
- fidelity: int32 [8192, 1], P('seq'), may hold values from 0 to 15; in each aligned block of 256 rows (0 to 255, 256 to 511, ...) at most 32 rows name the same one
- w_query: bfloat16 [2048, 2048], P(None, 'tp'), may hold values from -2 to 2
- w_key: bfloat16 [2048, 2048], P(None, 'tp'), may hold values from -2 to 2
- w_value: bfloat16 [2048, 2048], P(None, 'tp'), may hold values from -0.125 to 0.125
- w_output: bfloat16 [2048, 2048], P('tp'), may hold values from -0.125 to 0.125
- norm_gain: float32 [2048], replicated, may hold values from 0.1 to 1.9
- expert_gate: bfloat16 [32, 2048, 2816], P('seq', None, 'tp'), may hold values from -0.125 to 0.125
- expert_up: bfloat16 [32, 2048, 2816], P('seq', None, 'tp'), may hold values from -0.125 to 0.125
- expert_down: bfloat16 [32, 2816, 2048], P('seq', 'tp'), may hold values from -0.078125 to 0.078125
Outputs:
- result: bfloat16 [8192, 2048], P('seq', 'tp')
The draws below stay inside these ranges and needn't reach their ends.
Inputs may be any that keep to these rules, and one draw needn't show every extreme that they name: `frames`: frame numbers never fall along the tokens; a frame holds 1 to 256 tokens, one exactly 256. `fidelity`: among the tokens of one index of seq (aligned blocks of 256 rows) no expert is named more than 32 times, a bound that some block reaches; every expert is named by some token.
All inputs are finite; a program needn't handle non-finite values.
Results may differ from the reference program's by a relative error of at most 0.02.
Values may be sent and summed in bfloat16 or wider, within the bound.
No kernel may reach another device: no remote copies, remote signals or barrier semaphores. Data moves between devices by JAX's collectives and lax.ppermute only.
A program may use at most 128 MiB of HBM per device.

```python
import math
import jax
import jax.numpy as jnp
import numpy as np
from jax import lax

D = 2048
HEADS = 16
HEAD = 128
QW = 2048
FF = 5632
EXPERTS = 16
TOK_DEV = 256
TOKENS = 8192
CAP = 32
RSPLIT = 2
FFB = 2816
FRAMES = 64
FRAME_MOST = 256
N_SEQ = 32
N_TP = 8


def projection_pair(key):
    query_part = jnp.clip(jax.random.normal(jax.random.fold_in(key, 11), (D, QW), jnp.float32), -6.0, 6.0) / math.sqrt(D)
    other_part = jnp.clip(jax.random.normal(jax.random.fold_in(key, 12), (D, QW), jnp.float32), -6.0, 6.0) / math.sqrt(D)
    return (query_part, other_part)


def draw_w_query(key, part):
    return projection_pair(key)[0].astype(jnp.bfloat16)


def draw_w_key(key, part):
    query_part, other_part = projection_pair(key)
    return other_part.astype(jnp.bfloat16)


def draw_stream(key, part):
    return jnp.clip(jax.random.normal(key, (TOKENS, D), jnp.float32), -6.0, 6.0).astype(jnp.bfloat16)


def level_of(stream_key, dims, cuts, smallest, top_value):
    gain = 1.0
    for position, shards_of in cuts:
        heights = jax.random.uniform(jax.random.fold_in(jax.random.fold_in(stream_key, 6), position), (shards_of,), jnp.float32, smallest / len(cuts), top_value / len(cuts))
        gain = gain * jnp.repeat(jnp.exp(heights), dims[position] // shards_of).reshape((-1,) + (1,) * (len(dims) - 1 - position))
    return gain


def profile(count, total, most, slope):
    weights = [(1 << 20) // math.isqrt(rank ** slope) + 1 for rank in range(2, count + 1)]
    spare, holding = total - most - (count - 1), [1] * (count - 1)
    while spare > 0:
        candidates = [i for i in range(count - 1) if holding[i] < most]
        mass, remaining = sum([weights[i] for i in candidates]), spare
        for i in candidates:
            addition = min(most - holding[i], max(1, remaining * weights[i] // mass), spare)
            holding[i] = holding[i] + addition
            spare = spare - addition
    return np.array([most] + holding)


def ragged(key, amount, total, bound, lean):
    if amount == 2:
        one = jax.random.randint(key, (), max(1, total - bound), min(bound, total - 1) + 1)
        return jnp.stack([one, total - one])
    sizes = jnp.asarray(profile(amount, total, bound, lean), jnp.int32)
    couples = (amount - 1) // 2
    giver, receiver = sizes[1:1 + 2 * couples:2], sizes[2:2 + 2 * couples:2]
    slack = jnp.minimum(giver - 1, bound - receiver)
    passed = jax.random.randint(jax.random.fold_in(key, 1), (couples,), 0, 1 << 20) % (slack + 1)
    sizes = sizes.at[1:1 + 2 * couples:2].set(giver - passed).at[2:2 + 2 * couples:2].set(receiver + passed)
    return sizes[jax.random.permutation(jax.random.fold_in(key, 2), amount)]


def deal_out(stream_key, own, number, rows, amount, top, reach, slope):
    ranking = jax.random.permutation(stream_key, amount)
    heavy_load, common = load_shares(amount, rows * top, reach, slope, True), load_shares(amount, rows * top, reach, slope, False)
    places = jnp.arange(amount)

    def named(tallies, rotation):
        used = int((tallies > 0).sum())
        fixed = max(1, used // 4)
        shifted = fixed + (places - fixed + rotation * (used - fixed)) % max(1, amount - fixed)
        return jnp.zeros((amount,), jnp.int32).at[ranking[jnp.where(places < fixed, places, shifted)]].set(jnp.asarray(tallies, jnp.int32))

    tallies = jnp.where(number % 4 == 0, named(heavy_load, number // 4), named(common, number - number // 4 - 1))
    mixed = jax.random.permutation(jax.random.fold_in(own, 3), amount)
    donor, taker = mixed[0:amount // 2 * 2:2], mixed[1:amount // 2 * 2:2]
    slack = jnp.minimum(tallies[donor] - 1, reach - tallies[taker]) // 2
    slack = jnp.where((donor == ranking[0]) | (taker == ranking[0]) | (tallies[taker] == 0), 0, jnp.maximum(slack, 0))
    shifted = jax.random.randint(jax.random.fold_in(own, 4), (amount // 2,), 0, 1 << 20) % (slack + 1)
    tallies = tallies.at[donor].add(-shifted).at[taker].add(shifted)
    labels = jnp.searchsorted(jnp.cumsum(tallies), jnp.arange(rows * top), side="right").astype(jnp.int32)
    table = labels.reshape(top, rows).T
    table = table[jax.random.permutation(jax.random.fold_in(own, 1), rows)]
    rotation = jax.random.randint(jax.random.fold_in(own, 2), (rows, 1), 0, top)
    return jnp.take_along_axis(table, (jnp.arange(top)[None, :] + rotation) % top, axis=1)


def load_shares(count, total, limit, skew, full):
    loads = [(1 << 20) // math.isqrt(standing ** skew) + 1 for standing in range(1, count + 1)]
    largest = limit if full else min(limit, max(-(-total // count), total * loads[0] // sum(loads)))
    least = 1 if total - largest >= count - 1 else 0
    counts, spare = [largest] + [least] * (count - 1), total - largest - least * (count - 1)
    while spare > 0:
        candidates = [i for i in range(1, count) if counts[i] < largest] or [i for i in range(1, count) if counts[i] < limit]
        pool, left = sum([loads[i] for i in candidates]), spare
        for i in candidates:
            extra = min(limit - counts[i], max(1, left * loads[i] // pool), spare)
            counts[i] = counts[i] + extra
            spare = spare - extra
    return np.array(counts)


def normal_values(key, dims, width, reach, cuts=(), kind=jnp.bfloat16):
    loudness = level_of(key, dims, cuts, -0.22, 0.18) if cuts else 1.0
    result = jax.random.normal(key, dims, jnp.float32) * width * loudness
    return jnp.minimum(jnp.maximum(result, -reach), reach).astype(kind)


def setup_inputs(seed: int = 0) -> dict:
    arg_keys = jax.random.split(jax.random.key(seed), 12)
    stream = draw_stream(jax.random.fold_in(arg_keys[11], 71), 0)
    frames = jnp.searchsorted(jnp.cumsum(ragged(arg_keys[1], FRAMES, TOKENS, FRAME_MOST, 1)), jnp.arange(TOKENS), side="right").astype(jnp.int32)
    fidelity_keys = jax.random.split(jax.random.fold_in(arg_keys[2], 1), TOKENS // TOK_DEV)
    fidelity_turns = jax.random.permutation(jax.random.fold_in(arg_keys[2], 3), TOKENS // TOK_DEV)
    fidelity = jax.vmap(lambda own, number: deal_out(jax.random.fold_in(arg_keys[2], 2), own, number, TOK_DEV, EXPERTS, 1, CAP, 2))(fidelity_keys, fidelity_turns).reshape((TOKENS, 1))
    w_query = draw_w_query(jax.random.fold_in(arg_keys[11], 71), 0)
    w_key = draw_w_key(jax.random.fold_in(arg_keys[11], 71), 0)
    w_value = normal_values(arg_keys[5], (D, QW), D ** -0.5, 0.125, ((1, 8),))
    w_output = normal_values(arg_keys[6], (QW, D), QW ** -0.5, 0.125, ((0, 8),))
    norm_gain = jnp.clip(1.0 + 0.18 * jax.random.normal(arg_keys[7], (D,), jnp.float32), 0.1, 1.9)
    expert_gate = normal_values(arg_keys[8], (EXPERTS * RSPLIT, D, FFB), D ** -0.5, 0.125, ((0, 32), (2, 8)))
    expert_up = normal_values(arg_keys[9], (EXPERTS * RSPLIT, D, FFB), D ** -0.5, 0.125, ((0, 32), (2, 8)))
    expert_down = normal_values(arg_keys[10], (EXPERTS * RSPLIT, FFB, D), FF ** -0.5, 0.078125, ((0, 32), (1, 8)))
    return {"stream": stream, "frames": frames, "fidelity": fidelity, "w_query": w_query, "w_key": w_key, "w_value": w_value, "w_output": w_output, "norm_gain": norm_gain, "expert_gate": expert_gate, "expert_up": expert_up, "expert_down": expert_down}


def project(rows_in, weight):
    return jnp.dot(rows_in, weight, preferred_element_type=jnp.float32).astype(jnp.bfloat16)

def slot_rows(route_ids):
    onehot = (route_ids[:, None] == jnp.arange(EXPERTS, dtype=jnp.int32)[None, :]).astype(jnp.int32)
    places = lax.optimization_barrier(jnp.sum(onehot * (jnp.cumsum(onehot, axis=0) - 1), axis=1)).astype(jnp.int32)
    flat_slot = (route_ids * CAP + places).astype(jnp.int32)
    owner_table = jnp.full((EXPERTS * CAP,), TOK_DEV, jnp.int32).at[flat_slot].set(jnp.arange(TOK_DEV, dtype=jnp.int32))
    return (flat_slot, owner_table)

def reference(stream, frames, fidelity, w_query, w_key, w_value, w_output, norm_gain, expert_gate, expert_up, expert_down):
    query_rows = project(stream, w_query)
    key_rows = project(stream, w_key)
    value_rows = project(stream, w_value)
    score_scale = 1.0 / math.sqrt(HEAD)
    key_all = key_rows.astype(jnp.float32).reshape(TOKENS, HEADS, HEAD)
    value_all = value_rows.astype(jnp.float32).reshape(TOKENS, HEADS, HEAD)
    block_rows = math.gcd(TOKENS, 512)
    query_blocks = query_rows.reshape(TOKENS // block_rows, block_rows, HEADS, HEAD)
    frame_blocks = frames.reshape(TOKENS // block_rows, block_rows)

    def attend_block(inputs):
        query_part, frame_part = inputs
        scores = jnp.einsum('qhd,khd->hqk', query_part.astype(jnp.float32), key_all) * score_scale
        allowed = frames[None, None, :] <= frame_part[None, :, None]
        scores = jnp.where(allowed, scores, -jnp.inf)
        row_top = lax.optimization_barrier(jnp.max(scores, axis=2, keepdims=True))
        weights = jnp.where(allowed, jnp.exp(scores - row_top), 0.0)
        totals = lax.optimization_barrier(jnp.sum(weights, axis=2))
        rounded = lax.optimization_barrier(weights.astype(jnp.bfloat16)).astype(jnp.float32)
        weighted = jnp.einsum('hqk,khd->qhd', rounded, value_all)
        return (weighted / jnp.transpose(totals)[:, :, None]).reshape(block_rows, QW).astype(jnp.bfloat16)
    attended = lax.map(attend_block, (query_blocks, frame_blocks)).reshape(TOKENS, QW)
    mixed = (stream.astype(jnp.float32) + jnp.dot(attended, w_output, preferred_element_type=jnp.float32)).astype(jnp.bfloat16)
    mixed_float = mixed.astype(jnp.float32)
    normed = (mixed_float * lax.rsqrt(lax.optimization_barrier(jnp.mean(mixed_float * mixed_float, axis=1, keepdims=True)) + 1e-05) * norm_gain[None, :]).astype(jnp.bfloat16)
    route_ids = fidelity[:, 0].reshape(N_SEQ, TOK_DEV).astype(jnp.int32)
    flat_slots, owner_tables = jax.vmap(slot_rows)(route_ids)
    padded = jnp.concatenate([normed.reshape(N_SEQ, TOK_DEV, D), jnp.zeros((N_SEQ, 1, D), jnp.bfloat16)], axis=1)
    dispatched = jax.vmap(lambda source, index: jnp.take(source, index, axis=0))(padded, owner_tables)
    per_expert = jnp.transpose(dispatched.reshape(N_SEQ, EXPERTS, CAP, D), (1, 0, 2, 3)).reshape(EXPERTS, N_SEQ * CAP, D)
    gate_blocks = expert_gate.reshape(EXPERTS, RSPLIT, D, FFB)
    up_blocks = expert_up.reshape(EXPERTS, RSPLIT, D, FFB)
    down_blocks = expert_down.reshape(EXPERTS, RSPLIT, FFB, D)
    group = FFB // N_TP

    def one_expert(inputs):
        expert_rows, gate_set, up_set, down_set = inputs

        def one_block(inner):
            gate_weight, up_weight, down_weight = inner
            gate_act = jnp.dot(expert_rows, gate_weight, preferred_element_type=jnp.float32)
            up_act = jnp.dot(expert_rows, up_weight, preferred_element_type=jnp.float32)
            hidden = (jax.nn.silu(gate_act) * up_act).astype(jnp.bfloat16)
            pieces = jnp.einsum('rtf,tfd->trd', hidden.reshape(-1, N_TP, group).astype(jnp.float32), down_weight.reshape(N_TP, group, D).astype(jnp.float32))
            pieces = lax.optimization_barrier(pieces.astype(jnp.bfloat16)).astype(jnp.float32)
            summed = lax.optimization_barrier(lax.optimization_barrier(jnp.sum(pieces, axis=0)).astype(jnp.bfloat16))
            return summed.astype(jnp.float32)
        return lax.optimization_barrier(jnp.sum(lax.map(one_block, (gate_set, up_set, down_set)), axis=0))
    expert_out = lax.map(one_expert, (per_expert, gate_blocks, up_blocks, down_blocks))
    returned = jnp.transpose(expert_out.reshape(EXPERTS, N_SEQ, CAP, D), (1, 0, 2, 3)).reshape(N_SEQ, EXPERTS * CAP, D)
    own_rows = jax.vmap(lambda source, index: jnp.take(source, index, axis=0))(returned, flat_slots).reshape(TOKENS, D)
    return (mixed_float + own_rows).astype(jnp.bfloat16)
```

```python
import math

import jax
import jax.numpy as jnp
import numpy as np
from jax import lax
from jax.experimental import pallas as pl
from jax.experimental.pallas import tpu as pltpu
from jax.sharding import Mesh, PartitionSpec as P

HEAD = 128
EXPERTS = 16
CAP = 32
BLK = 256
NEG = -1e30
NORM_EPS = 1e-05
SEQ = ("z", "yh", "c")
CHIPS = ("z", "yh")
TP = ("x", "yl")
F32 = jnp.float32
BF16 = jnp.bfloat16

VMEM = pl.BlockSpec(memory_space=pltpu.VMEM)
SMEM = pl.BlockSpec(memory_space=pltpu.SMEM)


def nt_dot(a, b):
    return lax.dot_general(a, b, (((1,), (1,)), ((), ())), preferred_element_type=F32)


def tn_dot(a, b):
    return lax.dot_general(a, b, (((0,), (0,)), ((), ())), preferred_element_type=F32)


def qkv_kernel(info, *refs):
    blocks = refs[:8]
    wq, wk, wv, ends, kv_own, pack_c, q_own, pack_yc = refs[8:]
    first = info[8] == 0

    def project(w):
        total = None
        for j in range(8):
            rows = pl.ds(pl.multiple_of(info[j] * BLK, BLK), BLK)
            term = jnp.dot(blocks[j][...], w[rows, :], preferred_element_type=F32)
            total = term if total is None else total + term
        left, right = total[:, :HEAD], total[:, HEAD:]
        mine = jnp.where(first, left, right).astype(BF16)
        other = jnp.where(first, right, left).astype(BF16)
        return mine, other

    mine, other = project(wk)
    kv_own[:, :HEAD] = mine
    pack_c[:BLK, HEAD : 2 * HEAD] = other
    mine, other = project(wv)
    kv_own[:, HEAD:] = mine
    pack_c[:BLK, 2 * HEAD :] = other
    mine, other = project(wq)
    q_own[:BLK, :] = mine
    pack_c[:BLK, :HEAD] = other
    pack_yc[:BLK, :] = other
    tail = ends[...]
    q_own[BLK:, :] = tail
    pack_yc[BLK:, :] = tail
    pack_c[BLK:, :HEAD] = tail
    pack_c[BLK:, HEAD : 2 * HEAD] = tail
    pack_c[BLK:, 2 * HEAD :] = tail


def qkv(info, blocks, wq, wk, wv, ends):
    return pl.pallas_call(
        qkv_kernel,
        out_shape=(
            jax.ShapeDtypeStruct((BLK, 2 * HEAD), BF16),
            jax.ShapeDtypeStruct((BLK + 16, 3 * HEAD), BF16),
            jax.ShapeDtypeStruct((BLK + 16, HEAD), BF16),
            jax.ShapeDtypeStruct((BLK + 16, HEAD), BF16),
        ),
        in_specs=[SMEM] + [VMEM] * 12,
        out_specs=(VMEM,) * 4,
        cost_estimate=pl.CostEstimate(
            flops=2 * BLK * 2048 * 768, bytes_accessed=5 << 20, transcendentals=0
        ),
        name="qkv",
    )(info, *blocks, wq, wk, wv, ends)


def attend_kernel(info, q0, q1, q2, q3, kv, out, q_s, end_s, m_s, l_s, acc_s):
    z = info[0]
    scale = 1.0 / math.sqrt(HEAD)
    for g, q in enumerate((q0, q1, q2, q3)):
        cols = slice(g * BLK, (g + 1) * BLK)
        q_s[cols, :] = q[:BLK, :HEAD]
        for half in range(2):
            line = q[BLK + half : BLK + half + 1, :HEAD].astype(F32)
            lanes = slice(g * BLK + half * HEAD, g * BLK + (half + 1) * HEAD)
            end_s[:, lanes] = line.astype(jnp.int32) + BLK * (info[1 + g] + 1)
    m_s[...] = jnp.full_like(m_s, NEG)
    l_s[...] = jnp.zeros_like(l_s)
    acc_s[...] = jnp.zeros_like(acc_s)

    def visit(zk, masked):
        keys = kv[zk, :, :HEAD]
        values = kv[zk, :, HEAD:]
        for part in range(2):
            lanes = slice(part * 2 * BLK, (part + 1) * 2 * BLK)
            s = nt_dot(keys, q_s[lanes, :]) * scale
            old = m_s[:, lanes]
            if masked:
                row = lax.broadcasted_iota(jnp.int32, s.shape, 0)
                base = jnp.where(row < BLK, info[5] + 4 * zk, info[6] + 4 * zk - 1) * BLK
                ok = row + base < end_s[:, lanes]
                s = jnp.where(ok, s, NEG)
            top = jnp.maximum(old, jnp.max(s, axis=0, keepdims=True))
            p = jnp.exp(s - top)
            if masked:
                p = jnp.where(ok, p, 0.0)
            decay = jnp.exp(old - top)
            m_s[:, lanes] = top
            l_s[:, lanes] = l_s[:, lanes] * decay + jnp.sum(p, axis=0, keepdims=True)
            acc_s[:, lanes] = acc_s[:, lanes] * decay + tn_dot(values, p.astype(BF16))

    visit(z, True)

    def body(zk, carry):
        visit(zk, False)
        return carry

    lax.fori_loop(0, z, body, 0)

    @pl.when((z < 7) & (info[7] == 0))
    def _():
        visit(z + 1, True)

    for g in range(4):
        lanes = slice(g * BLK, (g + 1) * BLK)
        total = l_s[:, lanes]
        some = total > 0.0
        safe = jnp.where(some, total, 1.0)
        out[g, :HEAD, :] = acc_s[:, lanes] / safe
        lse = jnp.where(some, m_s[:, lanes] + jnp.log(safe), NEG)
        out[g, HEAD:, :] = jnp.broadcast_to(lse, (8, BLK))


def attend(info, q0, q1, q2, q3, kv):
    return pl.pallas_call(
        attend_kernel,
        out_shape=jax.ShapeDtypeStruct((4, HEAD + 8, BLK), F32),
        in_specs=[SMEM] + [VMEM] * 5,
        out_specs=VMEM,
        scratch_shapes=[
            pltpu.VMEM((4 * BLK, HEAD), BF16),
            pltpu.VMEM((1, 4 * BLK), jnp.int32),
            pltpu.VMEM((1, 4 * BLK), F32),
            pltpu.VMEM((1, 4 * BLK), F32),
            pltpu.VMEM((HEAD, 4 * BLK), F32),
        ],
        cost_estimate=pl.CostEstimate(
            flops=4 * 1024 * 4096 * HEAD, bytes_accessed=3 << 20, transcendentals=1024 * 4096
        ),
        name="attend",
    )(info, q0, q1, q2, q3, kv)


def merge_kernel(info, a0, a1, b0, b1, w, out):
    c = info[0]

    def merged(a, b):
        la, lb = a[HEAD : HEAD + 1, :], b[HEAD : HEAD + 1, :]
        top = jnp.maximum(la, lb)
        wa, wb = jnp.exp(la - top), jnp.exp(lb - top)
        inv = 1.0 / (wa + wb)
        return (a[:HEAD, :] * (wa * inv) + b[:HEAD, :] * (wb * inv)).astype(BF16)

    mine, other = merged(a0, a1), merged(b0, b1)
    rows_mine = pl.ds(pl.multiple_of(c * HEAD, HEAD), HEAD)
    rows_other = pl.ds(pl.multiple_of((1 - c) * HEAD, HEAD), HEAD)
    for t in range(8):
        cols = slice(t * BLK, (t + 1) * BLK)
        out[t] = (tn_dot(mine, w[rows_mine, cols]) + tn_dot(other, w[rows_other, cols])).astype(BF16)


def merge(info, a0, a1, b0, b1, w):
    return pl.pallas_call(
        merge_kernel,
        out_shape=jax.ShapeDtypeStruct((8, BLK, BLK), BF16),
        in_specs=[SMEM] + [VMEM] * 5,
        out_specs=VMEM,
        cost_estimate=pl.CostEstimate(
            flops=2 * BLK * BLK * 2048, bytes_accessed=3 << 20, transcendentals=1024
        ),
        name="merge",
    )(info, a0, a1, b0, b1, w)


def slots_kernel(parts, stream, slot, mixed, rows):
    total = stream[...].astype(F32) + jnp.sum(parts[...].astype(F32), axis=0)
    kept = total.astype(BF16)
    mixed[...] = kept
    ids = lax.broadcasted_iota(jnp.int32, (EXPERTS * CAP, BLK), 0)
    pick = jnp.where(ids == slot[...], 1.0, 0.0).astype(BF16)
    rows[...] = jnp.dot(pick, kept, preferred_element_type=F32).astype(BF16)


def to_slots(parts, stream, slot):
    return pl.pallas_call(
        slots_kernel,
        out_shape=(
            jax.ShapeDtypeStruct((BLK, BLK), BF16),
            jax.ShapeDtypeStruct((EXPERTS * CAP, BLK), BF16),
        ),
        in_specs=[VMEM] * 3,
        out_specs=(VMEM, VMEM),
        cost_estimate=pl.CostEstimate(
            flops=2 * 512 * BLK * BLK, bytes_accessed=2 << 20, transcendentals=0
        ),
        name="slots",
    )(parts, stream, slot)


def expert_kernel(x, gain, gate, up, down, out, n_s):
    square = None
    for t in range(8):
        v = x[0, t].astype(F32)
        term = jnp.sum(v * v, axis=1, keepdims=True)
        square = term if square is None else square + term
    inv = lax.rsqrt(square * (1.0 / 2048) + NORM_EPS)
    for t in range(8):
        cols = slice(t * BLK, (t + 1) * BLK)
        n_s[:, cols] = (x[0, t].astype(F32) * inv * gain[:, cols]).astype(BF16)
    g = nt_dot(n_s[...], gate[...])
    u = nt_dot(n_s[...], up[...])
    hidden = (g / (1.0 + jnp.exp(-g)) * u).astype(BF16)
    for t in range(8):
        cols = slice(t * BLK, (t + 1) * BLK)
        out[0, t] = jnp.dot(hidden, down[:, cols], preferred_element_type=F32).astype(BF16)


def expert(x, gain, gate, up, down):
    rows = 256
    units = gate.shape[0]
    whole = lambda i, j: (0, 0)
    return pl.pallas_call(
        expert_kernel,
        out_shape=jax.ShapeDtypeStruct(x.shape, BF16),
        grid=(2, x.shape[2] // rows),
        in_specs=[
            pl.BlockSpec((1, 8, rows, BLK), lambda i, j: (i, 0, j, 0)),
            pl.BlockSpec((1, 2048), whole),
            pl.BlockSpec((units, 2048), whole),
            pl.BlockSpec((units, 2048), whole),
            pl.BlockSpec((units, 2048), whole),
        ],
        out_specs=pl.BlockSpec((1, 8, rows, BLK), lambda i, j: (i, 0, j, 0)),
        scratch_shapes=[pltpu.VMEM((rows, 2048), BF16)],
        cost_estimate=pl.CostEstimate(
            flops=6 * 1024 * 2048 * units, bytes_accessed=13 << 20, transcendentals=1024 * units
        ),
        name="expert",
    )(x, gain, gate, up, down)


def finish_kernel(mixed, rows, slot, out):
    ids = lax.broadcasted_iota(jnp.int32, (EXPERTS * CAP, BLK), 0)
    pick = jnp.where(ids == slot[...], 1.0, 0.0).astype(BF16)
    out[...] = (mixed[...].astype(F32) + tn_dot(pick, rows[...])).astype(BF16)


def finish(mixed, rows, slot):
    return pl.pallas_call(
        finish_kernel,
        out_shape=jax.ShapeDtypeStruct((BLK, BLK), BF16),
        in_specs=[VMEM] * 3,
        out_specs=VMEM,
        cost_estimate=pl.CostEstimate(
            flops=2 * 512 * BLK * BLK, bytes_accessed=1 << 20, transcendentals=0
        ),
        name="finish",
    )(mixed, rows, slot)


def tp_shift(a, dx, dy):
    pairs = [(i * 2 + j, ((i + dx) % 4) * 2 + (j + dy) % 2) for i in range(4) for j in range(2)]
    return lax.ppermute(a, TP, pairs)


def swap(a, dy, dc):
    pairs = [(i * 2 + j, (i ^ dy) * 2 + (j ^ dc)) for i in range(2) for j in range(2)]
    return lax.ppermute(a, ("yh", "c"), pairs)


def shards(stream, frames, fidelity, wq, wk, wv, wo, gain, gate, up, down):
    z, yh, c = (lax.axis_index(a) for a in SEQ)
    x, yl = (lax.axis_index(a) for a in TP)

    shifts = [(dx, dy) for dx in range(4) for dy in range(2)]
    blocks = [stream if s == (0, 0) else tp_shift(stream, *s) for s in shifts]
    sources = [((x - dx) % 4) * 2 + (yl - dy) % 2 for dx, dy in shifts]

    follow = lax.ppermute(frames, SEQ, [((i + 1) % 32, i) for i in range(32)])
    last = (z == 7) & (yh == 1) & (c == 1)
    here = jnp.sum((frames[None, :] <= frames[:, None]).astype(jnp.int32), axis=1)
    after = jnp.sum((follow[None, :] <= frames[:, None]).astype(jnp.int32), axis=1)
    ends = here + jnp.where(last, 0, after) - BLK
    ends = jnp.pad(ends.reshape(2, HEAD), ((0, 14), (0, 0))).astype(BF16)

    route = fidelity[:, 0]
    spot = lax.iota(jnp.int32, BLK)
    same = (route[:, None] == route[None, :]) & (spot[None, :] < spot[:, None])
    slot = (route * CAP + jnp.sum(same.astype(jnp.int32), axis=1))[None, :]

    info = jnp.stack(sources + [c]).astype(jnp.int32)
    kv_own, pack_c, q_own, pack_yc = qkv(info, blocks, wq, wk, wv, ends)
    from_c = swap(pack_c, 0, 1)
    from_y = swap(q_own, 1, 0)
    from_yc = swap(pack_yc, 1, 1)
    kv = jnp.concatenate([kv_own, from_c[:BLK, HEAD:]], axis=0)
    kv = lax.all_gather(kv, "z", axis=0)

    block = lambda a, b: z * 4 + a * 2 + b
    info = jnp.stack(
        [z, block(yh, c), block(yh, 1 - c), block(1 - yh, c), block(1 - yh, 1 - c), yh * 2 + c, yh * 2 + 1 - c, yh]
    ).astype(jnp.int32)
    partial = attend(info, q_own, from_c, from_y, from_yc, kv)
    b0 = swap(partial[1], 0, 1)
    a1 = swap(partial[2], 1, 0)
    b1 = swap(partial[3], 1, 1)
    projected = merge(c.astype(jnp.int32)[None], partial[0], a1, b0, b1, wo)
    parts = lax.all_to_all(projected, TP, 0, 0, tiled=True)
    mixed, rows = to_slots(parts, stream, slot)

    sent = lax.all_to_all(rows.reshape(EXPERTS, CAP, BLK), CHIPS, 0, 0, tiled=True)
    full = lax.all_gather(sent.reshape(EXPERTS * CAP, BLK), ("c",) + TP, axis=0)
    full = full.reshape(2, 8, EXPERTS * CAP, BLK)
    lowered = expert(full, gain[None, :], gate[0].T, up[0].T, down[0])
    kept = lax.dynamic_index_in_dim(lowered, c, 0, keepdims=False)
    given = lax.dynamic_index_in_dim(lowered, 1 - c, 0, keepdims=False)
    taken = lax.ppermute(given, "c", [(0, 1), (1, 0)])
    pair = (kept.astype(F32) + taken.astype(F32)).astype(BF16)
    pieces = lax.all_to_all(pair, TP, 0, 0, tiled=True)
    summed = jnp.sum(pieces.astype(F32), axis=0).astype(BF16)
    back = lax.all_to_all(summed.reshape(EXPERTS, CAP, BLK), CHIPS, 0, 0, tiled=True)
    return finish(mixed, back.reshape(EXPERTS * CAP, BLK), slot)


def solution(mesh):
    axes = ("z", "yh", "c", "x", "yl")
    fine = Mesh(np.asarray(mesh.devices).reshape(8, 2, 2, 4, 2), axes)
    return jax.shard_map(
        shards,
        mesh=fine,
        in_specs=(
            P(SEQ, TP),
            P(SEQ),
            P(SEQ, None),
            P(None, TP),
            P(None, TP),
            P(None, TP),
            P(TP, None),
            P(),
            P(SEQ, None, TP),
            P(SEQ, None, TP),
            P(SEQ, TP, None),
        ),
        out_specs=P(SEQ, TP),
        check_vma=False,
    )
```

```python
import functools
import math

import jax
import jax.numpy as jnp
import numpy as np
from jax import lax
from jax.experimental import pallas as pl
from jax.experimental.pallas import tpu as pltpu
from jax.sharding import Mesh, PartitionSpec as P

HEAD = 128
EXPERTS = 16
CAP = 32
BLK = 256
NEG = -1e30
NORM_EPS = 1e-05
SEQ = ("z", "yh", "c")
CHIPS = ("z", "yh")
TP = ("x", "yl")
SHIFTS = [(dx, dy) for dx in range(4) for dy in range(2)]
F32 = jnp.float32
BF16 = jnp.bfloat16

VMEM = pl.BlockSpec(memory_space=pltpu.VMEM)
SMEM = pl.BlockSpec(memory_space=pltpu.SMEM)


def nt_dot(a, b):
    return lax.dot_general(a, b, (((1,), (1,)), ((), ())), preferred_element_type=F32)


def tn_dot(a, b):
    return lax.dot_general(a, b, (((0,), (0,)), ((), ())), preferred_element_type=F32)


def qkv_kernel(*refs):
    blocks = refs[:8]
    wq, wk, wv, frames, kv_own, kv_c, q_own, q_c = refs[8:]
    first = lax.axis_index("c") == 0
    x, yl = lax.axis_index("x"), lax.axis_index("yl")

    def project(w):
        total = None
        for j, (dx, dy) in enumerate(SHIFTS):
            source = ((x + 4 - dx) % 4) * 2 + (yl + dy) % 2
            rows = pl.ds(pl.multiple_of(source * BLK, BLK), BLK)
            term = jnp.dot(blocks[j][...], w[rows, :], preferred_element_type=F32)
            total = term if total is None else total + term
        left, right = total[:, :HEAD], total[:, HEAD:]
        mine = jnp.where(first, left, right).astype(BF16)
        other = jnp.where(first, right, left).astype(BF16)
        return mine, other

    tail = jnp.broadcast_to(frames[...], (16, BLK)).astype(BF16)
    kv_own[:BLK, :HEAD], kv_c[:BLK, :HEAD] = project(wk)
    kv_own[:BLK, HEAD:], kv_c[:BLK, HEAD:] = project(wv)
    kv_own[BLK:, :] = tail
    kv_c[BLK:, :] = tail
    q_own[:BLK, :], q_c[:BLK, :] = project(wq)
    for q in (q_own, q_c):
        q[BLK : BLK + 16, :] = tail[:, :HEAD]
        q[BLK + 16 :, :] = tail[:, HEAD:]


def qkv(blocks, wq, wk, wv, frames):
    kv = jax.ShapeDtypeStruct((BLK + 16, 2 * HEAD), BF16)
    q = jax.ShapeDtypeStruct((BLK + 32, HEAD), BF16)
    return pl.pallas_call(
        qkv_kernel,
        out_shape=(kv, kv, q, q),
        in_specs=[VMEM] * 12,
        out_specs=(VMEM,) * 4,
        cost_estimate=pl.CostEstimate(
            flops=2 * BLK * 2048 * 768, bytes_accessed=5 << 20, transcendentals=0
        ),
        name="qkv",
    )(*blocks, wq, wk, wv, frames)


def visit(q_s, f_s, m_s, l_s, acc_s, pair, masked):
    scale = 1.0 / math.sqrt(HEAD)

    def columns():
        lines = [jnp.broadcast_to(kv[BLK : BLK + 1, :].astype(F32), (HEAD, BLK)) for kv in pair]
        return [jnp.transpose(line)[:, :1] for line in lines]

    key_frames = columns() if masked else None

    def part(i, carry):
        lanes = pl.ds(pl.multiple_of(i * BLK, BLK), BLK)
        old = m_s[:, lanes]
        top, scores, allowed = old, [], []
        for j, kv in enumerate(pair):
            s = nt_dot(kv[:BLK, :HEAD], q_s[lanes, :]) * scale
            if masked:
                ok = key_frames[j] <= f_s[:, lanes]
                s = jnp.where(ok, s, NEG)
                allowed.append(ok)
            scores.append(s)
            top = jnp.maximum(top, jnp.max(s, axis=0, keepdims=True))
        decay = jnp.exp(old - top)
        total, acc = l_s[:, lanes] * decay, acc_s[:, lanes] * decay
        for j, kv in enumerate(pair):
            p = jnp.exp(scores[j] - top)
            if masked:
                p = jnp.where(allowed[j], p, 0.0)
            total = total + jnp.sum(p, axis=0, keepdims=True)
            acc = acc + tn_dot(kv[:BLK, HEAD:], p.astype(BF16))
        m_s[:, lanes], l_s[:, lanes], acc_s[:, lanes] = top, total, acc
        return carry

    lax.fori_loop(0, 4, part, 0)


def local_kernel(q0, q1, q2, q3, kv_a, kv_b, q_s, f_s, m_s, l_s, acc_s):
    for g, q in enumerate((q0, q1, q2, q3)):
        q_s[g * BLK : (g + 1) * BLK, :] = q[:BLK, :]
        for half in range(2):
            lanes = slice(g * BLK + half * HEAD, g * BLK + (half + 1) * HEAD)
            f_s[:, lanes] = q[BLK + 16 * half : BLK + 16 * half + 1, :].astype(F32)
    m_s[...] = jnp.full_like(m_s, NEG)
    l_s[...] = jnp.zeros_like(l_s)
    acc_s[...] = jnp.zeros_like(acc_s)
    visit(q_s, f_s, m_s, l_s, acc_s, (kv_a, kv_b), True)


STATE = (
    jax.ShapeDtypeStruct((4 * BLK, HEAD), BF16),
    jax.ShapeDtypeStruct((1, 4 * BLK), F32),
    jax.ShapeDtypeStruct((1, 4 * BLK), F32),
    jax.ShapeDtypeStruct((1, 4 * BLK), F32),
    jax.ShapeDtypeStruct((HEAD, 4 * BLK), F32),
)


def visit_cost(blocks):
    work = 1024 * BLK * blocks
    return pl.CostEstimate(flops=4 * work * HEAD, bytes_accessed=2 << 20, transcendentals=work)


def local(q0, q1, q2, q3, kv_a, kv_b):
    return pl.pallas_call(
        local_kernel,
        out_shape=STATE,
        in_specs=[VMEM] * 6,
        out_specs=(VMEM,) * 5,
        cost_estimate=visit_cost(4),
        name="local",
    )(q0, q1, q2, q3, kv_a, kv_b)


def step_kernel(k, q_s, f_s, m_i, l_i, acc_i, fa, fb, ba, bb, m_s, l_s, acc_s):
    z = lax.axis_index("z")
    m_s[...] = m_i[...]
    l_s[...] = l_i[...]
    acc_s[...] = acc_i[...]

    @pl.when(z >= k)
    def _():
        visit(q_s, f_s, m_s, l_s, acc_s, (fa, fb), False)

    @pl.when(z + k >= 8)
    def _():
        visit(q_s, f_s, m_s, l_s, acc_s, (ba, bb), False)

    if k == 1:

        @pl.when((z < 7) & (lax.axis_index("yh") == 0))
        def _():
            visit(q_s, f_s, m_s, l_s, acc_s, (ba, bb), True)


def step(k, state, fa, fb, ba, bb):
    m, l, acc = pl.pallas_call(
        functools.partial(step_kernel, k),
        out_shape=STATE[2:],
        in_specs=[VMEM] * 9,
        out_specs=(VMEM,) * 3,
        cost_estimate=visit_cost(4),
        name="step",
    )(*state, fa, fb, ba, bb)
    return state[0], state[1], m, l, acc


def last_kernel(q_s, f_s, m_i, l_i, acc_i, a, b, o0, o1, o2, o3, m_s, l_s, acc_s):
    m_s[...] = m_i[...]
    l_s[...] = l_i[...]
    acc_s[...] = acc_i[...]

    @pl.when(lax.axis_index("z") >= 4)
    def _():
        visit(q_s, f_s, m_s, l_s, acc_s, (a, b), False)

    for g, out in enumerate((o0, o1, o2, o3)):
        lanes = slice(g * BLK, (g + 1) * BLK)
        total = l_s[:, lanes]
        some = total > 0.0
        safe = jnp.where(some, total, 1.0)
        out[:HEAD, :] = acc_s[:, lanes] / safe
        lse = jnp.where(some, m_s[:, lanes] + jnp.log(safe), NEG)
        out[HEAD:, :] = jnp.broadcast_to(lse, (8, BLK))


def last(state, a, b):
    return pl.pallas_call(
        last_kernel,
        out_shape=(jax.ShapeDtypeStruct((HEAD + 8, BLK), F32),) * 4,
        in_specs=[VMEM] * 7,
        out_specs=(VMEM,) * 4,
        scratch_shapes=[pltpu.VMEM(s.shape, s.dtype) for s in STATE[2:]],
        cost_estimate=visit_cost(2),
        name="last",
    )(*state, a, b)


def merge_kernel(a0, a1, b0, b1, w, out):
    c = lax.axis_index("c")

    def merged(a, b):
        la, lb = a[HEAD : HEAD + 1, :], b[HEAD : HEAD + 1, :]
        top = jnp.maximum(la, lb)
        wa, wb = jnp.exp(la - top), jnp.exp(lb - top)
        inv = 1.0 / (wa + wb)
        return (a[:HEAD, :] * (wa * inv) + b[:HEAD, :] * (wb * inv)).astype(BF16)

    mine, other = merged(a0, a1), merged(b0, b1)
    rows_mine = pl.ds(pl.multiple_of(c * HEAD, HEAD), HEAD)
    rows_other = pl.ds(pl.multiple_of((1 - c) * HEAD, HEAD), HEAD)
    for t in range(8):
        cols = slice(t * BLK, (t + 1) * BLK)
        out[t] = (tn_dot(mine, w[rows_mine, cols]) + tn_dot(other, w[rows_other, cols])).astype(BF16)


def merge(a0, a1, b0, b1, w):
    return pl.pallas_call(
        merge_kernel,
        out_shape=jax.ShapeDtypeStruct((8, BLK, BLK), BF16),
        in_specs=[VMEM] * 5,
        out_specs=VMEM,
        cost_estimate=pl.CostEstimate(
            flops=2 * BLK * BLK * 2048, bytes_accessed=3 << 20, transcendentals=1024
        ),
        name="merge",
    )(a0, a1, b0, b1, w)


def slots_kernel(parts, stream, slot, mixed, rows):
    total = stream[...].astype(F32) + jnp.sum(parts[...].astype(F32), axis=0)
    kept = total.astype(BF16)
    mixed[...] = kept
    ids = lax.broadcasted_iota(jnp.int32, (EXPERTS * CAP, BLK), 0)
    pick = jnp.where(ids == slot[...], 1.0, 0.0).astype(BF16)
    rows[...] = jnp.dot(pick, kept, preferred_element_type=F32).astype(BF16)


def to_slots(parts, stream, slot):
    return pl.pallas_call(
        slots_kernel,
        out_shape=(
            jax.ShapeDtypeStruct((BLK, BLK), BF16),
            jax.ShapeDtypeStruct((EXPERTS * CAP, BLK), BF16),
        ),
        in_specs=[VMEM] * 3,
        out_specs=(VMEM, VMEM),
        cost_estimate=pl.CostEstimate(
            flops=2 * 512 * BLK * BLK, bytes_accessed=2 << 20, transcendentals=0
        ),
        name="slots",
    )(parts, stream, slot)


GATES = 768


def expert_kernel(x, gain, g0, g1, u0, u1, d0, d1, out, n_s, w1, w2, sem):
    units = g0.shape[0]

    def copies(some):
        places = [(g0, w1, 0), (g1, w1, units), (u0, w1, GATES), (u1, w1, GATES + units), (d0, w2, 0), (d1, w2, units)]
        return [
            pltpu.make_async_copy(src, dst.at[pl.ds(at, units), :], sem.at[i])
            for i, (src, dst, at) in list(enumerate(places))[some]
        ]

    first = pl.program_id(0) == 0

    @pl.when(first)
    def _():
        for copy in copies(slice(0, 6)):
            copy.start()
        pad = jnp.zeros((GATES - 2 * units, 2048), BF16)
        w1[2 * units : GATES, :] = pad
        w1[GATES + 2 * units :, :] = pad
        w2[2 * units :, :] = pad

    square = None
    for t in range(8):
        v = x[t].astype(F32)
        term = jnp.sum(v * v, axis=1, keepdims=True)
        square = term if square is None else square + term
    inv = lax.rsqrt(square * (1.0 / 2048) + NORM_EPS)
    for t in range(8):
        cols = slice(t * BLK, (t + 1) * BLK)
        n_s[:, cols] = (x[t].astype(F32) * inv * gain[:, cols]).astype(BF16)

    @pl.when(first)
    def _():
        for copy in copies(slice(0, 4)):
            copy.wait()

    both = nt_dot(n_s[...], w1[...])
    g, u = both[:, :GATES], both[:, GATES:]
    hidden = (g / (1.0 + jnp.exp(-g)) * u).astype(BF16)

    @pl.when(first)
    def _():
        for copy in copies(slice(4, 6)):
            copy.wait()

    for t in range(8):
        cols = slice(t * BLK, (t + 1) * BLK)
        out[t] = jnp.dot(hidden, w2[:, cols], preferred_element_type=F32).astype(BF16)


def expert(x, gain, gates, ups, downs):
    rows = 128
    units = gates[0].shape[0]
    hbm = pl.BlockSpec(memory_space=pl.ANY)
    return pl.pallas_call(
        expert_kernel,
        out_shape=jax.ShapeDtypeStruct(x.shape, BF16),
        grid=(x.shape[1] // rows,),
        in_specs=[
            pl.BlockSpec((8, rows, BLK), lambda j: (0, j, 0)),
            pl.BlockSpec((1, 2048), lambda j: (0, 0)),
        ]
        + [hbm] * 6,
        out_specs=pl.BlockSpec((8, rows, BLK), lambda j: (0, j, 0)),
        scratch_shapes=[
            pltpu.VMEM((rows, 2048), BF16),
            pltpu.VMEM((2 * GATES, 2048), BF16),
            pltpu.VMEM((GATES, 2048), BF16),
            pltpu.SemaphoreType.DMA((6,)),
        ],
        cost_estimate=pl.CostEstimate(
            flops=12 * 512 * 2048 * units, bytes_accessed=13 << 20, transcendentals=1024 * units
        ),
        name="expert",
    )(x, gain, *gates, *ups, *downs)


def finish_kernel(mixed, rows, slot, out):
    ids = lax.broadcasted_iota(jnp.int32, (EXPERTS * CAP, BLK), 0)
    pick = jnp.where(ids == slot[...], 1.0, 0.0).astype(BF16)
    out[...] = (mixed[...].astype(F32) + tn_dot(pick, rows[...])).astype(BF16)


def finish(mixed, rows, slot):
    return pl.pallas_call(
        finish_kernel,
        out_shape=jax.ShapeDtypeStruct((BLK, BLK), BF16),
        in_specs=[VMEM] * 3,
        out_specs=VMEM,
        cost_estimate=pl.CostEstimate(
            flops=2 * 512 * BLK * BLK, bytes_accessed=1 << 20, transcendentals=0
        ),
        name="finish",
    )(mixed, rows, slot)


def tp_shift(a, dx, dy):
    pairs = [(i * 2 + j, ((i + dx) % 4) * 2 + (j + dy) % 2) for i in range(4) for j in range(2)]
    return lax.ppermute(a, TP, pairs)


def swap(a, dy, dc):
    pairs = [(i * 2 + j, (i ^ dy) * 2 + (j ^ dc)) for i in range(2) for j in range(2)]
    return lax.ppermute(a, ("yh", "c"), pairs)


def ring(a, step):
    return lax.ppermute(a, "z", [(i, (i + step) % 8) for i in range(8)])


def attention(q_own, q_c, kv_own, kv_c):
    kv_b = swap(kv_c, 0, 1)
    fa, ba = ring(kv_own, 1), ring(kv_own, -1)
    qs = (q_own, swap(q_c, 0, 1), swap(q_own, 1, 0), swap(q_c, 1, 1))
    fb, bb = ring(kv_b, 1), ring(kv_b, -1)
    state = local(*qs, kv_own, kv_b)
    for k in range(1, 4):
        here = (fa, fb, ba, bb)
        if k > 1:
            held = lax.optimization_barrier((*here, *state))
            here, state = held[:4], held[4:]
        fa, fb, ba, bb = here
        if k < 3:
            fa, ba, fb, bb = ring(fa, 1), ring(ba, -1), ring(fb, 1), ring(bb, -1)
        else:
            fa, bb = ring(fa, 1), ring(bb, -1)
        state = step(k, state, *here)
    return last(state, fa, bb)


def shards(stream, frames, fidelity, wq, wk, wv, wo, gain, gate, up, down):
    blocks = [stream if s == (0, 0) else tp_shift(stream, *s) for s in SHIFTS]

    route = fidelity[:, 0]
    spot = lax.iota(jnp.int32, BLK)
    same = (route[:, None] == route[None, :]) & (spot[None, :] < spot[:, None])
    slot = (route * CAP + jnp.sum(same.astype(jnp.int32), axis=1))[None, :]

    kv_own, kv_c, q_own, q_c = qkv(blocks, wq, wk, wv, frames[None, :])
    own = (gate[0].T, up[0].T, down[0])
    *sending, q_c = lax.optimization_barrier((*own, q_c))
    far = [lax.ppermute(w, "c", [(0, 1), (1, 0)]) for w in sending]

    p0, p1, p2, p3 = attention(q_own, q_c, kv_own, kv_c)
    b0, a1, b1 = swap(p1, 0, 1), swap(p2, 1, 0), swap(p3, 1, 1)
    projected = merge(p0, a1, b0, b1, wo)
    parts = lax.all_to_all(projected, TP, 0, 0, tiled=True)
    mixed, rows = to_slots(parts, stream, slot)

    sent = lax.all_to_all(rows.reshape(EXPERTS, CAP, BLK), CHIPS, 0, 0, tiled=True)
    sent = jnp.broadcast_to(sent.reshape(1, EXPERTS * CAP, BLK), (8, EXPERTS * CAP, BLK))
    full = lax.all_to_all(sent, TP, 0, 0, tiled=True)
    lowered = expert(full, gain[None, :], *zip(own, far))
    pieces = lax.all_to_all(lowered, TP, 0, 0, tiled=True)
    summed = jnp.sum(pieces.astype(F32), axis=0).astype(BF16)
    back = lax.all_to_all(summed.reshape(EXPERTS, CAP, BLK), CHIPS, 0, 0, tiled=True)
    return finish(mixed, back.reshape(EXPERTS * CAP, BLK), slot)


def solution(mesh):
    axes = ("z", "yh", "c", "x", "yl")
    fine = Mesh(np.asarray(mesh.devices).reshape(8, 2, 2, 4, 2), axes)
    return jax.shard_map(
        shards,
        mesh=fine,
        in_specs=(
            P(SEQ, TP),
            P(SEQ),
            P(SEQ, None),
            P(None, TP),
            P(None, TP),
            P(None, TP),
            P(TP, None),
            P(),
            P(SEQ, None, TP),
            P(SEQ, None, TP),
            P(SEQ, TP, None),
        ),
        out_specs=P(SEQ, TP),
        check_vma=False,
    )
```

```python
import functools
import math

import jax
import jax.numpy as jnp
import numpy as np
from jax import lax
from jax.experimental import pallas as pl
from jax.experimental.pallas import tpu as pltpu
from jax.sharding import Mesh, PartitionSpec as P

HEAD = 128
EXPERTS = 16
CAP = 32
BLK = 256
NEG = -1e30
NORM_EPS = 1e-05
SEQ = ("z", "yh", "c")
CHIPS = ("z", "yh")
TP = ("x", "yl")
SHIFTS = [(dx, dy) for dx in range(4) for dy in range(2)]
F32 = jnp.float32
BF16 = jnp.bfloat16

VMEM = pl.BlockSpec(memory_space=pltpu.VMEM)
SMEM = pl.BlockSpec(memory_space=pltpu.SMEM)


def nt_dot(a, b):
    return lax.dot_general(a, b, (((1,), (1,)), ((), ())), preferred_element_type=F32)


def tn_dot(a, b):
    return lax.dot_general(a, b, (((0,), (0,)), ((), ())), preferred_element_type=F32)


def vmem(mib):
    return pltpu.CompilerParams(vmem_limit_bytes=mib << 20)


def project(blocks, w):
    first = lax.axis_index("c") == 0
    x, yl = lax.axis_index("x"), lax.axis_index("yl")
    total = None
    for j, (dx, dy) in enumerate(SHIFTS):
        source = ((x + 4 - dx) % 4) * 2 + (yl + dy) % 2
        rows = pl.ds(pl.multiple_of(source * BLK, BLK), BLK)
        term = jnp.dot(blocks[j][...], w[rows, :], preferred_element_type=F32)
        total = term if total is None else total + term
    left, right = total[:, :HEAD], total[:, HEAD:]
    mine = jnp.where(first, left, right).astype(BF16)
    other = jnp.where(first, right, left).astype(BF16)
    return mine, other


def kv_kernel(*refs):
    blocks = refs[:8]
    wk, wv, frames, kv_own, kv_c = refs[8:]
    kv_own[:BLK, :HEAD], kv_c[:BLK, :HEAD] = project(blocks, wk)
    kv_own[:BLK, HEAD:], kv_c[:BLK, HEAD:] = project(blocks, wv)
    tail = jnp.broadcast_to(frames[...], (16, BLK)).astype(BF16)
    kv_own[BLK:, :] = tail
    kv_c[BLK:, :] = tail


def q_kernel(*refs):
    blocks = refs[:8]
    wq, frames, q_own, q_c = refs[8:]
    tail = jnp.broadcast_to(frames[...], (16, BLK)).astype(BF16)
    q_own[:BLK, :], q_c[:BLK, :] = project(blocks, wq)
    for q in (q_own, q_c):
        q[BLK : BLK + 16, :] = tail[:, :HEAD]
        q[BLK + 16 :, :] = tail[:, HEAD:]


def keys_values(blocks, wk, wv, frames):
    kv = jax.ShapeDtypeStruct((BLK + 16, 2 * HEAD), BF16)
    return pl.pallas_call(
        kv_kernel,
        out_shape=(kv, kv),
        in_specs=[VMEM] * 11,
        out_specs=(VMEM,) * 2,
        cost_estimate=pl.CostEstimate(
            flops=2 * BLK * 2048 * 512, bytes_accessed=3 << 20, transcendentals=0
        ),
        compiler_params=vmem(16),
        name="keys_values",
    )(*blocks, wk, wv, frames)


def queries(blocks, wq, frames):
    q = jax.ShapeDtypeStruct((BLK + 32, HEAD), BF16)
    return pl.pallas_call(
        q_kernel,
        out_shape=(q, q),
        in_specs=[VMEM] * 10,
        out_specs=(VMEM,) * 2,
        cost_estimate=pl.CostEstimate(
            flops=2 * BLK * 2048 * 256, bytes_accessed=2 << 20, transcendentals=0
        ),
        compiler_params=vmem(16),
        name="queries",
    )(*blocks, wq, frames)


def join_kernel(own, got, out):
    out[:BLK, :] = own[:BLK, :]
    out[BLK : 2 * BLK, :] = got[:BLK, :]
    row = lax.broadcasted_iota(jnp.int32, (16, BLK), 0)
    out[2 * BLK :, :] = jnp.where(row == 0, own[BLK:, :].astype(F32), got[BLK:, :].astype(F32)).astype(BF16)


def join(own, got):
    return pl.pallas_call(
        join_kernel,
        out_shape=jax.ShapeDtypeStruct((2 * BLK + 16, 2 * HEAD), BF16),
        in_specs=[VMEM] * 2,
        out_specs=VMEM,
        cost_estimate=pl.CostEstimate(flops=BLK * BLK, bytes_accessed=1 << 19, transcendentals=0),
        compiler_params=vmem(8),
        name="join",
    )(own, got)


def visit(q_s, f_s, m_s, l_s, acc_s, kv, masked):
    scale = 1.0 / math.sqrt(HEAD)
    s = nt_dot(kv[: 2 * BLK, :HEAD], q_s[...]) * scale
    if masked:
        lines = [jnp.broadcast_to(kv[r : r + 1, :].astype(F32), (HEAD, BLK)) for r in (2 * BLK, 2 * BLK + 1)]
        frames = jnp.concatenate([jnp.transpose(line)[:, :1] for line in lines], axis=0)
        allowed = frames <= f_s[...]
        s = jnp.where(allowed, s, NEG)
    old = m_s[...]
    top = jnp.maximum(old, jnp.max(s, axis=0, keepdims=True))
    decay = jnp.exp(old - top)
    p = jnp.exp(s - top)
    if masked:
        p = jnp.where(allowed, p, 0.0)
    m_s[...] = top
    l_s[...] = l_s[...] * decay + jnp.sum(p, axis=0, keepdims=True)
    acc_s[...] = acc_s[...] * decay + tn_dot(kv[: 2 * BLK, HEAD:], p.astype(BF16))


def local_kernel(q0, q1, q2, q3, kv, q_s, f_s, m_s, l_s, acc_s):
    for g, q in enumerate((q0, q1, q2, q3)):
        q_s[g * BLK : (g + 1) * BLK, :] = q[:BLK, :]
        for half in range(2):
            lanes = slice(g * BLK + half * HEAD, g * BLK + (half + 1) * HEAD)
            f_s[:, lanes] = q[BLK + 16 * half : BLK + 16 * half + 1, :].astype(F32)
    m_s[...] = jnp.full_like(m_s, NEG)
    l_s[...] = jnp.zeros_like(l_s)
    acc_s[...] = jnp.zeros_like(acc_s)
    visit(q_s, f_s, m_s, l_s, acc_s, kv, True)


STATE = (
    jax.ShapeDtypeStruct((4 * BLK, HEAD), BF16),
    jax.ShapeDtypeStruct((1, 4 * BLK), F32),
    jax.ShapeDtypeStruct((1, 4 * BLK), F32),
    jax.ShapeDtypeStruct((1, 4 * BLK), F32),
    jax.ShapeDtypeStruct((HEAD, 4 * BLK), F32),
)


def visit_cost(blocks):
    work = 1024 * BLK * blocks
    return pl.CostEstimate(flops=4 * work * HEAD, bytes_accessed=2 << 20, transcendentals=work)


def local(q0, q1, q2, q3, kv):
    return pl.pallas_call(
        local_kernel,
        out_shape=STATE,
        in_specs=[VMEM] * 5,
        out_specs=(VMEM,) * 5,
        cost_estimate=visit_cost(4),
        compiler_params=vmem(24),
        name="local",
    )(q0, q1, q2, q3, kv)


def step_kernel(k, q_s, f_s, m_i, l_i, acc_i, f, b, m_s, l_s, acc_s):
    z = lax.axis_index("z")
    m_s[...] = m_i[...]
    l_s[...] = l_i[...]
    acc_s[...] = acc_i[...]

    @pl.when(z >= k)
    def _():
        visit(q_s, f_s, m_s, l_s, acc_s, f, False)

    wrapped = z + k >= 8
    if k == 1:
        wrapped = wrapped | (lax.axis_index("yh") == 0)

    @pl.when(wrapped)
    def _():
        visit(q_s, f_s, m_s, l_s, acc_s, b, k == 1)


def step(k, state, f, b):
    m, l, acc = pl.pallas_call(
        functools.partial(step_kernel, k),
        out_shape=STATE[2:],
        in_specs=[VMEM] * 7,
        out_specs=(VMEM,) * 3,
        cost_estimate=visit_cost(4),
        compiler_params=vmem(24),
        name="step",
    )(*state, f, b)
    return state[0], state[1], m, l, acc


def last_kernel(q_s, f_s, m_i, l_i, acc_i, kv, o0, o1, o2, o3, m_s, l_s, acc_s):
    m_s[...] = m_i[...]
    l_s[...] = l_i[...]
    acc_s[...] = acc_i[...]

    @pl.when(lax.axis_index("z") >= 4)
    def _():
        visit(q_s, f_s, m_s, l_s, acc_s, kv, False)

    for g, out in enumerate((o0, o1, o2, o3)):
        lanes = slice(g * BLK, (g + 1) * BLK)
        total = l_s[:, lanes]
        some = total > 0.0
        safe = jnp.where(some, total, 1.0)
        out[:HEAD, :] = acc_s[:, lanes] * (1.0 / safe)
        lse = jnp.where(some, m_s[:, lanes] + jnp.log(safe), NEG)
        out[HEAD:, :] = jnp.broadcast_to(lse, (8, BLK))


def last(state, kv):
    return pl.pallas_call(
        last_kernel,
        out_shape=(jax.ShapeDtypeStruct((HEAD + 8, BLK), F32),) * 4,
        in_specs=[VMEM] * 6,
        out_specs=(VMEM,) * 4,
        scratch_shapes=[pltpu.VMEM(s.shape, s.dtype) for s in STATE[2:]],
        cost_estimate=visit_cost(2),
        compiler_params=vmem(24),
        name="last",
    )(*state, kv)


def merge_kernel(a0, a1, b0, b1, w, out):
    c = lax.axis_index("c")

    def merged(a, b):
        la, lb = a[HEAD : HEAD + 1, :], b[HEAD : HEAD + 1, :]
        top = jnp.maximum(la, lb)
        wa, wb = jnp.exp(la - top), jnp.exp(lb - top)
        inv = 1.0 / (wa + wb)
        return (a[:HEAD, :] * (wa * inv) + b[:HEAD, :] * (wb * inv)).astype(BF16)

    mine, other = merged(a0, a1), merged(b0, b1)
    rows_mine = pl.ds(pl.multiple_of(c * HEAD, HEAD), HEAD)
    rows_other = pl.ds(pl.multiple_of((1 - c) * HEAD, HEAD), HEAD)
    for t in range(8):
        cols = slice(t * BLK, (t + 1) * BLK)
        out[t] = (tn_dot(mine, w[rows_mine, cols]) + tn_dot(other, w[rows_other, cols])).astype(BF16)


def merge(a0, a1, b0, b1, w):
    return pl.pallas_call(
        merge_kernel,
        out_shape=jax.ShapeDtypeStruct((8, BLK, BLK), BF16),
        in_specs=[VMEM] * 5,
        out_specs=VMEM,
        cost_estimate=pl.CostEstimate(
            flops=2 * BLK * BLK * 2048, bytes_accessed=3 << 20, transcendentals=1024
        ),
        compiler_params=vmem(16),
        name="merge",
    )(a0, a1, b0, b1, w)


def slots_kernel(parts, stream, slot, mixed, rows):
    total = stream[...].astype(F32) + jnp.sum(parts[...].astype(F32), axis=0)
    kept = total.astype(BF16)
    mixed[...] = kept
    ids = lax.broadcasted_iota(jnp.int32, (EXPERTS * CAP, BLK), 0)
    pick = jnp.where(ids == slot[...], 1.0, 0.0).astype(BF16)
    rows[...] = jnp.dot(pick, kept, preferred_element_type=F32).astype(BF16)


def to_slots(parts, stream, slot):
    return pl.pallas_call(
        slots_kernel,
        out_shape=(
            jax.ShapeDtypeStruct((BLK, BLK), BF16),
            jax.ShapeDtypeStruct((EXPERTS * CAP, BLK), BF16),
        ),
        in_specs=[VMEM] * 3,
        out_specs=(VMEM, VMEM),
        cost_estimate=pl.CostEstimate(
            flops=2 * 512 * BLK * BLK, bytes_accessed=2 << 20, transcendentals=0
        ),
        compiler_params=vmem(16),
        name="slots",
    )(parts, stream, slot)


UNITS = 704
WIDE = 768


def pack_kernel(g0, g1, u0, u1, d0, d1, w1, w2):
    half = UNITS // 2
    pad = jnp.zeros((WIDE - UNITS, 2048), BF16)
    for w, at, a, b in ((w1, 0, g0, g1), (w1, WIDE, u0, u1), (w2, 0, d0, d1)):
        w[at : at + half, :] = a[...]
        w[at + half : at + UNITS, :] = b[...]
        w[at + UNITS : at + WIDE, :] = pad


def pack(own, far):
    return pl.pallas_call(
        pack_kernel,
        out_shape=(
            jax.ShapeDtypeStruct((2 * WIDE, 2048), BF16),
            jax.ShapeDtypeStruct((WIDE, 2048), BF16),
        ),
        in_specs=[VMEM] * 6,
        out_specs=(VMEM,) * 2,
        cost_estimate=pl.CostEstimate(flops=0, bytes_accessed=18 << 20, transcendentals=0),
        compiler_params=vmem(24),
        name="pack",
    )(own[0], far[0], own[1], far[1], own[2], far[2])


def expert_kernel(x, gain, w1_h, w2_h, out, n_s, h_s, r_s, w1, w2, sem):
    copies = [pltpu.make_async_copy(w1_h, w1, sem.at[0]), pltpu.make_async_copy(w2_h, w2, sem.at[1])]
    for copy in copies:
        copy.start()
    rows = x.shape[1]
    some = 64

    def prepare(i, carry):
        at = pl.ds(pl.multiple_of(i * some, some), some)
        square = None
        for t in range(8):
            cols = slice(t * BLK, (t + 1) * BLK)
            v = x[t, at, :].astype(F32)
            n_s[at, cols] = (v * gain[:, cols]).astype(BF16)
            square = v * v if square is None else square + v * v
        mean = jnp.sum(square, axis=1, keepdims=True) * (1.0 / 2048)
        r_s[at, :] = lax.rsqrt(mean + NORM_EPS)
        return carry

    lax.fori_loop(0, rows // some, prepare, 0)
    factor = r_s[...]
    copies[0].wait()
    for j in range(WIDE // BLK):
        cols = slice(j * BLK, (j + 1) * BLK)
        g = nt_dot(n_s[...], w1[cols, :]) * factor
        u = nt_dot(n_s[...], w1[WIDE + j * BLK : WIDE + (j + 1) * BLK, :]) * factor
        h_s[:, cols] = (g / (1.0 + jnp.exp(-g)) * u).astype(BF16)
    copies[1].wait()
    for t in range(8):
        cols = slice(t * BLK, (t + 1) * BLK)
        out[t] = jnp.dot(h_s[...], w2[:, cols], preferred_element_type=F32).astype(BF16)


def expert(x, gain, w1, w2):
    rows = x.shape[1]
    return pl.pallas_call(
        expert_kernel,
        out_shape=jax.ShapeDtypeStruct(x.shape, BF16),
        in_specs=[VMEM] * 2 + [pl.BlockSpec(memory_space=pl.ANY)] * 2,
        out_specs=VMEM,
        scratch_shapes=[
            pltpu.VMEM((rows, 2048), BF16),
            pltpu.VMEM((rows, WIDE), BF16),
            pltpu.VMEM((rows, 1), F32),
            pltpu.VMEM((2 * WIDE, 2048), BF16),
            pltpu.VMEM((WIDE, 2048), BF16),
            pltpu.SemaphoreType.DMA((2,)),
        ],
        cost_estimate=pl.CostEstimate(
            flops=6 * rows * 2048 * WIDE, bytes_accessed=13 << 20, transcendentals=rows * WIDE
        ),
        compiler_params=vmem(32),
        name="expert",
    )(x, gain, w1, w2)


def finish_kernel(mixed, rows, slot, out):
    ids = lax.broadcasted_iota(jnp.int32, (EXPERTS * CAP, BLK), 0)
    pick = jnp.where(ids == slot[...], 1.0, 0.0).astype(BF16)
    out[...] = (mixed[...].astype(F32) + tn_dot(pick, rows[...])).astype(BF16)


def finish(mixed, rows, slot):
    return pl.pallas_call(
        finish_kernel,
        out_shape=jax.ShapeDtypeStruct((BLK, BLK), BF16),
        in_specs=[VMEM] * 3,
        out_specs=VMEM,
        cost_estimate=pl.CostEstimate(
            flops=2 * 512 * BLK * BLK, bytes_accessed=1 << 20, transcendentals=0
        ),
        compiler_params=vmem(8),
        name="finish",
    )(mixed, rows, slot)


def tp_shift(a, dx, dy):
    pairs = [(i * 2 + j, ((i + dx) % 4) * 2 + (j + dy) % 2) for i in range(4) for j in range(2)]
    return lax.ppermute(a, TP, pairs)


def swap(a, dy, dc):
    pairs = [(i * 2 + j, (i ^ dy) * 2 + (j ^ dc)) for i in range(2) for j in range(2)]
    return lax.ppermute(a, ("yh", "c"), pairs)


def ring(a, step):
    return lax.ppermute(a, "z", [(i, (i + step) % 8) for i in range(8)])


def attention(blocks, wq, wk, wv, frames):
    kv_own, kv_c = keys_values(blocks, wk, wv, frames)
    kv = join(kv_own, swap(kv_c, 0, 1))
    q_own, q_c = queries(blocks, wq, frames)
    f, b = ring(kv, 1), ring(kv, -1)
    qs = (q_own, swap(q_c, 0, 1), swap(q_own, 1, 0), swap(q_c, 1, 1))
    state = local(*qs, kv)
    for k in range(1, 4):
        if k > 1:
            f, b, *state = lax.optimization_barrier((f, b, *state))
        else:
            f, b, _ = lax.optimization_barrier((f, b, q_own))
        here = f, b
        if k < 3:
            f, b = ring(f, 1), ring(b, -1)
        else:
            way = jnp.where(lax.axis_index("c") == 0, f, b)
            hops = [(i * 2 + c, (i + (-1 if c else 1)) % 8 * 2 + c) for i in range(8) for c in range(2)]
            far = lax.ppermute(way, ("z", "c"), hops)
        state = step(k, state, *here)
    return last(state, far)


def shards(stream, frames, fidelity, wq, wk, wv, wo, gain, gate, up, down):
    blocks = [stream if s == (0, 0) else tp_shift(stream, *s) for s in SHIFTS]

    route = fidelity[:, 0]
    spot = lax.iota(jnp.int32, BLK)
    same = (route[:, None] == route[None, :]) & (spot[None, :] < spot[:, None])
    slot = (route * CAP + jnp.sum(same.astype(jnp.int32), axis=1))[None, :]

    p0, p1, p2, p3 = attention(blocks, wq, wk, wv, frames[None, :])
    b0, a1, b1 = swap(p1, 0, 1), swap(p2, 1, 0), swap(p3, 1, 1)
    projected = merge(p0, a1, b0, b1, wo)

    own = (gate[0].T, up[0].T, down[0])
    *sending, projected = lax.optimization_barrier((*own, projected))
    w1, w2 = pack(own, [lax.ppermute(w, "c", [(0, 1), (1, 0)]) for w in sending])

    parts = lax.all_to_all(projected, TP, 0, 0, tiled=True)
    mixed, rows = to_slots(parts, stream, slot)
    sent = lax.all_to_all(rows.reshape(EXPERTS, CAP, BLK), CHIPS, 0, 0, tiled=True)
    sent = jnp.broadcast_to(sent.reshape(1, EXPERTS * CAP, BLK), (8, EXPERTS * CAP, BLK))
    full = lax.all_to_all(sent, TP, 0, 0, tiled=True)
    lowered = expert(full, gain[None, :], w1, w2)
    pieces = lax.all_to_all(lowered, TP, 0, 0, tiled=True)
    summed = jnp.sum(pieces.astype(F32), axis=0).astype(BF16)
    back = lax.all_to_all(summed.reshape(EXPERTS, CAP, BLK), CHIPS, 0, 0, tiled=True)
    return finish(mixed, back.reshape(EXPERTS * CAP, BLK), slot)


def solution(mesh):
    axes = ("z", "yh", "c", "x", "yl")
    fine = Mesh(np.asarray(mesh.devices).reshape(8, 2, 2, 4, 2), axes)
    return jax.shard_map(
        shards,
        mesh=fine,
        in_specs=(
            P(SEQ, TP),
            P(SEQ),
            P(SEQ, None),
            P(None, TP),
            P(None, TP),
            P(None, TP),
            P(TP, None),
            P(),
            P(SEQ, None, TP),
            P(SEQ, None, TP),
            P(SEQ, TP, None),
        ),
        out_specs=P(SEQ, TP),
        check_vma=False,
    )
```

```python
import functools
import math

import jax
import jax.numpy as jnp
import numpy as np
from jax import lax
from jax.experimental import pallas as pl
from jax.experimental.pallas import tpu as pltpu
from jax.sharding import Mesh, PartitionSpec as P

HEAD = 128
EXPERTS = 16
CAP = 32
BLK = 256
NEG = -1e30
NORM_EPS = 1e-05
SEQ = ("z", "yh", "c")
CHIPS = ("z", "yh")
TP = ("x", "yl")
NEAR = ((0, 0), (1, 0), (3, 1), (3, 0), (1, 1), (0, 1))
FAR = ((2, 0), (2, 1))
F32 = jnp.float32
BF16 = jnp.bfloat16

VMEM = pl.BlockSpec(memory_space=pltpu.VMEM)
SMEM = pl.BlockSpec(memory_space=pltpu.SMEM)


def nt_dot(a, b):
    return lax.dot_general(a, b, (((1,), (1,)), ((), ())), preferred_element_type=F32)


def tn_dot(a, b):
    return lax.dot_general(a, b, (((0,), (0,)), ((), ())), preferred_element_type=F32)


def vmem(mib):
    return pltpu.CompilerParams(vmem_limit_bytes=mib << 20)


def source_rows(dx, dy):
    x, yl = lax.axis_index("x"), lax.axis_index("yl")
    source = ((x + 4 - dx) % 4) * 2 + (yl + dy) % 2
    return pl.ds(pl.multiple_of(source * BLK, BLK), BLK)


def near_kernel(*refs):
    blocks = refs[:6]
    weights = refs[6:9]
    acc, rest = refs[9:]
    for i, w in enumerate(weights):
        cols = slice(i * BLK, (i + 1) * BLK)
        total = None
        for block, shift in zip(blocks, NEAR):
            term = jnp.dot(block[...], w[source_rows(*shift), :], preferred_element_type=F32)
            total = term if total is None else total + term
        acc[:, cols] = total
        for j, shift in enumerate(FAR):
            rest[j * BLK : (j + 1) * BLK, cols] = w[source_rows(*shift), :]


def project_near(blocks, wk, wv, wq):
    return pl.pallas_call(
        near_kernel,
        out_shape=(
            jax.ShapeDtypeStruct((BLK, 3 * BLK), F32),
            jax.ShapeDtypeStruct((2 * BLK, 3 * BLK), BF16),
        ),
        in_specs=[VMEM] * 9,
        out_specs=(VMEM,) * 2,
        cost_estimate=pl.CostEstimate(
            flops=2 * BLK * 1536 * 768, bytes_accessed=5 << 20, transcendentals=0
        ),
        compiler_params=vmem(20),
        name="project_near",
    )(*blocks, wk, wv, wq)


def far_kernel(acc, rest, b0, b1, frames, kv_own, kv_c, q_own, q_c):
    total = acc[...]
    for j, block in enumerate((b0, b1)):
        total = total + jnp.dot(
            block[...], rest[j * BLK : (j + 1) * BLK, :], preferred_element_type=F32
        )
    first = lax.axis_index("c") == 0

    def split(i):
        left = total[:, i * BLK : i * BLK + HEAD]
        right = total[:, i * BLK + HEAD : (i + 1) * BLK]
        return jnp.where(first, left, right).astype(BF16), jnp.where(first, right, left).astype(BF16)

    kv_own[:BLK, :HEAD], kv_c[:BLK, :HEAD] = split(0)
    kv_own[:BLK, HEAD:], kv_c[:BLK, HEAD:] = split(1)
    q_own[:BLK, :], q_c[:BLK, :] = split(2)
    tail = jnp.broadcast_to(frames[...], (16, BLK)).astype(BF16)
    kv_own[BLK:, :] = tail
    kv_c[BLK:, :] = tail
    for q in (q_own, q_c):
        q[BLK : BLK + 16, :] = tail[:, :HEAD]
        q[BLK + 16 :, :] = tail[:, HEAD:]


def project_far(acc, rest, b0, b1, frames):
    kv = jax.ShapeDtypeStruct((BLK + 16, 2 * HEAD), BF16)
    q = jax.ShapeDtypeStruct((BLK + 32, HEAD), BF16)
    return pl.pallas_call(
        far_kernel,
        out_shape=(kv, kv, q, q),
        in_specs=[VMEM] * 5,
        out_specs=(VMEM,) * 4,
        cost_estimate=pl.CostEstimate(
            flops=2 * BLK * 512 * 768, bytes_accessed=2 << 20, transcendentals=0
        ),
        compiler_params=vmem(16),
        name="project_far",
    )(acc, rest, b0, b1, frames)


def join_kernel(own, got, out):
    out[:BLK, :] = own[:BLK, :]
    out[BLK : 2 * BLK, :] = got[:BLK, :]
    row = lax.broadcasted_iota(jnp.int32, (16, BLK), 0)
    out[2 * BLK :, :] = jnp.where(row == 0, own[BLK:, :].astype(F32), got[BLK:, :].astype(F32)).astype(BF16)


def join(own, got):
    return pl.pallas_call(
        join_kernel,
        out_shape=jax.ShapeDtypeStruct((2 * BLK + 16, 2 * HEAD), BF16),
        in_specs=[VMEM] * 2,
        out_specs=VMEM,
        cost_estimate=pl.CostEstimate(flops=BLK * BLK, bytes_accessed=1 << 19, transcendentals=0),
        compiler_params=vmem(8),
        name="join",
    )(own, got)


def visit(q_s, f_s, m_s, l_s, acc_s, kv, masked):
    scale = 1.0 / math.sqrt(HEAD)
    if masked:
        lines = [jnp.broadcast_to(kv[r : r + 1, :].astype(F32), (HEAD, BLK)) for r in (2 * BLK, 2 * BLK + 1)]
        frames = jnp.concatenate([jnp.transpose(line)[:, :1] for line in lines], axis=0)

    def part(i, carry):
        lanes = pl.ds(pl.multiple_of(i * 2 * BLK, 2 * BLK), 2 * BLK)
        s = nt_dot(kv[: 2 * BLK, :HEAD], q_s[lanes, :]) * scale
        if masked:
            allowed = frames <= f_s[:, lanes]
            s = jnp.where(allowed, s, NEG)
        old = m_s[:, lanes]
        top = jnp.maximum(old, jnp.max(s, axis=0, keepdims=True))
        decay = jnp.exp(old - top)
        p = jnp.exp(s - top)
        if masked:
            p = jnp.where(allowed, p, 0.0)
        m_s[:, lanes] = top
        l_s[:, lanes] = l_s[:, lanes] * decay + jnp.sum(p, axis=0, keepdims=True)
        acc_s[:, lanes] = acc_s[:, lanes] * decay + tn_dot(kv[: 2 * BLK, HEAD:], p.astype(BF16))
        return carry

    lax.fori_loop(0, 2, part, 0)


def local_kernel(q0, q1, q2, q3, kv, q_s, f_s, m_s, l_s, acc_s):
    for g, q in enumerate((q0, q1, q2, q3)):
        q_s[g * BLK : (g + 1) * BLK, :] = q[:BLK, :]
        for half in range(2):
            lanes = slice(g * BLK + half * HEAD, g * BLK + (half + 1) * HEAD)
            f_s[:, lanes] = q[BLK + 16 * half : BLK + 16 * half + 1, :].astype(F32)
    m_s[...] = jnp.full_like(m_s, NEG)
    l_s[...] = jnp.zeros_like(l_s)
    acc_s[...] = jnp.zeros_like(acc_s)
    visit(q_s, f_s, m_s, l_s, acc_s, kv, True)


STATE = (
    jax.ShapeDtypeStruct((4 * BLK, HEAD), BF16),
    jax.ShapeDtypeStruct((1, 4 * BLK), F32),
    jax.ShapeDtypeStruct((1, 4 * BLK), F32),
    jax.ShapeDtypeStruct((1, 4 * BLK), F32),
    jax.ShapeDtypeStruct((HEAD, 4 * BLK), F32),
)


def visit_cost(blocks):
    work = 1024 * BLK * blocks
    return pl.CostEstimate(flops=4 * work * HEAD, bytes_accessed=2 << 20, transcendentals=work)


def local(q0, q1, q2, q3, kv):
    return pl.pallas_call(
        local_kernel,
        out_shape=STATE,
        in_specs=[VMEM] * 5,
        out_specs=(VMEM,) * 5,
        cost_estimate=visit_cost(4),
        compiler_params=vmem(24),
        name="local",
    )(q0, q1, q2, q3, kv)


def step_kernel(k, q_s, f_s, m_i, l_i, acc_i, f, b, m_s, l_s, acc_s, kv):
    z = lax.axis_index("z")
    m_s[...] = m_i[...]
    l_s[...] = l_i[...]
    acc_s[...] = acc_i[...]
    wrapped = z + k >= 8
    if k == 1:
        wrapped = wrapped | (lax.axis_index("yh") == 0)

    def side(j, carry):
        @pl.when((j == 0) & (z >= k))
        def _():
            kv[...] = f[...]

        @pl.when((j == 1) & wrapped)
        def _():
            kv[...] = b[...]

        @pl.when(((j == 0) & (z >= k)) | ((j == 1) & wrapped))
        def _():
            visit(q_s, f_s, m_s, l_s, acc_s, kv, k == 1)

        return carry

    lax.fori_loop(0, 2, side, 0)


def step(k, state, f, b):
    m, l, acc = pl.pallas_call(
        functools.partial(step_kernel, k),
        out_shape=STATE[2:],
        in_specs=[VMEM] * 7,
        out_specs=(VMEM,) * 3,
        scratch_shapes=[pltpu.VMEM(f.shape, BF16)],
        cost_estimate=visit_cost(4),
        compiler_params=vmem(24),
        name="step",
    )(*state, f, b)
    return state[0], state[1], m, l, acc


def last_kernel(q_s, f_s, m_i, l_i, acc_i, kv, o0, o1, o2, o3, m_s, l_s, acc_s):
    m_s[...] = m_i[...]
    l_s[...] = l_i[...]
    acc_s[...] = acc_i[...]

    @pl.when(lax.axis_index("z") >= 4)
    def _():
        visit(q_s, f_s, m_s, l_s, acc_s, kv, False)

    for g, out in enumerate((o0, o1, o2, o3)):
        lanes = slice(g * BLK, (g + 1) * BLK)
        total = l_s[:, lanes]
        some = total > 0.0
        safe = jnp.where(some, total, 1.0)
        out[:HEAD, :] = (acc_s[:, lanes] * (1.0 / safe)).astype(BF16)
        log = jnp.where(some, m_s[:, lanes] + jnp.log(safe), NEG)
        row = lax.broadcasted_iota(jnp.int32, (16, BLK), 0)
        high = log.astype(BF16).astype(F32)
        middle = (log - high).astype(BF16).astype(F32)
        low = log - high - middle
        terms = jnp.where(row == 0, high, jnp.where(row == 1, middle, jnp.where(row == 2, low, 0.0)))
        out[HEAD:, :] = terms.astype(BF16)


def last(state, kv):
    return pl.pallas_call(
        last_kernel,
        out_shape=(jax.ShapeDtypeStruct((HEAD + 16, BLK), BF16),) * 4,
        in_specs=[VMEM] * 6,
        out_specs=(VMEM,) * 4,
        scratch_shapes=[pltpu.VMEM(s.shape, s.dtype) for s in STATE[2:]],
        cost_estimate=visit_cost(2),
        compiler_params=vmem(24),
        name="last",
    )(*state, kv)


def merge_kernel(a0, a1, b0, b1, w, *outs):
    c = lax.axis_index("c")

    def merged(a, b):
        la = jnp.sum(a[HEAD:, :].astype(F32), axis=0, keepdims=True)
        lb = jnp.sum(b[HEAD:, :].astype(F32), axis=0, keepdims=True)
        top = jnp.maximum(la, lb)
        wa, wb = jnp.exp(la - top), jnp.exp(lb - top)
        inv = 1.0 / (wa + wb)
        return (a[:HEAD, :].astype(F32) * (wa * inv) + b[:HEAD, :].astype(F32) * (wb * inv)).astype(BF16)

    mine, other = merged(a0, a1), merged(b0, b1)
    rows_mine = pl.ds(pl.multiple_of(c * HEAD, HEAD), HEAD)
    rows_other = pl.ds(pl.multiple_of((1 - c) * HEAD, HEAD), HEAD)
    for out, shift in zip(outs, NEAR + FAR):
        cols = target_cols(*shift)
        out[...] = (tn_dot(mine, w[rows_mine, cols]) + tn_dot(other, w[rows_other, cols])).astype(BF16)


def target_cols(dx, dy):
    x, yl = lax.axis_index("x"), lax.axis_index("yl")
    target = ((x + dx) % 4) * 2 + (yl + dy) % 2
    return pl.ds(pl.multiple_of(target * BLK, BLK), BLK)


def merge(a0, a1, b0, b1, w):
    return pl.pallas_call(
        merge_kernel,
        out_shape=(jax.ShapeDtypeStruct((BLK, BLK), BF16),) * 8,
        in_specs=[VMEM] * 5,
        out_specs=(VMEM,) * 8,
        cost_estimate=pl.CostEstimate(
            flops=2 * BLK * BLK * 2048, bytes_accessed=3 << 20, transcendentals=1024
        ),
        compiler_params=vmem(16),
        name="merge",
    )(a0, a1, b0, b1, w)


def add_kernel(a0, b0, a1, b1, out0, out1):
    out0[...] = (a0[...].astype(F32) + b0[...].astype(F32)).astype(BF16)
    out1[...] = (a1[...].astype(F32) + b1[...].astype(F32)).astype(BF16)


def add_pairs(a0, b0, a1, b1):
    return pl.pallas_call(
        add_kernel,
        out_shape=(jax.ShapeDtypeStruct(a0.shape, BF16),) * 2,
        in_specs=[VMEM] * 4,
        out_specs=(VMEM,) * 2,
        cost_estimate=pl.CostEstimate(flops=a0.size, bytes_accessed=12 * a0.size, transcendentals=0),
        compiler_params=vmem(8),
        name="add_pairs",
    )(a0, b0, a1, b1)


def sum_kernel(*refs):
    total = refs[0][...].astype(F32)
    for ref in refs[1:-1]:
        total = total + ref[...].astype(F32)
    refs[-1][...] = total.astype(BF16)


def sum_all(terms):
    return pl.pallas_call(
        sum_kernel,
        out_shape=jax.ShapeDtypeStruct(terms[0].shape, BF16),
        in_specs=[VMEM] * len(terms),
        out_specs=VMEM,
        cost_estimate=pl.CostEstimate(
            flops=6 * terms[0].size, bytes_accessed=14 * terms[0].size, transcendentals=0
        ),
        compiler_params=vmem(8),
        name="sum_all",
    )(*terms)


def slots_kernel(*refs):
    terms = refs[:6]
    stream, slot, mixed, rows = refs[6:]
    total = stream[...].astype(F32)
    for term in terms:
        total = total + term[...].astype(F32)
    kept = total.astype(BF16)
    mixed[...] = kept
    ids = lax.broadcasted_iota(jnp.int32, (EXPERTS * CAP, BLK), 0)
    pick = jnp.where(ids == slot[...], 1.0, 0.0).astype(BF16)
    rows[...] = jnp.dot(pick, kept, preferred_element_type=F32).astype(BF16)


def to_slots(terms, stream, slot):
    return pl.pallas_call(
        slots_kernel,
        out_shape=(
            jax.ShapeDtypeStruct((BLK, BLK), BF16),
            jax.ShapeDtypeStruct((EXPERTS * CAP, BLK), BF16),
        ),
        in_specs=[VMEM] * 8,
        out_specs=(VMEM, VMEM),
        cost_estimate=pl.CostEstimate(
            flops=2 * 512 * BLK * BLK, bytes_accessed=2 << 20, transcendentals=0
        ),
        compiler_params=vmem(16),
        name="slots",
    )(*terms, stream, slot)


UNITS = 704
WIDE = 768


def expert_kernel(*refs):
    blocks = refs[:8]
    gain, g0, g1, u0, u1, d0, d1 = refs[8:15]
    outs = refs[15:23]
    n_s, h_s, r_s, w1, w2, sem = refs[23:]
    half = UNITS // 2
    places = [(g0, w1, 0), (g1, w1, half), (u0, w1, WIDE), (u1, w1, WIDE + half), (d0, w2, 0), (d1, w2, half)]
    copies = [
        pltpu.make_async_copy(src, dst.at[pl.ds(at, half), :], sem.at[i])
        for i, (src, dst, at) in enumerate(places)
    ]
    for copy in copies:
        copy.start()
    pad = jnp.zeros((WIDE - UNITS, 2048), BF16)
    w1[UNITS:WIDE, :] = pad
    w1[WIDE + UNITS :, :] = pad
    w2[UNITS:, :] = pad
    rows = n_s.shape[0]
    some = 64

    def prepare(i, carry):
        at = pl.ds(pl.multiple_of(i * some, some), some)
        square = None
        for block, shift in zip(blocks, NEAR + FAR):
            cols = source_rows(*shift)
            v = block[at, :].astype(F32)
            n_s[at, cols] = (v * gain[:, cols]).astype(BF16)
            square = v * v if square is None else square + v * v
        mean = jnp.sum(square, axis=1, keepdims=True) * (1.0 / 2048)
        r_s[at, :] = lax.rsqrt(mean + NORM_EPS)
        return carry

    lax.fori_loop(0, rows // some, prepare, 0)
    factor = r_s[...]
    for copy in copies[:4]:
        copy.wait()

    def hidden(j, carry):
        cols = pl.ds(pl.multiple_of(j * BLK, BLK), BLK)
        g = nt_dot(n_s[...], w1[cols, :]) * factor
        u = nt_dot(n_s[...], w1[pl.ds(pl.multiple_of(WIDE + j * BLK, BLK), BLK), :]) * factor
        h_s[:, cols] = (g / (1.0 + jnp.exp(-g)) * u).astype(BF16)
        return carry

    lax.fori_loop(0, WIDE // BLK, hidden, 0)
    for copy in copies[4:]:
        copy.wait()

    def lower(i, carry):
        at = pl.ds(pl.multiple_of(i * BLK, BLK), BLK)
        for out, shift in zip(outs, NEAR + FAR):
            out[at, :] = jnp.dot(
                h_s[at, :], w2[:, target_cols(*shift)], preferred_element_type=F32
            ).astype(BF16)
        return carry

    lax.fori_loop(0, rows // BLK, lower, 0)


def expert(blocks, gain, own, far):
    rows = blocks[0].shape[0]
    return pl.pallas_call(
        expert_kernel,
        out_shape=(jax.ShapeDtypeStruct(blocks[0].shape, BF16),) * 8,
        in_specs=[VMEM] * 9 + [pl.BlockSpec(memory_space=pltpu.HBM)] * 6,
        out_specs=(VMEM,) * 8,
        scratch_shapes=[
            pltpu.VMEM((rows, 2048), BF16),
            pltpu.VMEM((rows, WIDE), BF16),
            pltpu.VMEM((rows, 1), F32),
            pltpu.VMEM((2 * WIDE, 2048), BF16),
            pltpu.VMEM((WIDE, 2048), BF16),
            pltpu.SemaphoreType.DMA((6,)),
        ],
        cost_estimate=pl.CostEstimate(
            flops=6 * rows * 2048 * WIDE, bytes_accessed=13 << 20, transcendentals=rows * WIDE
        ),
        compiler_params=vmem(32),
        name="expert",
    )(*blocks, gain, own[0], far[0], own[1], far[1], own[2], far[2])


def finish_kernel(mixed, rows, slot, out):
    ids = lax.broadcasted_iota(jnp.int32, (EXPERTS * CAP, BLK), 0)
    pick = jnp.where(ids == slot[...], 1.0, 0.0).astype(BF16)
    out[...] = (mixed[...].astype(F32) + tn_dot(pick, rows[...])).astype(BF16)


def finish(mixed, rows, slot):
    return pl.pallas_call(
        finish_kernel,
        out_shape=jax.ShapeDtypeStruct((BLK, BLK), BF16),
        in_specs=[VMEM] * 3,
        out_specs=VMEM,
        cost_estimate=pl.CostEstimate(
            flops=2 * 512 * BLK * BLK, bytes_accessed=1 << 20, transcendentals=0
        ),
        compiler_params=vmem(8),
        name="finish",
    )(mixed, rows, slot)


def tp_shift(a, dx, dy):
    pairs = [(i * 2 + j, ((i + dx) % 4) * 2 + (j + dy) % 2) for i in range(4) for j in range(2)]
    return lax.ppermute(a, TP, pairs)


def tp_gather(a):
    near = [a] + [tp_shift(a, *s) for s in NEAR[1:]]
    return near + [tp_shift(near[1], 1, 0), tp_shift(near[2], 3, 0)]


def tp_scatter(pieces):
    got = tp_shift(pieces[6], 1, 0), tp_shift(pieces[7], 3, 0)
    straight = [tp_shift(p, *s) for p, s in zip(pieces[3:6], NEAR[3:6])]
    sums = add_pairs(pieces[1], got[0], pieces[2], got[1])
    return [pieces[0]] + straight + [tp_shift(p, *s) for p, s in zip(sums, NEAR[1:3])]


def swap(a, dy, dc):
    pairs = [(i * 2 + j, (i ^ dy) * 2 + (j ^ dc)) for i in range(2) for j in range(2)]
    return lax.ppermute(a, ("yh", "c"), pairs)


def ring(a, step):
    return lax.ppermute(a, "z", [(i, (i + step) % 8) for i in range(8)])


def attention(blocks, wq, wk, wv, frames):
    acc, rest = project_near(blocks[:6], wk, wv, wq)
    kv_own, kv_c, q_own, q_c = project_far(acc, rest, *blocks[6:], frames)
    kv = join(kv_own, swap(kv_c, 0, 1))
    f, b = ring(kv, 1), ring(kv, -1)
    qs = [q_own, swap(q_c, 0, 1), swap(q_own, 1, 0), swap(q_c, 1, 1)]
    f, b, *qs = lax.optimization_barrier((f, b, *qs))
    state = local(*qs, kv)
    for k in range(1, 4):
        if k > 1:
            f, b, *state = lax.optimization_barrier((f, b, *state))
        here = f, b
        if k < 3:
            f, b = ring(f, 1), ring(b, -1)
        else:
            way = jnp.where(lax.axis_index("c") == 0, f, b)
            hops = [(i * 2 + c, (i + (-1 if c else 1)) % 8 * 2 + c) for i in range(8) for c in range(2)]
            far = lax.ppermute(way, ("z", "c"), hops)
        state = step(k, state, *here)
    return last(state, far)


def shards(stream, frames, fidelity, wq, wk, wv, wo, gain, gate, up, down):
    route = fidelity[:, 0]
    spot = lax.iota(jnp.int32, BLK)
    same = (route[:, None] == route[None, :]) & (spot[None, :] < spot[:, None])
    slot = (route * CAP + jnp.sum(same.astype(jnp.int32), axis=1))[None, :]

    p0, p1, p2, p3 = attention(tp_gather(stream), wq, wk, wv, frames[None, :])
    b0, a1, b1 = swap(p1, 0, 1), swap(p2, 1, 0), swap(p3, 1, 1)
    projected = merge(p0, a1, b0, b1, wo)

    mixed, rows = to_slots(tp_scatter(projected), stream, slot)

    own = (gate[0].T, up[0].T, down[0])
    *sending, rows = lax.optimization_barrier((*own, rows))
    far = [lax.ppermute(w, "c", [(0, 1), (1, 0)]) for w in sending]
    sent = lax.all_to_all(rows.reshape(EXPERTS, CAP, BLK), CHIPS, 0, 0, tiled=True)
    sent, *far = lax.optimization_barrier((sent, *far))
    lowered = expert(tp_gather(sent.reshape(EXPERTS * CAP, BLK)), gain[None, :], own, far)
    summed = sum_all(tp_scatter(lowered))
    back = lax.all_to_all(summed.reshape(EXPERTS, CAP, BLK), CHIPS, 0, 0, tiled=True)
    return finish(mixed, back.reshape(EXPERTS * CAP, BLK), slot)


def solution(mesh):
    axes = ("z", "yh", "c", "x", "yl")
    fine = Mesh(np.asarray(mesh.devices).reshape(8, 2, 2, 4, 2), axes)
    return jax.shard_map(
        shards,
        mesh=fine,
        in_specs=(
            P(SEQ, TP),
            P(SEQ),
            P(SEQ, None),
            P(None, TP),
            P(None, TP),
            P(None, TP),
            P(TP, None),
            P(),
            P(SEQ, None, TP),
            P(SEQ, None, TP),
            P(SEQ, TP, None),
        ),
        out_specs=P(SEQ, TP),
        check_vma=False,
    )
```

```python
import functools
import math

import jax
import jax.numpy as jnp
import numpy as np
from jax import lax
from jax.experimental import pallas as pl
from jax.experimental.pallas import tpu as pltpu
from jax.sharding import Mesh, PartitionSpec as P

HEAD = 128
EXPERTS = 16
CAP = 32
BLK = 256
NEG = -1e30
NORM_EPS = 1e-05
SEQ = ("z", "yh", "c")
CHIPS = ("z", "yh")
TP = ("x", "yl")
NEAR = ((0, 0), (1, 0), (3, 1), (3, 0), (1, 1), (0, 1))
FAR = ((2, 0), (2, 1))
F32 = jnp.float32
BF16 = jnp.bfloat16

VMEM = pl.BlockSpec(memory_space=pltpu.VMEM)
HBM = pl.BlockSpec(memory_space=pltpu.HBM)


def nt_dot(a, b):
    return lax.dot_general(a, b, (((1,), (1,)), ((), ())), preferred_element_type=F32)


def tn_dot(a, b):
    return lax.dot_general(a, b, (((0,), (0,)), ((), ())), preferred_element_type=F32)


def vmem(mib):
    return pltpu.CompilerParams(vmem_limit_bytes=mib << 20)


def source_rows(dx, dy):
    x, yl = lax.axis_index("x"), lax.axis_index("yl")
    source = ((x + 4 - dx) % 4) * 2 + (yl + dy) % 2
    return pl.ds(pl.multiple_of(source * BLK, BLK), BLK)


def fetch_kernel(wk, wv, wq, out, sem):
    copies = [
        pltpu.make_async_copy(src, out.at[:, pl.ds(i * BLK, BLK)], sem.at[i])
        for i, src in enumerate((wk, wv, wq))
    ]
    for copy in copies:
        copy.start()
    for copy in copies:
        copy.wait()


def fetch(*weights):
    return pl.pallas_call(
        fetch_kernel,
        out_shape=jax.ShapeDtypeStruct((2048, 3 * BLK), BF16),
        in_specs=[HBM] * 3,
        out_specs=VMEM,
        scratch_shapes=[pltpu.SemaphoreType.DMA((3,))],
        cost_estimate=pl.CostEstimate(flops=0, bytes_accessed=6 << 20, transcendentals=0),
        compiler_params=vmem(8),
        name="fetch",
    )(*weights)


def near_kernel(*refs):
    blocks = refs[:6]
    weights, acc, rest = refs[6:]

    def some(i, carry):
        cols = pl.ds(pl.multiple_of(i * BLK, BLK), BLK)
        total = None
        for block, shift in zip(blocks, NEAR):
            term = jnp.dot(block[...], weights[source_rows(*shift), cols], preferred_element_type=F32)
            total = term if total is None else total + term
        acc[:, cols] = total
        for j, shift in enumerate(FAR):
            rest[j * BLK : (j + 1) * BLK, cols] = weights[source_rows(*shift), cols]
        return carry

    lax.fori_loop(0, 3, some, 0)


def project_near(blocks, weights):
    return pl.pallas_call(
        near_kernel,
        out_shape=(
            jax.ShapeDtypeStruct((BLK, 3 * BLK), F32),
            jax.ShapeDtypeStruct((2 * BLK, 3 * BLK), BF16),
        ),
        in_specs=[VMEM] * 7,
        out_specs=(VMEM,) * 2,
        cost_estimate=pl.CostEstimate(
            flops=2 * BLK * 1536 * 768, bytes_accessed=5 << 20, transcendentals=0
        ),
        compiler_params=vmem(20),
        name="project_near",
    )(*blocks, weights)


def far_kernel(acc, rest, b0, b1, frames, own, other):
    first = lax.axis_index("c") == 0

    def some(i, carry):
        cols = pl.ds(pl.multiple_of(i * BLK, BLK), BLK)
        total = acc[:, cols]
        for j, block in enumerate((b0, b1)):
            total = total + jnp.dot(
                block[...], rest[j * BLK : (j + 1) * BLK, cols], preferred_element_type=F32
            )
        left, right = total[:, :HEAD], total[:, HEAD:]
        cols = pl.ds(pl.multiple_of(i * HEAD, HEAD), HEAD)
        own[:BLK, cols] = jnp.where(first, left, right).astype(BF16)
        other[:BLK, cols] = jnp.where(first, right, left).astype(BF16)
        return carry

    lax.fori_loop(0, 3, some, 0)
    tail = jnp.broadcast_to(frames[...], (16, BLK)).astype(BF16)
    for out in (own, other):
        out[BLK:, : 2 * HEAD] = tail
        out[BLK:, 2 * HEAD :] = tail[:, :HEAD]


def project_far(acc, rest, b0, b1, frames):
    packet = jax.ShapeDtypeStruct((BLK + 16, 3 * HEAD), BF16)
    return pl.pallas_call(
        far_kernel,
        out_shape=(packet, packet),
        in_specs=[VMEM] * 5,
        out_specs=(VMEM,) * 2,
        cost_estimate=pl.CostEstimate(
            flops=2 * BLK * 512 * 768, bytes_accessed=2 << 20, transcendentals=0
        ),
        compiler_params=vmem(16),
        name="project_far",
    )(acc, rest, b0, b1, frames)


def join_kernel(own, got, kv, q):
    row = lax.broadcasted_iota(jnp.int32, (16, BLK), 0)
    both = [ref[BLK:, : 2 * HEAD].astype(F32) for ref in (own, got)]
    tail = jnp.where(row == 0, both[0], both[1])
    for i, ref in enumerate((own, got)):
        rows = slice(i * BLK, (i + 1) * BLK)
        kv[rows, :] = ref[:BLK, : 2 * HEAD]
        q[rows, :] = ref[:BLK, 2 * HEAD :]
    kv[2 * BLK :, :] = tail.astype(BF16)
    row = lax.broadcasted_iota(jnp.int32, (16, HEAD), 0)
    parts = [b[:, h * HEAD : (h + 1) * HEAD] for b in both for h in range(2)]
    lines = jnp.where(row == 0, parts[0], jnp.where(row == 1, parts[1], jnp.where(row == 2, parts[2], parts[3])))
    q[2 * BLK :, :] = lines.astype(BF16)


def join(own, got):
    return pl.pallas_call(
        join_kernel,
        out_shape=(
            jax.ShapeDtypeStruct((2 * BLK + 16, 2 * HEAD), BF16),
            jax.ShapeDtypeStruct((2 * BLK + 16, HEAD), BF16),
        ),
        in_specs=[VMEM] * 2,
        out_specs=(VMEM,) * 2,
        cost_estimate=pl.CostEstimate(flops=BLK * BLK, bytes_accessed=1 << 19, transcendentals=0),
        compiler_params=vmem(8),
        name="join",
    )(own, got)


def visit(q_s, f_s, m_s, l_s, acc_s, kv, masked):
    scale = 1.0 / math.sqrt(HEAD)
    if masked:
        lines = [jnp.broadcast_to(kv[r : r + 1, :].astype(F32), (HEAD, BLK)) for r in (2 * BLK, 2 * BLK + 1)]
        frames = jnp.concatenate([jnp.transpose(line)[:, :1] for line in lines], axis=0)

    def part(i, carry):
        lanes = pl.ds(pl.multiple_of(i * BLK, BLK), BLK)
        s = nt_dot(kv[: 2 * BLK, :HEAD], q_s[lanes, :]) * scale
        if masked:
            allowed = frames <= f_s[:, lanes]
            s = jnp.where(allowed, s, NEG)
        old = m_s[:, lanes]
        top = jnp.maximum(old, jnp.max(s, axis=0, keepdims=True))
        decay = jnp.exp(old - top)
        p = jnp.exp(s - top)
        if masked:
            p = jnp.where(allowed, p, 0.0)
        m_s[:, lanes] = top
        l_s[:, lanes] = l_s[:, lanes] * decay + jnp.sum(p, axis=0, keepdims=True)
        acc_s[:, lanes] = acc_s[:, lanes] * decay + tn_dot(kv[: 2 * BLK, HEAD:], p.astype(BF16))
        return carry

    lax.fori_loop(0, 4, part, 0)


def local_kernel(mine, theirs, kv, q_s, f_s, m_s, l_s, acc_s):
    for g, q in enumerate((mine, theirs)):
        q_s[g * 2 * BLK : (g + 1) * 2 * BLK, :] = q[: 2 * BLK, :]
        for i in range(4):
            lanes = slice((g * 4 + i) * HEAD, (g * 4 + i + 1) * HEAD)
            f_s[:, lanes] = q[2 * BLK + i : 2 * BLK + i + 1, :].astype(F32)
    m_s[...] = jnp.full_like(m_s, NEG)
    l_s[...] = jnp.zeros_like(l_s)
    acc_s[...] = jnp.zeros_like(acc_s)
    visit(q_s, f_s, m_s, l_s, acc_s, kv, True)


STATE = (
    jax.ShapeDtypeStruct((4 * BLK, HEAD), BF16),
    jax.ShapeDtypeStruct((1, 4 * BLK), F32),
    jax.ShapeDtypeStruct((1, 4 * BLK), F32),
    jax.ShapeDtypeStruct((1, 4 * BLK), F32),
    jax.ShapeDtypeStruct((HEAD, 4 * BLK), F32),
)


def visit_cost(blocks):
    work = 1024 * BLK * blocks
    return pl.CostEstimate(flops=4 * work * HEAD, bytes_accessed=2 << 20, transcendentals=work)


def local(mine, theirs, kv):
    return pl.pallas_call(
        local_kernel,
        out_shape=STATE,
        in_specs=[VMEM] * 3,
        out_specs=(VMEM,) * 5,
        cost_estimate=visit_cost(4),
        compiler_params=vmem(24),
        name="local",
    )(mine, theirs, kv)


def step_kernel(k, q_s, f_s, m_i, l_i, acc_i, f, b, m_s, l_s, acc_s, kv):
    z = lax.axis_index("z")
    m_s[...] = m_i[...]
    l_s[...] = l_i[...]
    acc_s[...] = acc_i[...]
    wrapped = z + k >= 8
    if k == 1:
        wrapped = wrapped | (lax.axis_index("yh") == 0)

    def side(j, carry):
        @pl.when((j == 0) & (z >= k))
        def _():
            kv[...] = f[...]

        @pl.when((j == 1) & wrapped)
        def _():
            kv[...] = b[...]

        @pl.when(((j == 0) & (z >= k)) | ((j == 1) & wrapped))
        def _():
            visit(q_s, f_s, m_s, l_s, acc_s, kv, k == 1)

        return carry

    lax.fori_loop(0, 2, side, 0)


def step(k, state, f, b):
    m, l, acc = pl.pallas_call(
        functools.partial(step_kernel, k),
        out_shape=STATE[2:],
        in_specs=[VMEM] * 7,
        out_specs=(VMEM,) * 3,
        scratch_shapes=[pltpu.VMEM(f.shape, BF16)],
        cost_estimate=visit_cost(4),
        compiler_params=vmem(24),
        name="step",
    )(*state, f, b)
    return state[0], state[1], m, l, acc


def last_kernel(q_s, f_s, m_i, l_i, acc_i, kv, mine, theirs, m_s, l_s, acc_s):
    m_s[...] = m_i[...]
    l_s[...] = l_i[...]
    acc_s[...] = acc_i[...]

    @pl.when(lax.axis_index("z") >= 4)
    def _():
        visit(q_s, f_s, m_s, l_s, acc_s, kv, False)

    for g, out in enumerate((mine, theirs)):
        lanes = slice(g * 2 * BLK, (g + 1) * 2 * BLK)
        total = l_s[:, lanes]
        some = total > 0.0
        safe = jnp.where(some, total, 1.0)
        out[:HEAD, :] = (acc_s[:, lanes] * (1.0 / safe)).astype(BF16)
        log = jnp.where(some, m_s[:, lanes] + jnp.log(safe), NEG)
        row = lax.broadcasted_iota(jnp.int32, (16, 2 * BLK), 0)
        high = log.astype(BF16).astype(F32)
        middle = (log - high).astype(BF16).astype(F32)
        low = log - high - middle
        terms = jnp.where(row == 0, high, jnp.where(row == 1, middle, jnp.where(row == 2, low, 0.0)))
        out[HEAD:, :] = terms.astype(BF16)


def last(state, kv):
    return pl.pallas_call(
        last_kernel,
        out_shape=(jax.ShapeDtypeStruct((HEAD + 16, 2 * BLK), BF16),) * 2,
        in_specs=[VMEM] * 6,
        out_specs=(VMEM,) * 2,
        scratch_shapes=[pltpu.VMEM(s.shape, s.dtype) for s in STATE[2:]],
        cost_estimate=visit_cost(2),
        compiler_params=vmem(24),
        name="last",
    )(*state, kv)


def merge_kernel(a, b, mine, other):
    la = jnp.sum(a[HEAD:, :].astype(F32), axis=0, keepdims=True)
    lb = jnp.sum(b[HEAD:, :].astype(F32), axis=0, keepdims=True)
    top = jnp.maximum(la, lb)
    wa, wb = jnp.exp(la - top), jnp.exp(lb - top)
    inv = 1.0 / (wa + wb)
    total = (a[:HEAD, :].astype(F32) * (wa * inv) + b[:HEAD, :].astype(F32) * (wb * inv)).astype(BF16)
    mine[...] = total[:, :BLK]
    other[...] = total[:, BLK:]


def merge(a, b):
    half = jax.ShapeDtypeStruct((HEAD, BLK), BF16)
    return pl.pallas_call(
        merge_kernel,
        out_shape=(half, half),
        in_specs=[VMEM] * 2,
        out_specs=(VMEM,) * 2,
        cost_estimate=pl.CostEstimate(flops=1 << 18, bytes_accessed=1 << 19, transcendentals=1024),
        compiler_params=vmem(8),
        name="merge",
    )(a, b)


def output_kernel(mine, other, w, *outs):
    first = lax.axis_index("c") == 0
    a, b = (jnp.transpose(ref[...].astype(F32)) for ref in (mine, other))
    rows = jnp.concatenate([jnp.where(first, a, b), jnp.where(first, b, a)], axis=1).astype(BF16)
    for out, shift in zip(outs, NEAR + FAR):
        out[...] = jnp.dot(rows, w[:, target_cols(*shift)], preferred_element_type=F32).astype(BF16)


def target_cols(dx, dy):
    x, yl = lax.axis_index("x"), lax.axis_index("yl")
    target = ((x + dx) % 4) * 2 + (yl + dy) % 2
    return pl.ds(pl.multiple_of(target * BLK, BLK), BLK)


def output(mine, other, w):
    return pl.pallas_call(
        output_kernel,
        out_shape=(jax.ShapeDtypeStruct((BLK, BLK), BF16),) * 8,
        in_specs=[VMEM] * 3,
        out_specs=(VMEM,) * 8,
        cost_estimate=pl.CostEstimate(
            flops=2 * BLK * BLK * 2048, bytes_accessed=3 << 20, transcendentals=0
        ),
        compiler_params=vmem(16),
        name="output",
    )(mine, other, w)


def add_kernel(a0, b0, a1, b1, out0, out1):
    out0[...] = (a0[...].astype(F32) + b0[...].astype(F32)).astype(BF16)
    out1[...] = (a1[...].astype(F32) + b1[...].astype(F32)).astype(BF16)


def add_pairs(a0, b0, a1, b1):
    return pl.pallas_call(
        add_kernel,
        out_shape=(jax.ShapeDtypeStruct(a0.shape, BF16),) * 2,
        in_specs=[VMEM] * 4,
        out_specs=(VMEM,) * 2,
        cost_estimate=pl.CostEstimate(flops=a0.size, bytes_accessed=12 * a0.size, transcendentals=0),
        compiler_params=vmem(8),
        name="add_pairs",
    )(a0, b0, a1, b1)


def sum_kernel(*refs):
    total = refs[0][...].astype(F32)
    for ref in refs[1:-1]:
        total = total + ref[...].astype(F32)
    refs[-1][...] = total.astype(BF16)


def sum_all(terms):
    return pl.pallas_call(
        sum_kernel,
        out_shape=jax.ShapeDtypeStruct(terms[0].shape, BF16),
        in_specs=[VMEM] * len(terms),
        out_specs=VMEM,
        cost_estimate=pl.CostEstimate(
            flops=6 * terms[0].size, bytes_accessed=14 * terms[0].size, transcendentals=0
        ),
        compiler_params=vmem(8),
        name="sum_all",
    )(*terms)


def slots_kernel(*refs):
    terms = refs[:6]
    stream, slot, mixed, rows = refs[6:]
    total = stream[...].astype(F32)
    for term in terms:
        total = total + term[...].astype(F32)
    kept = total.astype(BF16)
    mixed[...] = kept
    ids = lax.broadcasted_iota(jnp.int32, (EXPERTS * CAP, BLK), 0)
    pick = jnp.where(ids == slot[...], 1.0, 0.0).astype(BF16)
    rows[...] = jnp.dot(pick, kept, preferred_element_type=F32).astype(BF16)


def to_slots(terms, stream, slot):
    return pl.pallas_call(
        slots_kernel,
        out_shape=(
            jax.ShapeDtypeStruct((BLK, BLK), BF16),
            jax.ShapeDtypeStruct((EXPERTS * CAP, BLK), BF16),
        ),
        in_specs=[VMEM] * 8,
        out_specs=(VMEM, VMEM),
        cost_estimate=pl.CostEstimate(
            flops=2 * 512 * BLK * BLK, bytes_accessed=2 << 20, transcendentals=0
        ),
        compiler_params=vmem(16),
        name="slots",
    )(*terms, stream, slot)


UNITS = 704
WIDE = 768
SOME = 64


def prepare(blocks, shifts, places, gain, n_s, square):
    def some_rows(i, carry):
        at = pl.ds(pl.multiple_of(i * SOME, SOME), SOME)
        total = None
        for block, shift, cols in zip(blocks, shifts, places):
            v = block[at, :].astype(F32)
            n_s[at, cols] = (v * gain[:, source_rows(*shift)]).astype(BF16)
            total = v * v if total is None else total + v * v
        square[at, :] = jnp.sum(total, axis=1, keepdims=True)
        return carry

    lax.fori_loop(0, blocks[0].shape[0] // SOME, some_rows, 0)


def expert_near_kernel(*refs):
    blocks = refs[:6]
    gain, own, far = refs[6:9]
    acc, square, rest, w2 = refs[9:13]
    n_s, w1, sem = refs[13:]
    half = UNITS // 2
    places = [(w1, 0), (w1, WIDE), (w2, 0)]
    copies = [
        pltpu.make_async_copy(
            src.at[pl.ds(i * half, half), :], dst.at[pl.ds(at + j * half, half), :], sem.at[3 * j + i]
        )
        for i, (dst, at) in enumerate(places)
        for j, src in enumerate((own, far))
    ]
    for copy in copies:
        copy.start()
    pad = jnp.zeros((WIDE - UNITS, 2048), BF16)
    w1[UNITS:WIDE, :] = pad
    w1[WIDE + UNITS :, :] = pad
    w2[UNITS:, :] = pad
    for shift in FAR:
        n_s[:, source_rows(*shift)] = jnp.zeros((n_s.shape[0], BLK), BF16)
    prepare(blocks, NEAR, [source_rows(*shift) for shift in NEAR], gain, n_s, square)
    for copy in copies:
        copy.wait()
    for j, shift in enumerate(FAR):
        rest[:, j * BLK : (j + 1) * BLK] = w1[:, source_rows(*shift)]

    def tile(j, carry):
        cols = pl.ds(pl.multiple_of(j * BLK, BLK), BLK)
        acc[:, cols] = nt_dot(n_s[...], w1[cols, :])
        return carry

    lax.fori_loop(0, 2 * WIDE // BLK, tile, 0)


def expert_near(blocks, gain, own, far):
    rows = blocks[0].shape[0]
    return pl.pallas_call(
        expert_near_kernel,
        out_shape=(
            jax.ShapeDtypeStruct((rows, 2 * WIDE), F32),
            jax.ShapeDtypeStruct((rows, 1), F32),
            jax.ShapeDtypeStruct((2 * WIDE, 2 * BLK), BF16),
            jax.ShapeDtypeStruct((WIDE, 2048), BF16),
        ),
        in_specs=[VMEM] * 7 + [HBM] * 2,
        out_specs=(VMEM,) * 4,
        scratch_shapes=[
            pltpu.VMEM((rows, 2048), BF16),
            pltpu.VMEM((2 * WIDE, 2048), BF16),
            pltpu.SemaphoreType.DMA((6,)),
        ],
        cost_estimate=pl.CostEstimate(
            flops=4 * rows * 2048 * WIDE, bytes_accessed=13 << 20, transcendentals=0
        ),
        compiler_params=vmem(24),
        name="expert_near",
    )(*blocks, gain, own, far)


def expert_far_kernel(b0, b1, gain, acc, square, rest, w2, *refs):
    outs = refs[:8]
    n_s, h_s, r_s = refs[8:]
    rows = n_s.shape[0]
    prepare((b0, b1), FAR, (slice(0, BLK), slice(BLK, 2 * BLK)), gain, n_s, r_s)
    factor = lax.rsqrt((square[...] + r_s[...]) * (1.0 / 2048) + NORM_EPS)

    def hidden(j, carry):
        cols = pl.ds(pl.multiple_of(j * BLK, BLK), BLK)
        later = pl.ds(pl.multiple_of(WIDE + j * BLK, BLK), BLK)
        g = (acc[:, cols] + nt_dot(n_s[...], rest[cols, :])) * factor
        u = (acc[:, later] + nt_dot(n_s[...], rest[later, :])) * factor
        h_s[:, cols] = (g / (1.0 + jnp.exp(-g)) * u).astype(BF16)
        return carry

    lax.fori_loop(0, WIDE // BLK, hidden, 0)

    def lower(i, carry):
        at = pl.ds(pl.multiple_of(i * BLK, BLK), BLK)
        for out, shift in zip(outs, NEAR + FAR):
            out[at, :] = jnp.dot(
                h_s[at, :], w2[:, target_cols(*shift)], preferred_element_type=F32
            ).astype(BF16)
        return carry

    lax.fori_loop(0, rows // BLK, lower, 0)


def expert_far(b0, b1, gain, acc, square, rest, w2):
    rows = b0.shape[0]
    return pl.pallas_call(
        expert_far_kernel,
        out_shape=(jax.ShapeDtypeStruct(b0.shape, BF16),) * 8,
        in_specs=[VMEM] * 7,
        out_specs=(VMEM,) * 8,
        scratch_shapes=[
            pltpu.VMEM((rows, 2 * BLK), BF16),
            pltpu.VMEM((rows, WIDE), BF16),
            pltpu.VMEM((rows, 1), F32),
        ],
        cost_estimate=pl.CostEstimate(
            flops=4 * rows * 1024 * WIDE, bytes_accessed=10 << 20, transcendentals=rows * WIDE
        ),
        compiler_params=vmem(24),
        name="expert_far",
    )(b0, b1, gain, acc, square, rest, w2)


def finish_kernel(mixed, rows, slot, out):
    ids = lax.broadcasted_iota(jnp.int32, (EXPERTS * CAP, BLK), 0)
    pick = jnp.where(ids == slot[...], 1.0, 0.0).astype(BF16)
    out[...] = (mixed[...].astype(F32) + tn_dot(pick, rows[...])).astype(BF16)


def finish(mixed, rows, slot):
    return pl.pallas_call(
        finish_kernel,
        out_shape=jax.ShapeDtypeStruct((BLK, BLK), BF16),
        in_specs=[VMEM] * 3,
        out_specs=VMEM,
        cost_estimate=pl.CostEstimate(
            flops=2 * 512 * BLK * BLK, bytes_accessed=1 << 20, transcendentals=0
        ),
        compiler_params=vmem(8),
        name="finish",
    )(mixed, rows, slot)


def tp_shift(a, dx, dy):
    pairs = [(i * 2 + j, ((i + dx) % 4) * 2 + (j + dy) % 2) for i in range(4) for j in range(2)]
    return lax.ppermute(a, TP, pairs)


def tp_gather(a):
    near = [a] + [tp_shift(a, *s) for s in NEAR[1:]]
    return near + [tp_shift(near[1], 1, 0), tp_shift(near[2], 3, 0)]


def tp_scatter(pieces):
    got = tp_shift(pieces[6], 1, 0), tp_shift(pieces[7], 3, 0)
    straight = [tp_shift(p, *s) for p, s in zip(pieces[3:6], NEAR[3:6])]
    sums = add_pairs(pieces[1], got[0], pieces[2], got[1])
    return [pieces[0]] + straight + [tp_shift(p, *s) for p, s in zip(sums, NEAR[1:3])]


def swap(a, dy, dc):
    pairs = [(i * 2 + j, (i ^ dy) * 2 + (j ^ dc)) for i in range(2) for j in range(2)]
    return lax.ppermute(a, ("yh", "c"), pairs)


def ring(a, step):
    return lax.ppermute(a, "z", [(i, (i + step) % 8) for i in range(8)])


def attention(blocks, wq, wk, wv, frames, weights):
    acc, rest = project_near(blocks[:6], fetch(wk, wv, wq))
    own, other = project_far(acc, rest, *blocks[6:], frames)
    kv, q = join(own, swap(other, 0, 1))
    f, b = ring(kv, 1), ring(kv, -1)
    theirs = swap(q, 1, 0)
    f, b, theirs = lax.optimization_barrier((f, b, theirs))
    state = local(q, theirs, kv)
    for k in range(1, 4):
        if k == 2:
            f, b, *held = lax.optimization_barrier((f, b, *state, *weights))
            state, weights = held[:5], held[5:]
            weights = jnp.concatenate(weights, axis=0)
        if k == 3:
            f, b, weights, *state = lax.optimization_barrier((f, b, weights, *state))
        here = f, b
        if k < 3:
            f, b = ring(f, 1), ring(b, -1)
        else:
            way = jnp.where(lax.axis_index("c") == 0, f, b)
            hops = [(i * 2 + c, (i + (-1 if c else 1)) % 8 * 2 + c) for i in range(8) for c in range(2)]
            far = lax.ppermute(way, ("z", "c"), hops)
        state = step(k, state, *here)
    mine, theirs = last(state, far)
    mine, other = merge(mine, swap(theirs, 1, 0))
    return mine, swap(other, 0, 1), weights


def shards(stream, frames, fidelity, wq, wk, wv, wo, gain, gate, up, down):
    route = fidelity[:, 0]
    spot = lax.iota(jnp.int32, BLK)
    same = (route[:, None] == route[None, :]) & (spot[None, :] < spot[:, None])
    slot = (route * CAP + jnp.sum(same.astype(jnp.int32), axis=1))[None, :]
    gain = gain[None, :]

    expert_weights = (gate[0].T, up[0].T, down[0])
    mine, other, own = attention(tp_gather(stream), wq, wk, wv, frames[None, :], expert_weights)
    mixed, rows = to_slots(tp_scatter(output(mine, other, wo)), stream, slot)

    sending, rows = lax.optimization_barrier((own, rows))
    far = lax.ppermute(sending, "c", [(0, 1), (1, 0)])
    sent = lax.all_to_all(rows.reshape(EXPERTS, CAP, BLK), CHIPS, 0, 0, tiled=True)
    sent, far = lax.optimization_barrier((sent, far))
    blocks = tp_gather(sent.reshape(EXPERTS * CAP, BLK))
    lowered = expert_far(*blocks[6:], gain, *expert_near(blocks[:6], gain, own, far))
    summed = sum_all(tp_scatter(lowered))
    back = lax.all_to_all(summed.reshape(EXPERTS, CAP, BLK), CHIPS, 0, 0, tiled=True)
    return finish(mixed, back.reshape(EXPERTS * CAP, BLK), slot)


def solution(mesh):
    axes = ("z", "yh", "c", "x", "yl")
    fine = Mesh(np.asarray(mesh.devices).reshape(8, 2, 2, 4, 2), axes)
    return jax.shard_map(
        shards,
        mesh=fine,
        in_specs=(
            P(SEQ, TP),
            P(SEQ),
            P(SEQ, None),
            P(None, TP),
            P(None, TP),
            P(None, TP),
            P(TP, None),
            P(),
            P(SEQ, None, TP),
            P(SEQ, None, TP),
            P(SEQ, TP, None),
        ),
        out_specs=P(SEQ, TP),
        check_vma=False,
    )
```

```python
import functools
import math

import jax
import jax.numpy as jnp
import numpy as np
from jax import lax
from jax.experimental import pallas as pl
from jax.experimental.pallas import tpu as pltpu
from jax.sharding import Mesh, PartitionSpec as P

HEAD = 128
EXPERTS = 16
CAP = 32
BLK = 256
NEG = -1e30
NORM_EPS = 1e-05
SEQ = ("z", "yh", "c")
CHIPS = ("z", "yh")
TP = ("x", "yl")
NEAR = ((0, 0), (1, 0), (3, 1), (3, 0), (1, 1), (0, 1))
FAR = ((2, 0), (2, 1))
F32 = jnp.float32
BF16 = jnp.bfloat16

VMEM = pl.BlockSpec(memory_space=pltpu.VMEM)
HBM = pl.BlockSpec(memory_space=pltpu.HBM)


def nt_dot(a, b):
    return lax.dot_general(a, b, (((1,), (1,)), ((), ())), preferred_element_type=F32)


def tn_dot(a, b):
    return lax.dot_general(a, b, (((0,), (0,)), ((), ())), preferred_element_type=F32)


def vmem(mib):
    return pltpu.CompilerParams(vmem_limit_bytes=mib << 20)


def source_rows(dx, dy):
    x, yl = lax.axis_index("x"), lax.axis_index("yl")
    source = ((x + 4 - dx) % 4) * 2 + (yl + dy) % 2
    return pl.ds(pl.multiple_of(source * BLK, BLK), BLK)


def fetch_kernel(wk, wv, wq, out, sem):
    copies = [
        pltpu.make_async_copy(src, out.at[:, pl.ds(i * BLK, BLK)], sem.at[i])
        for i, src in enumerate((wk, wv, wq))
    ]
    for copy in copies:
        copy.start()
    for copy in copies:
        copy.wait()


def fetch(*weights):
    return pl.pallas_call(
        fetch_kernel,
        out_shape=jax.ShapeDtypeStruct((2048, 3 * BLK), BF16),
        in_specs=[HBM] * 3,
        out_specs=VMEM,
        scratch_shapes=[pltpu.SemaphoreType.DMA((3,))],
        cost_estimate=pl.CostEstimate(flops=0, bytes_accessed=6 << 20, transcendentals=0),
        compiler_params=vmem(8),
        name="fetch",
    )(*weights)


def near_kernel(*refs):
    blocks = refs[:6]
    weights, acc, rest = refs[6:]

    def some(i, carry):
        cols = pl.ds(pl.multiple_of(i * BLK, BLK), BLK)
        total = None
        for block, shift in zip(blocks, NEAR):
            term = jnp.dot(block[...], weights[source_rows(*shift), cols], preferred_element_type=F32)
            total = term if total is None else total + term
        acc[:, cols] = total
        for j, shift in enumerate(FAR):
            rest[j * BLK : (j + 1) * BLK, cols] = weights[source_rows(*shift), cols]
        return carry

    lax.fori_loop(0, 3, some, 0)


def project_near(blocks, weights):
    return pl.pallas_call(
        near_kernel,
        out_shape=(
            jax.ShapeDtypeStruct((BLK, 3 * BLK), F32),
            jax.ShapeDtypeStruct((2 * BLK, 3 * BLK), BF16),
        ),
        in_specs=[VMEM] * 7,
        out_specs=(VMEM,) * 2,
        cost_estimate=pl.CostEstimate(
            flops=2 * BLK * 1536 * 768, bytes_accessed=5 << 20, transcendentals=0
        ),
        compiler_params=vmem(20),
        name="project_near",
    )(*blocks, weights)


def far_kernel(acc, rest, b0, b1, frames, own, other):
    first = lax.axis_index("c") == 0

    def some(i, carry):
        cols = pl.ds(pl.multiple_of(i * BLK, BLK), BLK)
        total = acc[:, cols]
        for j, block in enumerate((b0, b1)):
            total = total + jnp.dot(
                block[...], rest[j * BLK : (j + 1) * BLK, cols], preferred_element_type=F32
            )
        left, right = total[:, :HEAD], total[:, HEAD:]
        cols = pl.ds(pl.multiple_of(i * HEAD, HEAD), HEAD)
        own[:BLK, cols] = jnp.where(first, left, right).astype(BF16)
        other[:BLK, cols] = jnp.where(first, right, left).astype(BF16)
        return carry

    lax.fori_loop(0, 3, some, 0)
    tail = jnp.broadcast_to(frames[...], (16, BLK)).astype(BF16)
    for out in (own, other):
        out[BLK:, : 2 * HEAD] = tail
        out[BLK:, 2 * HEAD :] = tail[:, :HEAD]


def project_far(acc, rest, b0, b1, frames):
    packet = jax.ShapeDtypeStruct((BLK + 16, 3 * HEAD), BF16)
    return pl.pallas_call(
        far_kernel,
        out_shape=(packet, packet),
        in_specs=[VMEM] * 5,
        out_specs=(VMEM,) * 2,
        cost_estimate=pl.CostEstimate(
            flops=2 * BLK * 512 * 768, bytes_accessed=2 << 20, transcendentals=0
        ),
        compiler_params=vmem(16),
        name="project_far",
    )(acc, rest, b0, b1, frames)


def join_kernel(own, got, kv, q):
    row = lax.broadcasted_iota(jnp.int32, (16, BLK), 0)
    both = [ref[BLK:, : 2 * HEAD].astype(F32) for ref in (own, got)]
    tail = jnp.where(row == 0, both[0], both[1])
    for i, ref in enumerate((own, got)):
        rows = slice(i * BLK, (i + 1) * BLK)
        kv[rows, :] = ref[:BLK, : 2 * HEAD]
        q[rows, :] = ref[:BLK, 2 * HEAD :]
    kv[2 * BLK :, :] = tail.astype(BF16)
    row = lax.broadcasted_iota(jnp.int32, (16, HEAD), 0)
    parts = [b[:, h * HEAD : (h + 1) * HEAD] for b in both for h in range(2)]
    lines = jnp.where(row == 0, parts[0], jnp.where(row == 1, parts[1], jnp.where(row == 2, parts[2], parts[3])))
    q[2 * BLK :, :] = lines.astype(BF16)


def join(own, got):
    return pl.pallas_call(
        join_kernel,
        out_shape=(
            jax.ShapeDtypeStruct((2 * BLK + 16, 2 * HEAD), BF16),
            jax.ShapeDtypeStruct((2 * BLK + 16, HEAD), BF16),
        ),
        in_specs=[VMEM] * 2,
        out_specs=(VMEM,) * 2,
        cost_estimate=pl.CostEstimate(flops=BLK * BLK, bytes_accessed=1 << 19, transcendentals=0),
        compiler_params=vmem(8),
        name="join",
    )(own, got)


def visit(q_s, f_s, m_s, l_s, acc_s, kv, masked):
    scale = 1.0 / math.sqrt(HEAD)
    if masked:
        lines = [jnp.broadcast_to(kv[r : r + 1, :].astype(F32), (HEAD, BLK)) for r in (2 * BLK, 2 * BLK + 1)]
        frames = jnp.concatenate([jnp.transpose(line)[:, :1] for line in lines], axis=0)

    def part(i, carry):
        lanes = pl.ds(pl.multiple_of(i * BLK, BLK), BLK)
        s = nt_dot(kv[: 2 * BLK, :HEAD], q_s[lanes, :]) * scale
        if masked:
            allowed = frames <= f_s[:, lanes]
            s = jnp.where(allowed, s, NEG)
        old = m_s[:, lanes]
        top = jnp.maximum(old, jnp.max(s, axis=0, keepdims=True))
        decay = jnp.exp(old - top)
        p = jnp.exp(s - top)
        if masked:
            p = jnp.where(allowed, p, 0.0)
        m_s[:, lanes] = top
        l_s[:, lanes] = l_s[:, lanes] * decay + jnp.sum(p, axis=0, keepdims=True)
        acc_s[:, lanes] = acc_s[:, lanes] * decay + tn_dot(kv[: 2 * BLK, HEAD:], p.astype(BF16))
        return carry

    lax.fori_loop(0, 4, part, 0)


def local_kernel(mine, theirs, kv, q_s, f_s, m_s, l_s, acc_s):
    for g, q in enumerate((mine, theirs)):
        q_s[g * 2 * BLK : (g + 1) * 2 * BLK, :] = q[: 2 * BLK, :]
        for i in range(4):
            lanes = slice((g * 4 + i) * HEAD, (g * 4 + i + 1) * HEAD)
            f_s[:, lanes] = q[2 * BLK + i : 2 * BLK + i + 1, :].astype(F32)
    m_s[...] = jnp.full_like(m_s, NEG)
    l_s[...] = jnp.zeros_like(l_s)
    acc_s[...] = jnp.zeros_like(acc_s)
    visit(q_s, f_s, m_s, l_s, acc_s, kv, True)


STATE = (
    jax.ShapeDtypeStruct((4 * BLK, HEAD), BF16),
    jax.ShapeDtypeStruct((1, 4 * BLK), F32),
    jax.ShapeDtypeStruct((1, 4 * BLK), F32),
    jax.ShapeDtypeStruct((1, 4 * BLK), F32),
    jax.ShapeDtypeStruct((HEAD, 4 * BLK), F32),
)


def visit_cost(blocks):
    work = 1024 * BLK * blocks
    return pl.CostEstimate(flops=4 * work * HEAD, bytes_accessed=2 << 20, transcendentals=work)


def local(mine, theirs, kv):
    return pl.pallas_call(
        local_kernel,
        out_shape=STATE,
        in_specs=[VMEM] * 3,
        out_specs=(VMEM,) * 5,
        cost_estimate=visit_cost(4),
        compiler_params=vmem(24),
        name="local",
    )(mine, theirs, kv)


def step_kernel(k, q_s, f_s, m_i, l_i, acc_i, f, b, m_s, l_s, acc_s, kv):
    z = lax.axis_index("z")
    m_s[...] = m_i[...]
    l_s[...] = l_i[...]
    acc_s[...] = acc_i[...]
    wrapped = z + k >= 8
    if k == 1:
        wrapped = wrapped | (lax.axis_index("yh") == 0)

    def side(j, carry):
        @pl.when((j == 0) & (z >= k))
        def _():
            kv[...] = f[...]

        @pl.when((j == 1) & wrapped)
        def _():
            kv[...] = b[...]

        @pl.when(((j == 0) & (z >= k)) | ((j == 1) & wrapped))
        def _():
            visit(q_s, f_s, m_s, l_s, acc_s, kv, k == 1)

        return carry

    lax.fori_loop(0, 2, side, 0)


def step(k, state, f, b):
    m, l, acc = pl.pallas_call(
        functools.partial(step_kernel, k),
        out_shape=STATE[2:],
        in_specs=[VMEM] * 7,
        out_specs=(VMEM,) * 3,
        scratch_shapes=[pltpu.VMEM(f.shape, BF16)],
        cost_estimate=visit_cost(4),
        compiler_params=vmem(24),
        name="step",
    )(*state, f, b)
    return state[0], state[1], m, l, acc


def last_kernel(q_s, f_s, m_i, l_i, acc_i, kv, mine, theirs, m_s, l_s, acc_s):
    m_s[...] = m_i[...]
    l_s[...] = l_i[...]
    acc_s[...] = acc_i[...]

    @pl.when(lax.axis_index("z") >= 4)
    def _():
        visit(q_s, f_s, m_s, l_s, acc_s, kv, False)

    for g, out in enumerate((mine, theirs)):
        lanes = slice(g * 2 * BLK, (g + 1) * 2 * BLK)
        total = l_s[:, lanes]
        some = total > 0.0
        safe = jnp.where(some, total, 1.0)
        out[:HEAD, :] = (acc_s[:, lanes] * (1.0 / safe)).astype(BF16)
        log = jnp.where(some, m_s[:, lanes] + jnp.log(safe), NEG)
        row = lax.broadcasted_iota(jnp.int32, (16, 2 * BLK), 0)
        high = log.astype(BF16).astype(F32)
        middle = (log - high).astype(BF16).astype(F32)
        low = log - high - middle
        terms = jnp.where(row == 0, high, jnp.where(row == 1, middle, jnp.where(row == 2, low, 0.0)))
        out[HEAD:, :] = terms.astype(BF16)


def last(state, kv):
    return pl.pallas_call(
        last_kernel,
        out_shape=(jax.ShapeDtypeStruct((HEAD + 16, 2 * BLK), BF16),) * 2,
        in_specs=[VMEM] * 6,
        out_specs=(VMEM,) * 2,
        scratch_shapes=[pltpu.VMEM(s.shape, s.dtype) for s in STATE[2:]],
        cost_estimate=visit_cost(2),
        compiler_params=vmem(24),
        name="last",
    )(*state, kv)


def merge_kernel(a, b, mine, other):
    la = jnp.sum(a[HEAD:, :].astype(F32), axis=0, keepdims=True)
    lb = jnp.sum(b[HEAD:, :].astype(F32), axis=0, keepdims=True)
    top = jnp.maximum(la, lb)
    wa, wb = jnp.exp(la - top), jnp.exp(lb - top)
    inv = 1.0 / (wa + wb)
    total = (a[:HEAD, :].astype(F32) * (wa * inv) + b[:HEAD, :].astype(F32) * (wb * inv)).astype(BF16)
    mine[...] = total[:, :BLK]
    other[...] = total[:, BLK:]


def merge(a, b):
    half = jax.ShapeDtypeStruct((HEAD, BLK), BF16)
    return pl.pallas_call(
        merge_kernel,
        out_shape=(half, half),
        in_specs=[VMEM] * 2,
        out_specs=(VMEM,) * 2,
        cost_estimate=pl.CostEstimate(flops=1 << 18, bytes_accessed=1 << 19, transcendentals=1024),
        compiler_params=vmem(8),
        name="merge",
    )(a, b)


def output_kernel(mine, other, w, *outs):
    first = lax.axis_index("c") == 0
    a, b = (jnp.transpose(ref[...].astype(F32)) for ref in (mine, other))
    rows = jnp.concatenate([jnp.where(first, a, b), jnp.where(first, b, a)], axis=1).astype(BF16)
    for out, shift in zip(outs, NEAR + FAR):
        out[...] = jnp.dot(rows, w[:, target_cols(*shift)], preferred_element_type=F32).astype(BF16)


def target_cols(dx, dy):
    x, yl = lax.axis_index("x"), lax.axis_index("yl")
    target = ((x + dx) % 4) * 2 + (yl + dy) % 2
    return pl.ds(pl.multiple_of(target * BLK, BLK), BLK)


def output(mine, other, w):
    return pl.pallas_call(
        output_kernel,
        out_shape=(jax.ShapeDtypeStruct((BLK, BLK), BF16),) * 8,
        in_specs=[VMEM] * 3,
        out_specs=(VMEM,) * 8,
        cost_estimate=pl.CostEstimate(
            flops=2 * BLK * BLK * 2048, bytes_accessed=3 << 20, transcendentals=0
        ),
        compiler_params=vmem(16),
        name="output",
    )(mine, other, w)


def add_kernel(a0, b0, a1, b1, out0, out1):
    out0[...] = (a0[...].astype(F32) + b0[...].astype(F32)).astype(BF16)
    out1[...] = (a1[...].astype(F32) + b1[...].astype(F32)).astype(BF16)


def add_pairs(a0, b0, a1, b1):
    return pl.pallas_call(
        add_kernel,
        out_shape=(jax.ShapeDtypeStruct(a0.shape, BF16),) * 2,
        in_specs=[VMEM] * 4,
        out_specs=(VMEM,) * 2,
        cost_estimate=pl.CostEstimate(flops=a0.size, bytes_accessed=12 * a0.size, transcendentals=0),
        compiler_params=vmem(8),
        name="add_pairs",
    )(a0, b0, a1, b1)


def sum_kernel(*refs):
    total = refs[0][...].astype(F32)
    for ref in refs[1:-1]:
        total = total + ref[...].astype(F32)
    refs[-1][...] = total.astype(BF16)


def sum_all(terms):
    return pl.pallas_call(
        sum_kernel,
        out_shape=jax.ShapeDtypeStruct(terms[0].shape, BF16),
        in_specs=[VMEM] * len(terms),
        out_specs=VMEM,
        cost_estimate=pl.CostEstimate(
            flops=6 * terms[0].size, bytes_accessed=14 * terms[0].size, transcendentals=0
        ),
        compiler_params=vmem(8),
        name="sum_all",
    )(*terms)


def slots_kernel(*refs):
    terms = refs[:6]
    stream, slot, mixed, rows = refs[6:]
    total = stream[...].astype(F32)
    for term in terms:
        total = total + term[...].astype(F32)
    kept = total.astype(BF16)
    mixed[...] = kept
    ids = lax.broadcasted_iota(jnp.int32, (EXPERTS * CAP, BLK), 0)
    pick = jnp.where(ids == slot[...], 1.0, 0.0).astype(BF16)
    rows[...] = jnp.dot(pick, kept, preferred_element_type=F32).astype(BF16)


def to_slots(terms, stream, slot):
    return pl.pallas_call(
        slots_kernel,
        out_shape=(
            jax.ShapeDtypeStruct((BLK, BLK), BF16),
            jax.ShapeDtypeStruct((EXPERTS * CAP, BLK), BF16),
        ),
        in_specs=[VMEM] * 8,
        out_specs=(VMEM, VMEM),
        cost_estimate=pl.CostEstimate(
            flops=2 * 512 * BLK * BLK, bytes_accessed=2 << 20, transcendentals=0
        ),
        compiler_params=vmem(16),
        name="slots",
    )(*terms, stream, slot)


UNITS = 704
WIDE = 768
SOME = 64


def prepare(blocks, shifts, places, gain, n_s, square):
    def some_rows(i, carry):
        at = pl.ds(pl.multiple_of(i * SOME, SOME), SOME)
        total = None
        for block, shift, cols in zip(blocks, shifts, places):
            v = block[at, :].astype(F32)
            n_s[at, cols] = (v * gain[:, source_rows(*shift)]).astype(BF16)
            total = v * v if total is None else total + v * v
        square[at, :] = jnp.sum(total, axis=1, keepdims=True)
        return carry

    lax.fori_loop(0, blocks[0].shape[0] // SOME, some_rows, 0)


EARLY = 3


def ready_kernel(b0, b1, b2, gain, own, far, w1, w2, n_s, square, sem):
    half = UNITS // 2
    copies = [
        pltpu.make_async_copy(
            src.at[pl.ds(i * half, half), :], dst.at[pl.ds(at + j * half, half), :], sem.at[3 * j + i]
        )
        for i, (dst, at) in enumerate([(w1, 0), (w1, WIDE), (w2, 0)])
        for j, src in enumerate((own, far))
    ]
    for copy in copies:
        copy.start()
    pad = jnp.zeros((WIDE - UNITS, 2048), BF16)
    w1[UNITS:WIDE, :] = pad
    w1[WIDE + UNITS :, :] = pad
    w2[UNITS:, :] = pad
    places = [slice(j * BLK, (j + 1) * BLK) for j in range(EARLY)]
    prepare((b0, b1, b2), NEAR[:EARLY], places, gain, n_s, square)
    for copy in copies:
        copy.wait()


def expert_ready(blocks, gain, own, far):
    rows = blocks[0].shape[0]
    return pl.pallas_call(
        ready_kernel,
        out_shape=(
            jax.ShapeDtypeStruct((2 * WIDE, 2048), BF16),
            jax.ShapeDtypeStruct((WIDE, 2048), BF16),
            jax.ShapeDtypeStruct((rows, EARLY * BLK), BF16),
            jax.ShapeDtypeStruct((rows, 1), F32),
        ),
        in_specs=[VMEM] * 4 + [HBM] * 2,
        out_specs=(VMEM,) * 4,
        scratch_shapes=[pltpu.SemaphoreType.DMA((6,))],
        cost_estimate=pl.CostEstimate(flops=1 << 20, bytes_accessed=18 << 20, transcendentals=0),
        compiler_params=vmem(16),
        name="expert_ready",
    )(*blocks, gain, own, far)


def lower(h_s, w2, outs, shifts):
    def some_rows(i, carry):
        at = pl.ds(pl.multiple_of(i * BLK, BLK), BLK)
        for out, shift in zip(outs, shifts):
            out[at, :] = jnp.dot(
                h_s[at, :], w2[:, target_cols(*shift)], preferred_element_type=F32
            ).astype(BF16)
        return carry

    lax.fori_loop(0, h_s.shape[0] // BLK, some_rows, 0)


def hidden_kernel(*refs):
    blocks = refs[:5]
    gain, w1, w2, early, square, h_s, o0, o1, n_s, r_s = refs[5:]
    for j, shift in enumerate(NEAR[:EARLY]):
        n_s[:, source_rows(*shift)] = early[:, j * BLK : (j + 1) * BLK]
    shifts = NEAR[EARLY:] + FAR
    prepare(blocks, shifts, [source_rows(*shift) for shift in shifts], gain, n_s, r_s)
    factor = lax.rsqrt((square[...] + r_s[...]) * (1.0 / 2048) + NORM_EPS)

    def tile(j, carry):
        cols = pl.ds(pl.multiple_of(j * BLK, BLK), BLK)
        later = pl.ds(pl.multiple_of(WIDE + j * BLK, BLK), BLK)
        g = nt_dot(n_s[...], w1[cols, :]) * factor
        u = nt_dot(n_s[...], w1[later, :]) * factor
        h_s[:, cols] = (g / (1.0 + jnp.exp(-g)) * u).astype(BF16)
        return carry

    lax.fori_loop(0, WIDE // BLK, tile, 0)
    lower(h_s, w2, (o0, o1), FAR)


def expert_hidden(blocks, gain, w1, w2, early, square):
    rows = blocks[0].shape[0]
    piece = jax.ShapeDtypeStruct((rows, BLK), BF16)
    return pl.pallas_call(
        hidden_kernel,
        out_shape=(jax.ShapeDtypeStruct((rows, WIDE), BF16), piece, piece),
        in_specs=[VMEM] * 10,
        out_specs=(VMEM,) * 3,
        scratch_shapes=[pltpu.VMEM((rows, 2048), BF16), pltpu.VMEM((rows, 1), F32)],
        cost_estimate=pl.CostEstimate(
            flops=5 * rows * 2048 * WIDE, bytes_accessed=13 << 20, transcendentals=rows * WIDE
        ),
        compiler_params=vmem(16),
        name="expert_hidden",
    )(*blocks, gain, w1, w2, early, square)


def lower_kernel(h_s, w2, *outs):
    lower(h_s, w2, outs, NEAR)


def expert_lower(h, w2):
    rows = h.shape[0]
    return pl.pallas_call(
        lower_kernel,
        out_shape=(jax.ShapeDtypeStruct((rows, BLK), BF16),) * 6,
        in_specs=[VMEM] * 2,
        out_specs=(VMEM,) * 6,
        cost_estimate=pl.CostEstimate(
            flops=2 * rows * 1536 * WIDE, bytes_accessed=6 << 20, transcendentals=0
        ),
        compiler_params=vmem(16),
        name="expert_lower",
    )(h, w2)


def finish_kernel(mixed, rows, slot, out):
    ids = lax.broadcasted_iota(jnp.int32, (EXPERTS * CAP, BLK), 0)
    pick = jnp.where(ids == slot[...], 1.0, 0.0).astype(BF16)
    out[...] = (mixed[...].astype(F32) + tn_dot(pick, rows[...])).astype(BF16)


def finish(mixed, rows, slot):
    return pl.pallas_call(
        finish_kernel,
        out_shape=jax.ShapeDtypeStruct((BLK, BLK), BF16),
        in_specs=[VMEM] * 3,
        out_specs=VMEM,
        cost_estimate=pl.CostEstimate(
            flops=2 * 512 * BLK * BLK, bytes_accessed=1 << 20, transcendentals=0
        ),
        compiler_params=vmem(8),
        name="finish",
    )(mixed, rows, slot)


def tp_shift(a, dx, dy):
    pairs = [(i * 2 + j, ((i + dx) % 4) * 2 + (j + dy) % 2) for i in range(4) for j in range(2)]
    return lax.ppermute(a, TP, pairs)


def tp_gather(a):
    near = [a] + [tp_shift(a, *s) for s in NEAR[1:]]
    return near + [tp_shift(near[1], 1, 0), tp_shift(near[2], 3, 0)]


def tp_scatter(pieces):
    got = tp_shift(pieces[6], 1, 0), tp_shift(pieces[7], 3, 0)
    straight = [tp_shift(p, *s) for p, s in zip(pieces[3:6], NEAR[3:6])]
    sums = add_pairs(pieces[1], got[0], pieces[2], got[1])
    return [pieces[0]] + straight + [tp_shift(p, *s) for p, s in zip(sums, NEAR[1:3])]


def swap(a, dy, dc):
    pairs = [(i * 2 + j, (i ^ dy) * 2 + (j ^ dc)) for i in range(2) for j in range(2)]
    return lax.ppermute(a, ("yh", "c"), pairs)


def ring(a, step):
    return lax.ppermute(a, "z", [(i, (i + step) % 8) for i in range(8)])


def attention(blocks, wq, wk, wv, frames, weights):
    acc, rest = project_near(blocks[:6], fetch(wk, wv, wq))
    own, other = project_far(acc, rest, *blocks[6:], frames)
    kv, q = join(own, swap(other, 0, 1))
    f, b = ring(kv, 1), ring(kv, -1)
    theirs = swap(q, 1, 0)
    f, b, theirs = lax.optimization_barrier((f, b, theirs))
    state = local(q, theirs, kv)
    for k in range(1, 4):
        if k == 2:
            f, b, *held = lax.optimization_barrier((f, b, *state, *weights))
            state, weights = held[:5], held[5:]
            weights = jnp.concatenate(weights, axis=0)
        if k == 3:
            f, b, weights, *state = lax.optimization_barrier((f, b, weights, *state))
        here = f, b
        if k < 3:
            f, b = ring(f, 1), ring(b, -1)
        else:
            way = jnp.where(lax.axis_index("c") == 0, f, b)
            hops = [(i * 2 + c, (i + (-1 if c else 1)) % 8 * 2 + c) for i in range(8) for c in range(2)]
            far = lax.ppermute(way, ("z", "c"), hops)
        state = step(k, state, *here)
    mine, theirs = last(state, far)
    mine, other = merge(mine, swap(theirs, 1, 0))
    return mine, swap(other, 0, 1), weights


def shards(stream, frames, fidelity, wq, wk, wv, wo, gain, gate, up, down):
    route = fidelity[:, 0]
    spot = lax.iota(jnp.int32, BLK)
    same = (route[:, None] == route[None, :]) & (spot[None, :] < spot[:, None])
    slot = (route * CAP + jnp.sum(same.astype(jnp.int32), axis=1))[None, :]
    gain = gain[None, :]

    expert_weights = (gate[0].T, up[0].T, down[0])
    mine, other, own = attention(tp_gather(stream), wq, wk, wv, frames[None, :], expert_weights)
    mixed, rows = to_slots(tp_scatter(output(mine, other, wo)), stream, slot)

    sending, rows = lax.optimization_barrier((own, rows))
    far = lax.ppermute(sending, "c", [(0, 1), (1, 0)])
    sent = lax.all_to_all(rows.reshape(EXPERTS, CAP, BLK), CHIPS, 0, 0, tiled=True)
    sent, far = lax.optimization_barrier((sent, far))
    blocks = tp_gather(sent.reshape(EXPERTS * CAP, BLK))
    w1, w2, *early = expert_ready(blocks[:EARLY], gain, own, far)
    h, *far_pieces = expert_hidden(blocks[EARLY:], gain, w1, w2, *early)
    summed = sum_all(tp_scatter([*expert_lower(h, w2), *far_pieces]))
    back = lax.all_to_all(summed.reshape(EXPERTS, CAP, BLK), CHIPS, 0, 0, tiled=True)
    return finish(mixed, back.reshape(EXPERTS * CAP, BLK), slot)


def solution(mesh):
    axes = ("z", "yh", "c", "x", "yl")
    fine = Mesh(np.asarray(mesh.devices).reshape(8, 2, 2, 4, 2), axes)
    return jax.shard_map(
        shards,
        mesh=fine,
        in_specs=(
            P(SEQ, TP),
            P(SEQ),
            P(SEQ, None),
            P(None, TP),
            P(None, TP),
            P(None, TP),
            P(TP, None),
            P(),
            P(SEQ, None, TP),
            P(SEQ, None, TP),
            P(SEQ, TP, None),
        ),
        out_specs=P(SEQ, TP),
        check_vma=False,
    )
```

```python
import functools
import math

import jax
import jax.numpy as jnp
import numpy as np
from jax import lax
from jax.experimental import pallas as pl
from jax.experimental.pallas import tpu as pltpu
from jax.sharding import Mesh, PartitionSpec as P

HEAD = 128
EXPERTS = 16
CAP = 32
BLK = 256
NEG = -1e30
NORM_EPS = 1e-05
SEQ = ("z", "yh", "c")
CHIPS = ("z", "yh")
TP = ("x", "yl")
NEAR = ((0, 0), (1, 0), (3, 1), (0, 1), (1, 1), (3, 0))
FAR = ((2, 0), (2, 1))
F32 = jnp.float32
BF16 = jnp.bfloat16

VMEM = pl.BlockSpec(memory_space=pltpu.VMEM)
HBM = pl.BlockSpec(memory_space=pltpu.HBM)


def nt_dot(a, b):
    return lax.dot_general(a, b, (((1,), (1,)), ((), ())), preferred_element_type=F32)


def tn_dot(a, b):
    return lax.dot_general(a, b, (((0,), (0,)), ((), ())), preferred_element_type=F32)


def vmem(mib):
    return pltpu.CompilerParams(vmem_limit_bytes=mib << 20)


def source_rows(dx, dy):
    x, yl = lax.axis_index("x"), lax.axis_index("yl")
    source = ((x + 4 - dx) % 4) * 2 + (yl + dy) % 2
    return pl.ds(pl.multiple_of(source * BLK, BLK), BLK)


def near_kernel(*refs):
    blocks = refs[:6]
    weights, acc, rest = refs[6:]

    def some(i, carry):
        cols = pl.ds(pl.multiple_of(i * BLK, BLK), BLK)
        total = None
        for block, shift in zip(blocks, NEAR):
            term = jnp.dot(block[...], weights[source_rows(*shift), cols], preferred_element_type=F32)
            total = term if total is None else total + term
        acc[:, cols] = total
        for j, shift in enumerate(FAR):
            rest[j * BLK : (j + 1) * BLK, cols] = weights[source_rows(*shift), cols]
        return carry

    lax.fori_loop(0, 3, some, 0)


def project_near(blocks, weights):
    return pl.pallas_call(
        near_kernel,
        out_shape=(
            jax.ShapeDtypeStruct((BLK, 3 * BLK), F32),
            jax.ShapeDtypeStruct((2 * BLK, 3 * BLK), BF16),
        ),
        in_specs=[VMEM] * 7,
        out_specs=(VMEM,) * 2,
        cost_estimate=pl.CostEstimate(
            flops=2 * BLK * 1536 * 768, bytes_accessed=5 << 20, transcendentals=0
        ),
        compiler_params=vmem(20),
        name="project_near",
    )(*blocks, weights)


def far_kernel(acc, rest, b0, b1, frames, own, other):
    first = lax.axis_index("c") == 0

    def some(i, carry):
        cols = pl.ds(pl.multiple_of(i * BLK, BLK), BLK)
        total = acc[:, cols]
        for j, block in enumerate((b0, b1)):
            total = total + jnp.dot(
                block[...], rest[j * BLK : (j + 1) * BLK, cols], preferred_element_type=F32
            )
        left, right = total[:, :HEAD], total[:, HEAD:]
        cols = pl.ds(pl.multiple_of(i * HEAD, HEAD), HEAD)
        own[:BLK, cols] = jnp.where(first, left, right).astype(BF16)
        other[:BLK, cols] = jnp.where(first, right, left).astype(BF16)
        return carry

    lax.fori_loop(0, 3, some, 0)
    tail = jnp.broadcast_to(frames[...], (16, BLK)).astype(BF16)
    for out in (own, other):
        out[BLK:, : 2 * HEAD] = tail
        out[BLK:, 2 * HEAD :] = tail[:, :HEAD]


def project_far(acc, rest, b0, b1, frames):
    packet = jax.ShapeDtypeStruct((BLK + 16, 3 * HEAD), BF16)
    return pl.pallas_call(
        far_kernel,
        out_shape=(packet, packet),
        in_specs=[VMEM] * 5,
        out_specs=(VMEM,) * 2,
        cost_estimate=pl.CostEstimate(
            flops=2 * BLK * 512 * 768, bytes_accessed=2 << 20, transcendentals=0
        ),
        compiler_params=vmem(16),
        name="project_far",
    )(acc, rest, b0, b1, frames)


def join_kernel(own, got, kv, q):
    row = lax.broadcasted_iota(jnp.int32, (16, BLK), 0)
    both = [ref[BLK:, : 2 * HEAD].astype(F32) for ref in (own, got)]
    tail = jnp.where(row == 0, both[0], both[1])
    for i, ref in enumerate((own, got)):
        rows = slice(i * BLK, (i + 1) * BLK)
        kv[rows, :] = ref[:BLK, : 2 * HEAD]
        q[rows, :] = ref[:BLK, 2 * HEAD :]
    kv[2 * BLK :, :] = tail.astype(BF16)
    row = lax.broadcasted_iota(jnp.int32, (16, HEAD), 0)
    parts = [b[:, h * HEAD : (h + 1) * HEAD] for b in both for h in range(2)]
    lines = jnp.where(row == 0, parts[0], jnp.where(row == 1, parts[1], jnp.where(row == 2, parts[2], parts[3])))
    q[2 * BLK :, :] = lines.astype(BF16)


def join(own, got):
    return pl.pallas_call(
        join_kernel,
        out_shape=(
            jax.ShapeDtypeStruct((2 * BLK + 16, 2 * HEAD), BF16),
            jax.ShapeDtypeStruct((2 * BLK + 16, HEAD), BF16),
        ),
        in_specs=[VMEM] * 2,
        out_specs=(VMEM,) * 2,
        cost_estimate=pl.CostEstimate(flops=BLK * BLK, bytes_accessed=1 << 19, transcendentals=0),
        compiler_params=vmem(8),
        name="join",
    )(own, got)


def visit(q_s, f_s, m_s, l_s, acc_s, kv, masked):
    scale = 1.0 / math.sqrt(HEAD)
    if masked:
        lines = [jnp.broadcast_to(kv[r : r + 1, :].astype(F32), (HEAD, BLK)) for r in (2 * BLK, 2 * BLK + 1)]
        frames = jnp.concatenate([jnp.transpose(line)[:, :1] for line in lines], axis=0)

    def part(i, carry):
        lanes = pl.ds(pl.multiple_of(i * BLK, BLK), BLK)
        s = nt_dot(kv[: 2 * BLK, :HEAD], q_s[lanes, :]) * scale
        if masked:
            allowed = frames <= f_s[:, lanes]
            s = jnp.where(allowed, s, NEG)
        old = m_s[:, lanes]
        top = jnp.maximum(old, jnp.max(s, axis=0, keepdims=True))
        decay = jnp.exp(old - top)
        p = jnp.exp(s - top)
        if masked:
            p = jnp.where(allowed, p, 0.0)
        m_s[:, lanes] = top
        l_s[:, lanes] = l_s[:, lanes] * decay + jnp.sum(p, axis=0, keepdims=True)
        acc_s[:, lanes] = acc_s[:, lanes] * decay + tn_dot(kv[: 2 * BLK, HEAD:], p.astype(BF16))
        return carry

    lax.fori_loop(0, 4, part, 0)


def local_kernel(mine, theirs, kv, q_s, f_s, m_s, l_s, acc_s):
    for g, q in enumerate((mine, theirs)):
        q_s[g * 2 * BLK : (g + 1) * 2 * BLK, :] = q[: 2 * BLK, :]
        for i in range(4):
            lanes = slice((g * 4 + i) * HEAD, (g * 4 + i + 1) * HEAD)
            f_s[:, lanes] = q[2 * BLK + i : 2 * BLK + i + 1, :].astype(F32)
    m_s[...] = jnp.full_like(m_s, NEG)
    l_s[...] = jnp.zeros_like(l_s)
    acc_s[...] = jnp.zeros_like(acc_s)
    visit(q_s, f_s, m_s, l_s, acc_s, kv, True)


STATE = (
    jax.ShapeDtypeStruct((4 * BLK, HEAD), BF16),
    jax.ShapeDtypeStruct((1, 4 * BLK), F32),
    jax.ShapeDtypeStruct((1, 4 * BLK), F32),
    jax.ShapeDtypeStruct((1, 4 * BLK), F32),
    jax.ShapeDtypeStruct((HEAD, 4 * BLK), F32),
)


def visit_cost(blocks):
    work = 1024 * BLK * blocks
    return pl.CostEstimate(flops=4 * work * HEAD, bytes_accessed=2 << 20, transcendentals=work)


def local(mine, theirs, kv):
    return pl.pallas_call(
        local_kernel,
        out_shape=STATE,
        in_specs=[VMEM] * 3,
        out_specs=(VMEM,) * 5,
        cost_estimate=visit_cost(4),
        compiler_params=vmem(24),
        name="local",
    )(mine, theirs, kv)


def step_kernel(k, q_s, f_s, m_i, l_i, acc_i, f, b, m_s, l_s, acc_s, kv):
    z = lax.axis_index("z")
    m_s[...] = m_i[...]
    l_s[...] = l_i[...]
    acc_s[...] = acc_i[...]
    wrapped = z + k >= 8
    if k == 1:
        wrapped = wrapped | (lax.axis_index("yh") == 0)

    def side(j, carry):
        @pl.when((j == 0) & (z >= k))
        def _():
            kv[...] = f[...]

        @pl.when((j == 1) & wrapped)
        def _():
            kv[...] = b[...]

        @pl.when(((j == 0) & (z >= k)) | ((j == 1) & wrapped))
        def _():
            visit(q_s, f_s, m_s, l_s, acc_s, kv, k == 1)

        return carry

    lax.fori_loop(0, 2, side, 0)


def step(k, state, f, b):
    m, l, acc = pl.pallas_call(
        functools.partial(step_kernel, k),
        out_shape=STATE[2:],
        in_specs=[VMEM] * 7,
        out_specs=(VMEM,) * 3,
        scratch_shapes=[pltpu.VMEM(f.shape, BF16)],
        cost_estimate=visit_cost(4),
        compiler_params=vmem(24),
        name="step",
    )(*state, f, b)
    return state[0], state[1], m, l, acc


def last_kernel(q_s, f_s, m_i, l_i, acc_i, kv, mine, theirs, m_s, l_s, acc_s):
    m_s[...] = m_i[...]
    l_s[...] = l_i[...]
    acc_s[...] = acc_i[...]

    @pl.when(lax.axis_index("z") >= 4)
    def _():
        visit(q_s, f_s, m_s, l_s, acc_s, kv, False)

    for g, out in enumerate((mine, theirs)):
        lanes = slice(g * 2 * BLK, (g + 1) * 2 * BLK)
        total = l_s[:, lanes]
        some = total > 0.0
        safe = jnp.where(some, total, 1.0)
        out[:HEAD, :] = (acc_s[:, lanes] * (1.0 / safe)).astype(BF16)
        log = jnp.where(some, m_s[:, lanes] + jnp.log(safe), NEG)
        row = lax.broadcasted_iota(jnp.int32, (16, 2 * BLK), 0)
        high = log.astype(BF16).astype(F32)
        middle = (log - high).astype(BF16).astype(F32)
        low = log - high - middle
        terms = jnp.where(row == 0, high, jnp.where(row == 1, middle, jnp.where(row == 2, low, 0.0)))
        out[HEAD:, :] = terms.astype(BF16)


def last(state, kv):
    return pl.pallas_call(
        last_kernel,
        out_shape=(jax.ShapeDtypeStruct((HEAD + 16, 2 * BLK), BF16),) * 2,
        in_specs=[VMEM] * 6,
        out_specs=(VMEM,) * 2,
        scratch_shapes=[pltpu.VMEM(s.shape, s.dtype) for s in STATE[2:]],
        cost_estimate=visit_cost(2),
        compiler_params=vmem(24),
        name="last",
    )(*state, kv)


def merge_kernel(a, b, mine, other):
    la = jnp.sum(a[HEAD:, :].astype(F32), axis=0, keepdims=True)
    lb = jnp.sum(b[HEAD:, :].astype(F32), axis=0, keepdims=True)
    top = jnp.maximum(la, lb)
    wa, wb = jnp.exp(la - top), jnp.exp(lb - top)
    inv = 1.0 / (wa + wb)
    total = (a[:HEAD, :].astype(F32) * (wa * inv) + b[:HEAD, :].astype(F32) * (wb * inv)).astype(BF16)
    mine[...] = total[:, :BLK]
    other[...] = total[:, BLK:]


def merge(a, b):
    half = jax.ShapeDtypeStruct((HEAD, BLK), BF16)
    return pl.pallas_call(
        merge_kernel,
        out_shape=(half, half),
        in_specs=[VMEM] * 2,
        out_specs=(VMEM,) * 2,
        cost_estimate=pl.CostEstimate(flops=1 << 18, bytes_accessed=1 << 19, transcendentals=1024),
        compiler_params=vmem(8),
        name="merge",
    )(a, b)


def output_kernel(mine, other, w, *outs):
    first = lax.axis_index("c") == 0
    a, b = (jnp.transpose(ref[...].astype(F32)) for ref in (mine, other))
    rows = jnp.concatenate([jnp.where(first, a, b), jnp.where(first, b, a)], axis=1).astype(BF16)
    for out, shift in zip(outs, NEAR + FAR):
        out[...] = jnp.dot(rows, w[:, target_cols(*shift)], preferred_element_type=F32).astype(BF16)


def target_cols(dx, dy):
    x, yl = lax.axis_index("x"), lax.axis_index("yl")
    target = ((x + dx) % 4) * 2 + (yl + dy) % 2
    return pl.ds(pl.multiple_of(target * BLK, BLK), BLK)


def output(mine, other, w):
    return pl.pallas_call(
        output_kernel,
        out_shape=(jax.ShapeDtypeStruct((BLK, BLK), BF16),) * 8,
        in_specs=[VMEM] * 3,
        out_specs=(VMEM,) * 8,
        cost_estimate=pl.CostEstimate(
            flops=2 * BLK * BLK * 2048, bytes_accessed=3 << 20, transcendentals=0
        ),
        compiler_params=vmem(16),
        name="output",
    )(mine, other, w)


def add_kernel(a0, b0, a1, b1, out0, out1):
    out0[...] = (a0[...].astype(F32) + b0[...].astype(F32)).astype(BF16)
    out1[...] = (a1[...].astype(F32) + b1[...].astype(F32)).astype(BF16)


def add_pairs(a0, b0, a1, b1):
    return pl.pallas_call(
        add_kernel,
        out_shape=(jax.ShapeDtypeStruct(a0.shape, BF16),) * 2,
        in_specs=[VMEM] * 4,
        out_specs=(VMEM,) * 2,
        cost_estimate=pl.CostEstimate(flops=a0.size, bytes_accessed=12 * a0.size, transcendentals=0),
        compiler_params=vmem(8),
        name="add_pairs",
    )(a0, b0, a1, b1)


def sum_kernel(*refs):
    total = refs[0][...].astype(F32)
    for ref in refs[1:-1]:
        total = total + ref[...].astype(F32)
    refs[-1][...] = total.astype(BF16)


def sum_all(terms):
    return pl.pallas_call(
        sum_kernel,
        out_shape=jax.ShapeDtypeStruct(terms[0].shape, BF16),
        in_specs=[VMEM] * len(terms),
        out_specs=VMEM,
        cost_estimate=pl.CostEstimate(
            flops=6 * terms[0].size, bytes_accessed=14 * terms[0].size, transcendentals=0
        ),
        compiler_params=vmem(8),
        name="sum_all",
    )(*terms)


def slots_kernel(*refs):
    terms = refs[:6]
    stream, slot, mixed, rows = refs[6:]
    total = stream[...].astype(F32)
    for term in terms:
        total = total + term[...].astype(F32)
    kept = total.astype(BF16)
    mixed[...] = kept
    ids = lax.broadcasted_iota(jnp.int32, (EXPERTS * CAP, BLK), 0)
    pick = jnp.where(ids == slot[...], 1.0, 0.0).astype(BF16)
    rows[...] = jnp.dot(pick, kept, preferred_element_type=F32).astype(BF16)


def to_slots(terms, stream, slot):
    return pl.pallas_call(
        slots_kernel,
        out_shape=(
            jax.ShapeDtypeStruct((BLK, BLK), BF16),
            jax.ShapeDtypeStruct((EXPERTS * CAP, BLK), BF16),
        ),
        in_specs=[VMEM] * 8,
        out_specs=(VMEM, VMEM),
        cost_estimate=pl.CostEstimate(
            flops=2 * 512 * BLK * BLK, bytes_accessed=2 << 20, transcendentals=0
        ),
        compiler_params=vmem(16),
        name="slots",
    )(*terms, stream, slot)


UNITS = 704
WIDE = 768
SOME = 64


def prepare(blocks, shifts, places, gain, n_s, square):
    def some_rows(i, carry):
        at = pl.ds(pl.multiple_of(i * SOME, SOME), SOME)
        total = None
        for block, shift, cols in zip(blocks, shifts, places):
            v = block[at, :].astype(F32)
            n_s[at, cols] = (v * gain[:, source_rows(*shift)]).astype(BF16)
            total = v * v if total is None else total + v * v
        square[at, :] = jnp.sum(total, axis=1, keepdims=True)
        return carry

    lax.fori_loop(0, blocks[0].shape[0] // SOME, some_rows, 0)


FIRST_OUT = FAR + ((0, 1),)
NEXT_OUT = ((0, 0), (1, 0), (3, 1), (1, 1), (3, 0))
EARLY = 3


def ready_kernel(b0, b1, b2, gain, own, far, w1, w2, n_s, square, sem):
    half = UNITS // 2
    copies = [
        pltpu.make_async_copy(
            src.at[pl.ds(i * half, half), :], dst.at[pl.ds(at + j * half, half), :], sem.at[3 * j + i]
        )
        for i, (dst, at) in enumerate([(w1, 0), (w1, WIDE), (w2, 0)])
        for j, src in enumerate((own, far))
    ]
    for copy in copies:
        copy.start()
    pad = jnp.zeros((WIDE - UNITS, 2048), BF16)
    w1[UNITS:WIDE, :] = pad
    w1[WIDE + UNITS :, :] = pad
    w2[UNITS:, :] = pad
    places = [slice(j * BLK, (j + 1) * BLK) for j in range(EARLY)]
    prepare((b0, b1, b2), NEAR[:EARLY], places, gain, n_s, square)
    for copy in copies:
        copy.wait()


def expert_ready(blocks, gain, own, far):
    rows = blocks[0].shape[0]
    return pl.pallas_call(
        ready_kernel,
        out_shape=(
            jax.ShapeDtypeStruct((2 * WIDE, 2048), BF16),
            jax.ShapeDtypeStruct((WIDE, 2048), BF16),
            jax.ShapeDtypeStruct((rows, EARLY * BLK), BF16),
            jax.ShapeDtypeStruct((rows, 1), F32),
        ),
        in_specs=[VMEM] * 4 + [HBM] * 2,
        out_specs=(VMEM,) * 4,
        scratch_shapes=[pltpu.SemaphoreType.DMA((6,))],
        cost_estimate=pl.CostEstimate(flops=1 << 20, bytes_accessed=18 << 20, transcendentals=0),
        compiler_params=vmem(16),
        name="expert_ready",
    )(*blocks, gain, own, far)


def lower(h_s, w2, outs, shifts):
    def some_rows(i, carry):
        at = pl.ds(pl.multiple_of(i * BLK, BLK), BLK)
        for out, shift in zip(outs, shifts):
            out[at, :] = jnp.dot(
                h_s[at, :], w2[:, target_cols(*shift)], preferred_element_type=F32
            ).astype(BF16)
        return carry

    lax.fori_loop(0, h_s.shape[0] // BLK, some_rows, 0)


def hidden_kernel(*refs):
    blocks = refs[:5]
    gain, w1, w2, early, square, h_s, o0, o1, o2, n_s, r_s = refs[5:]
    for j, shift in enumerate(NEAR[:EARLY]):
        n_s[:, source_rows(*shift)] = early[:, j * BLK : (j + 1) * BLK]
    shifts = NEAR[EARLY:] + FAR
    prepare(blocks, shifts, [source_rows(*shift) for shift in shifts], gain, n_s, r_s)
    factor = lax.rsqrt((square[...] + r_s[...]) * (1.0 / 2048) + NORM_EPS)

    def tile(j, carry):
        cols = pl.ds(pl.multiple_of(j * BLK, BLK), BLK)
        later = pl.ds(pl.multiple_of(WIDE + j * BLK, BLK), BLK)
        g = nt_dot(n_s[...], w1[cols, :]) * factor
        u = nt_dot(n_s[...], w1[later, :]) * factor
        h_s[:, cols] = (g / (1.0 + jnp.exp(-g)) * u).astype(BF16)
        return carry

    lax.fori_loop(0, WIDE // BLK, tile, 0)
    lower(h_s, w2, (o0, o1, o2), FIRST_OUT)


def expert_hidden(blocks, gain, w1, w2, early, square):
    rows = blocks[0].shape[0]
    piece = jax.ShapeDtypeStruct((rows, BLK), BF16)
    return pl.pallas_call(
        hidden_kernel,
        out_shape=(jax.ShapeDtypeStruct((rows, WIDE), BF16), piece, piece, piece),
        in_specs=[VMEM] * 10,
        out_specs=(VMEM,) * 4,
        scratch_shapes=[pltpu.VMEM((rows, 2048), BF16), pltpu.VMEM((rows, 1), F32)],
        cost_estimate=pl.CostEstimate(
            flops=5 * rows * 2048 * WIDE, bytes_accessed=13 << 20, transcendentals=rows * WIDE
        ),
        compiler_params=vmem(16),
        name="expert_hidden",
    )(*blocks, gain, w1, w2, early, square)


def lower_kernel(h_s, w2, *outs):
    lower(h_s, w2, outs, NEXT_OUT)


def expert_lower(h, w2):
    rows = h.shape[0]
    return pl.pallas_call(
        lower_kernel,
        out_shape=(jax.ShapeDtypeStruct((rows, BLK), BF16),) * 5,
        in_specs=[VMEM] * 2,
        out_specs=(VMEM,) * 5,
        cost_estimate=pl.CostEstimate(
            flops=2 * rows * 1536 * WIDE, bytes_accessed=6 << 20, transcendentals=0
        ),
        compiler_params=vmem(16),
        name="expert_lower",
    )(h, w2)


def finish_kernel(mixed, rows, slot, out):
    ids = lax.broadcasted_iota(jnp.int32, (EXPERTS * CAP, BLK), 0)
    pick = jnp.where(ids == slot[...], 1.0, 0.0).astype(BF16)
    out[...] = (mixed[...].astype(F32) + tn_dot(pick, rows[...])).astype(BF16)


def finish(mixed, rows, slot):
    return pl.pallas_call(
        finish_kernel,
        out_shape=jax.ShapeDtypeStruct((BLK, BLK), BF16),
        in_specs=[VMEM] * 3,
        out_specs=VMEM,
        cost_estimate=pl.CostEstimate(
            flops=2 * 512 * BLK * BLK, bytes_accessed=1 << 20, transcendentals=0
        ),
        compiler_params=vmem(8),
        name="finish",
    )(mixed, rows, slot)


def tp_shift(a, dx, dy):
    pairs = [(i * 2 + j, ((i + dx) % 4) * 2 + (j + dy) % 2) for i in range(4) for j in range(2)]
    return lax.ppermute(a, TP, pairs)


def tp_gather(a):
    near = [a] + [tp_shift(a, *s) for s in NEAR[1:]]
    return near + [tp_shift(near[1], 1, 0), tp_shift(near[2], 3, 0)]


def tp_scatter(pieces, waves):
    got = tp_shift(pieces[6], 1, 0), tp_shift(pieces[7], 3, 0)
    beside = tp_shift(pieces[3], *NEAR[3])
    later = pieces[4:6]
    if waves:
        *got, beside, a, b = lax.optimization_barrier((*got, beside, *later))
        later = [a, b]
    sums = add_pairs(pieces[1], got[0], pieces[2], got[1])
    straight = [tp_shift(p, *s) for p, s in zip(later, NEAR[4:6])]
    return [pieces[0], beside] + straight + [tp_shift(p, *s) for p, s in zip(sums, NEAR[1:3])]


def swap(a, dy, dc):
    pairs = [(i * 2 + j, (i ^ dy) * 2 + (j ^ dc)) for i in range(2) for j in range(2)]
    return lax.ppermute(a, ("yh", "c"), pairs)


def ring(a, step):
    return lax.ppermute(a, "z", [(i, (i + step) % 8) for i in range(8)])


def attention(blocks, wq, wk, wv, frames, weights):
    acc, rest = project_near(blocks[:6], jnp.concatenate([wk, wv, wq], axis=1))
    own, other = project_far(acc, rest, *blocks[6:], frames)
    kv, q = join(own, swap(other, 0, 1))
    f, b = ring(kv, 1), ring(kv, -1)
    theirs = swap(q, 1, 0)
    f, b, theirs = lax.optimization_barrier((f, b, theirs))
    state = local(q, theirs, kv)
    for k in range(1, 4):
        if k == 2:
            f, b, *held = lax.optimization_barrier((f, b, *state, *weights))
            state, weights = held[:5], held[5:]
            weights = jnp.concatenate(weights, axis=0)
        if k == 3:
            f, b, weights, *state = lax.optimization_barrier((f, b, weights, *state))
        here = f, b
        if k < 3:
            f, b = ring(f, 1), ring(b, -1)
        else:
            way = jnp.where(lax.axis_index("c") == 0, f, b)
            hops = [(i * 2 + c, (i + (-1 if c else 1)) % 8 * 2 + c) for i in range(8) for c in range(2)]
            far = lax.ppermute(way, ("z", "c"), hops)
        state = step(k, state, *here)
    mine, theirs = last(state, far)
    mine, other = merge(mine, swap(theirs, 1, 0))
    return mine, swap(other, 0, 1), weights


def shards(stream, frames, fidelity, wq, wk, wv, wo, gain, gate, up, down):
    route = fidelity[:, 0]
    spot = lax.iota(jnp.int32, BLK)
    same = (route[:, None] == route[None, :]) & (spot[None, :] < spot[:, None])
    slot = (route * CAP + jnp.sum(same.astype(jnp.int32), axis=1))[None, :]
    gain = gain[None, :]

    expert_weights = (gate[0].T, up[0].T, down[0])
    mine, other, own = attention(tp_gather(stream), wq, wk, wv, frames[None, :], expert_weights)
    mixed, rows = to_slots(tp_scatter(output(mine, other, wo), False), stream, slot)

    sending, rows = lax.optimization_barrier((own, rows))
    far = lax.ppermute(sending, "c", [(0, 1), (1, 0)])
    sent = lax.all_to_all(rows.reshape(EXPERTS, CAP, BLK), CHIPS, 0, 0, tiled=True)
    sent, far = lax.optimization_barrier((sent, far))
    blocks = tp_gather(sent.reshape(EXPERTS * CAP, BLK))
    w1, w2, *early = expert_ready(blocks[:EARLY], gain, own, far)
    h, *lowered = expert_hidden(blocks[EARLY:], gain, w1, w2, *early)
    lowered = dict(zip(FIRST_OUT + NEXT_OUT, [*lowered, *expert_lower(h, w2)]))
    summed = sum_all(tp_scatter([lowered[shift] for shift in NEAR + FAR], True))
    back = lax.all_to_all(summed.reshape(EXPERTS, CAP, BLK), CHIPS, 0, 0, tiled=True)
    return finish(mixed, back.reshape(EXPERTS * CAP, BLK), slot)


def solution(mesh):
    axes = ("z", "yh", "c", "x", "yl")
    fine = Mesh(np.asarray(mesh.devices).reshape(8, 2, 2, 4, 2), axes)
    return jax.shard_map(
        shards,
        mesh=fine,
        in_specs=(
            P(SEQ, TP),
            P(SEQ),
            P(SEQ, None),
            P(None, TP),
            P(None, TP),
            P(None, TP),
            P(TP, None),
            P(),
            P(SEQ, None, TP),
            P(SEQ, None, TP),
            P(SEQ, TP, None),
        ),
        out_specs=P(SEQ, TP),
        check_vma=False,
    )
```

```python
import functools
import math

import jax
import jax.numpy as jnp
import numpy as np
from jax import lax
from jax.experimental import pallas as pl
from jax.experimental.pallas import tpu as pltpu
from jax.sharding import Mesh, PartitionSpec as P

HEAD = 128
EXPERTS = 16
CAP = 32
BLK = 256
NEG = -1e30
NORM_EPS = 1e-05
SEQ = ("z", "yh", "c")
CHIPS = ("z", "yh")
TP = ("x", "yl")
NEAR = ((0, 0), (1, 0), (3, 1), (0, 1), (1, 1), (3, 0))
FAR = ((2, 0), (2, 1))
F32 = jnp.float32
BF16 = jnp.bfloat16

VMEM = pl.BlockSpec(memory_space=pltpu.VMEM)
HBM = pl.BlockSpec(memory_space=pltpu.HBM)


def nt_dot(a, b):
    return lax.dot_general(a, b, (((1,), (1,)), ((), ())), preferred_element_type=F32)


def tn_dot(a, b):
    return lax.dot_general(a, b, (((0,), (0,)), ((), ())), preferred_element_type=F32)


def vmem(mib):
    return pltpu.CompilerParams(vmem_limit_bytes=mib << 20)


def source_rows(dx, dy):
    x, yl = lax.axis_index("x"), lax.axis_index("yl")
    source = ((x + 4 - dx) % 4) * 2 + (yl + dy) % 2
    return pl.ds(pl.multiple_of(source * BLK, BLK), BLK)


def near_kernel(*refs):
    blocks = refs[:6]
    weights, acc, rest = refs[6:]

    def some(i, carry):
        cols = pl.ds(pl.multiple_of(i * BLK, BLK), BLK)
        total = None
        for block, shift in zip(blocks, NEAR):
            term = jnp.dot(block[...], weights[source_rows(*shift), cols], preferred_element_type=F32)
            total = term if total is None else total + term
        acc[:, cols] = total
        for j, shift in enumerate(FAR):
            rest[j * BLK : (j + 1) * BLK, cols] = weights[source_rows(*shift), cols]
        return carry

    lax.fori_loop(0, 3, some, 0)


def project_near(blocks, weights):
    return pl.pallas_call(
        near_kernel,
        out_shape=(
            jax.ShapeDtypeStruct((BLK, 3 * BLK), F32),
            jax.ShapeDtypeStruct((2 * BLK, 3 * BLK), BF16),
        ),
        in_specs=[VMEM] * 7,
        out_specs=(VMEM,) * 2,
        cost_estimate=pl.CostEstimate(
            flops=2 * BLK * 1536 * 768, bytes_accessed=5 << 20, transcendentals=0
        ),
        compiler_params=vmem(20),
        name="project_near",
    )(*blocks, weights)


def far_kernel(acc, rest, b0, b1, frames, own, other):
    first = lax.axis_index("c") == 0

    def some(i, carry):
        cols = pl.ds(pl.multiple_of(i * BLK, BLK), BLK)
        total = acc[:, cols]
        for j, block in enumerate((b0, b1)):
            total = total + jnp.dot(
                block[...], rest[j * BLK : (j + 1) * BLK, cols], preferred_element_type=F32
            )
        left, right = total[:, :HEAD], total[:, HEAD:]
        cols = pl.ds(pl.multiple_of(i * HEAD, HEAD), HEAD)
        own[:BLK, cols] = jnp.where(first, left, right).astype(BF16)
        other[:BLK, cols] = jnp.where(first, right, left).astype(BF16)
        return carry

    lax.fori_loop(0, 3, some, 0)
    tail = jnp.broadcast_to(frames[...], (16, BLK)).astype(BF16)
    for out in (own, other):
        out[BLK:, : 2 * HEAD] = tail
        out[BLK:, 2 * HEAD :] = tail[:, :HEAD]


def project_far(acc, rest, b0, b1, frames):
    packet = jax.ShapeDtypeStruct((BLK + 16, 3 * HEAD), BF16)
    return pl.pallas_call(
        far_kernel,
        out_shape=(packet, packet),
        in_specs=[VMEM] * 5,
        out_specs=(VMEM,) * 2,
        cost_estimate=pl.CostEstimate(
            flops=2 * BLK * 512 * 768, bytes_accessed=2 << 20, transcendentals=0
        ),
        compiler_params=vmem(16),
        name="project_far",
    )(acc, rest, b0, b1, frames)


def join_kernel(own, got, kv, q):
    row = lax.broadcasted_iota(jnp.int32, (16, BLK), 0)
    both = [ref[BLK:, : 2 * HEAD].astype(F32) for ref in (own, got)]
    tail = jnp.where(row == 0, both[0], both[1])
    for i, ref in enumerate((own, got)):
        rows = slice(i * BLK, (i + 1) * BLK)
        kv[rows, :] = ref[:BLK, : 2 * HEAD]
        q[rows, :] = ref[:BLK, 2 * HEAD :]
    kv[2 * BLK :, :] = tail.astype(BF16)
    row = lax.broadcasted_iota(jnp.int32, (16, HEAD), 0)
    parts = [b[:, h * HEAD : (h + 1) * HEAD] for b in both for h in range(2)]
    lines = jnp.where(row == 0, parts[0], jnp.where(row == 1, parts[1], jnp.where(row == 2, parts[2], parts[3])))
    q[2 * BLK :, :] = lines.astype(BF16)


def join(own, got):
    return pl.pallas_call(
        join_kernel,
        out_shape=(
            jax.ShapeDtypeStruct((2 * BLK + 16, 2 * HEAD), BF16),
            jax.ShapeDtypeStruct((2 * BLK + 16, HEAD), BF16),
        ),
        in_specs=[VMEM] * 2,
        out_specs=(VMEM,) * 2,
        cost_estimate=pl.CostEstimate(flops=BLK * BLK, bytes_accessed=1 << 19, transcendentals=0),
        compiler_params=vmem(8),
        name="join",
    )(own, got)


def visit(q_s, f_s, m_s, l_s, acc_s, kv, masked, wide):
    scale = 1.0 / math.sqrt(HEAD)
    if masked:
        lines = [jnp.broadcast_to(kv[r : r + 1, :].astype(F32), (HEAD, BLK)) for r in (2 * BLK, 2 * BLK + 1)]
        frames = jnp.concatenate([jnp.transpose(line)[:, :1] for line in lines], axis=0)

    def part(i, carry):
        lanes = pl.ds(pl.multiple_of(i * wide, wide), wide)
        s = nt_dot(kv[: 2 * BLK, :HEAD], q_s[lanes, :]) * scale
        if masked:
            allowed = frames <= f_s[:, lanes]
            s = jnp.where(allowed, s, NEG)
        old = m_s[:, lanes]
        top = jnp.maximum(old, jnp.max(s, axis=0, keepdims=True))
        decay = jnp.exp(old - top)
        p = jnp.exp(s - top)
        if masked:
            p = jnp.where(allowed, p, 0.0)
        m_s[:, lanes] = top
        l_s[:, lanes] = l_s[:, lanes] * decay + jnp.sum(p, axis=0, keepdims=True)
        acc_s[:, lanes] = acc_s[:, lanes] * decay + tn_dot(kv[: 2 * BLK, HEAD:], p.astype(BF16))
        return carry

    lax.fori_loop(0, 4 * BLK // wide, part, 0)


def first_kernel(mine, theirs, own, f, b, q_s, f_s, m_s, l_s, acc_s, kv):
    for g, q in enumerate((mine, theirs)):
        q_s[g * 2 * BLK : (g + 1) * 2 * BLK, :] = q[: 2 * BLK, :]
        for i in range(4):
            lanes = slice((g * 4 + i) * HEAD, (g * 4 + i + 1) * HEAD)
            f_s[:, lanes] = q[2 * BLK + i : 2 * BLK + i + 1, :].astype(F32)
    m_s[...] = jnp.full_like(m_s, NEG)
    l_s[...] = jnp.zeros_like(l_s)
    acc_s[...] = jnp.zeros_like(acc_s)
    z = lax.axis_index("z")
    wanted = (z >= 0, z >= 1, (z == 7) | (lax.axis_index("yh") == 0))

    def side(j, carry):
        need = z < 0
        for i, (block, want) in enumerate(zip((own, f, b), wanted)):

            @pl.when((j == i) & want)
            def _():
                kv[...] = block[...]

            need = need | ((j == i) & want)

        @pl.when(need)
        def _():
            visit(q_s, f_s, m_s, l_s, acc_s, kv, True, 2 * BLK)

        return carry

    lax.fori_loop(0, 3, side, 0)


STATE = (
    jax.ShapeDtypeStruct((4 * BLK, HEAD), BF16),
    jax.ShapeDtypeStruct((1, 4 * BLK), F32),
    jax.ShapeDtypeStruct((1, 4 * BLK), F32),
    jax.ShapeDtypeStruct((1, 4 * BLK), F32),
    jax.ShapeDtypeStruct((HEAD, 4 * BLK), F32),
)


def visit_cost(blocks):
    work = 1024 * BLK * blocks
    return pl.CostEstimate(flops=4 * work * HEAD, bytes_accessed=2 << 20, transcendentals=work)


def first(mine, theirs, own, f, b):
    return pl.pallas_call(
        first_kernel,
        out_shape=STATE,
        in_specs=[VMEM] * 5,
        out_specs=(VMEM,) * 5,
        scratch_shapes=[pltpu.VMEM(f.shape, BF16)],
        cost_estimate=visit_cost(6),
        compiler_params=vmem(24),
        name="first",
    )(mine, theirs, own, f, b)


def step_kernel(k, q_s, f_s, m_i, l_i, acc_i, f, b, m_s, l_s, acc_s, kv):
    z = lax.axis_index("z")
    m_s[...] = m_i[...]
    l_s[...] = l_i[...]
    acc_s[...] = acc_i[...]

    def side(j, carry):
        @pl.when((j == 0) & (z >= k))
        def _():
            kv[...] = f[...]

        @pl.when((j == 1) & (z + k >= 8))
        def _():
            kv[...] = b[...]

        @pl.when(((j == 0) & (z >= k)) | ((j == 1) & (z + k >= 8)))
        def _():
            visit(q_s, f_s, m_s, l_s, acc_s, kv, False, BLK)

        return carry

    lax.fori_loop(0, 2, side, 0)


def step(k, state, f, b):
    m, l, acc = pl.pallas_call(
        functools.partial(step_kernel, k),
        out_shape=STATE[2:],
        in_specs=[VMEM] * 7,
        out_specs=(VMEM,) * 3,
        scratch_shapes=[pltpu.VMEM(f.shape, BF16)],
        cost_estimate=visit_cost(4),
        compiler_params=vmem(24),
        name="step",
    )(*state, f, b)
    return state[0], state[1], m, l, acc


def last_kernel(q_s, f_s, m_i, l_i, acc_i, kv, mine, theirs, m_s, l_s, acc_s):
    m_s[...] = m_i[...]
    l_s[...] = l_i[...]
    acc_s[...] = acc_i[...]

    @pl.when(lax.axis_index("z") >= 4)
    def _():
        visit(q_s, f_s, m_s, l_s, acc_s, kv, False, 2 * BLK)

    for g, out in enumerate((mine, theirs)):
        lanes = slice(g * 2 * BLK, (g + 1) * 2 * BLK)
        total = l_s[:, lanes]
        some = total > 0.0
        safe = jnp.where(some, total, 1.0)
        out[:HEAD, :] = (acc_s[:, lanes] * (1.0 / safe)).astype(BF16)
        log = jnp.where(some, m_s[:, lanes] + jnp.log(safe), NEG)
        row = lax.broadcasted_iota(jnp.int32, (16, 2 * BLK), 0)
        high = log.astype(BF16).astype(F32)
        middle = (log - high).astype(BF16).astype(F32)
        low = log - high - middle
        terms = jnp.where(row == 0, high, jnp.where(row == 1, middle, jnp.where(row == 2, low, 0.0)))
        out[HEAD:, :] = terms.astype(BF16)


def last(state, kv):
    return pl.pallas_call(
        last_kernel,
        out_shape=(jax.ShapeDtypeStruct((HEAD + 16, 2 * BLK), BF16),) * 2,
        in_specs=[VMEM] * 6,
        out_specs=(VMEM,) * 2,
        scratch_shapes=[pltpu.VMEM(s.shape, s.dtype) for s in STATE[2:]],
        cost_estimate=visit_cost(2),
        compiler_params=vmem(24),
        name="last",
    )(*state, kv)


def merge_kernel(a, b, mine, other):
    la = jnp.sum(a[HEAD:, :].astype(F32), axis=0, keepdims=True)
    lb = jnp.sum(b[HEAD:, :].astype(F32), axis=0, keepdims=True)
    top = jnp.maximum(la, lb)
    wa, wb = jnp.exp(la - top), jnp.exp(lb - top)
    inv = 1.0 / (wa + wb)
    total = (a[:HEAD, :].astype(F32) * (wa * inv) + b[:HEAD, :].astype(F32) * (wb * inv)).astype(BF16)
    mine[...] = total[:, :BLK]
    other[...] = total[:, BLK:]


def merge(a, b):
    half = jax.ShapeDtypeStruct((HEAD, BLK), BF16)
    return pl.pallas_call(
        merge_kernel,
        out_shape=(half, half),
        in_specs=[VMEM] * 2,
        out_specs=(VMEM,) * 2,
        cost_estimate=pl.CostEstimate(flops=1 << 18, bytes_accessed=1 << 19, transcendentals=1024),
        compiler_params=vmem(8),
        name="merge",
    )(a, b)


def output_kernel(mine, other, w, *outs):
    first = lax.axis_index("c") == 0
    a, b = (jnp.transpose(ref[...].astype(F32)) for ref in (mine, other))
    rows = jnp.concatenate([jnp.where(first, a, b), jnp.where(first, b, a)], axis=1).astype(BF16)
    for out, shift in zip(outs, NEAR + FAR):
        out[...] = jnp.dot(rows, w[:, target_cols(*shift)], preferred_element_type=F32).astype(BF16)


def target_cols(dx, dy):
    x, yl = lax.axis_index("x"), lax.axis_index("yl")
    target = ((x + dx) % 4) * 2 + (yl + dy) % 2
    return pl.ds(pl.multiple_of(target * BLK, BLK), BLK)


def output(mine, other, w):
    return pl.pallas_call(
        output_kernel,
        out_shape=(jax.ShapeDtypeStruct((BLK, BLK), BF16),) * 8,
        in_specs=[VMEM] * 3,
        out_specs=(VMEM,) * 8,
        cost_estimate=pl.CostEstimate(
            flops=2 * BLK * BLK * 2048, bytes_accessed=3 << 20, transcendentals=0
        ),
        compiler_params=vmem(16),
        name="output",
    )(mine, other, w)


def add_kernel(a0, b0, a1, b1, out0, out1):
    out0[...] = (a0[...].astype(F32) + b0[...].astype(F32)).astype(BF16)
    out1[...] = (a1[...].astype(F32) + b1[...].astype(F32)).astype(BF16)


def add_pairs(a0, b0, a1, b1):
    return pl.pallas_call(
        add_kernel,
        out_shape=(jax.ShapeDtypeStruct(a0.shape, BF16),) * 2,
        in_specs=[VMEM] * 4,
        out_specs=(VMEM,) * 2,
        cost_estimate=pl.CostEstimate(flops=a0.size, bytes_accessed=12 * a0.size, transcendentals=0),
        compiler_params=vmem(8),
        name="add_pairs",
    )(a0, b0, a1, b1)


def sum_kernel(*refs):
    total = refs[0][...].astype(F32)
    for ref in refs[1:-1]:
        total = total + ref[...].astype(F32)
    refs[-1][...] = total.astype(BF16)


def sum_all(terms):
    return pl.pallas_call(
        sum_kernel,
        out_shape=jax.ShapeDtypeStruct(terms[0].shape, BF16),
        in_specs=[VMEM] * len(terms),
        out_specs=VMEM,
        cost_estimate=pl.CostEstimate(
            flops=6 * terms[0].size, bytes_accessed=14 * terms[0].size, transcendentals=0
        ),
        compiler_params=vmem(8),
        name="sum_all",
    )(*terms)


def slots_kernel(*refs):
    terms = refs[:6]
    stream, slot, mixed, rows = refs[6:]
    total = stream[...].astype(F32)
    for term in terms:
        total = total + term[...].astype(F32)
    kept = total.astype(BF16)
    mixed[...] = kept
    ids = lax.broadcasted_iota(jnp.int32, (EXPERTS * CAP, BLK), 0)
    pick = jnp.where(ids == slot[...], 1.0, 0.0).astype(BF16)
    rows[...] = jnp.dot(pick, kept, preferred_element_type=F32).astype(BF16)


def to_slots(terms, stream, slot):
    return pl.pallas_call(
        slots_kernel,
        out_shape=(
            jax.ShapeDtypeStruct((BLK, BLK), BF16),
            jax.ShapeDtypeStruct((EXPERTS * CAP, BLK), BF16),
        ),
        in_specs=[VMEM] * 8,
        out_specs=(VMEM, VMEM),
        cost_estimate=pl.CostEstimate(
            flops=2 * 512 * BLK * BLK, bytes_accessed=2 << 20, transcendentals=0
        ),
        compiler_params=vmem(16),
        name="slots",
    )(*terms, stream, slot)


UNITS = 704
WIDE = 768
SOME = 64


def prepare(blocks, shifts, places, gain, n_s, square):
    def some_rows(i, carry):
        at = pl.ds(pl.multiple_of(i * SOME, SOME), SOME)
        total = None
        for block, shift, cols in zip(blocks, shifts, places):
            v = block[at, :].astype(F32)
            n_s[at, cols] = (v * gain[:, source_rows(*shift)]).astype(BF16)
            total = v * v if total is None else total + v * v
        square[at, :] = jnp.sum(total, axis=1, keepdims=True)
        return carry

    lax.fori_loop(0, blocks[0].shape[0] // SOME, some_rows, 0)


FIRST_OUT = FAR + ((0, 1),)
NEXT_OUT = ((0, 0), (1, 0), (3, 1), (1, 1), (3, 0))
EARLY = 3


def ready_kernel(b0, b1, b2, gain, own, far, w1, w2, n_s, square, sem):
    half = UNITS // 2
    copies = [
        pltpu.make_async_copy(
            src.at[pl.ds(i * half, half), :], dst.at[pl.ds(at + j * half, half), :], sem.at[3 * j + i]
        )
        for i, (dst, at) in enumerate([(w1, 0), (w1, WIDE), (w2, 0)])
        for j, src in enumerate((own, far))
    ]
    for copy in copies:
        copy.start()
    pad = jnp.zeros((WIDE - UNITS, 2048), BF16)
    w1[UNITS:WIDE, :] = pad
    w1[WIDE + UNITS :, :] = pad
    w2[UNITS:, :] = pad
    places = [slice(j * BLK, (j + 1) * BLK) for j in range(EARLY)]
    prepare((b0, b1, b2), NEAR[:EARLY], places, gain, n_s, square)
    for copy in copies:
        copy.wait()


def expert_ready(blocks, gain, own, far):
    rows = blocks[0].shape[0]
    return pl.pallas_call(
        ready_kernel,
        out_shape=(
            jax.ShapeDtypeStruct((2 * WIDE, 2048), BF16),
            jax.ShapeDtypeStruct((WIDE, 2048), BF16),
            jax.ShapeDtypeStruct((rows, EARLY * BLK), BF16),
            jax.ShapeDtypeStruct((rows, 1), F32),
        ),
        in_specs=[VMEM] * 4 + [HBM] * 2,
        out_specs=(VMEM,) * 4,
        scratch_shapes=[pltpu.SemaphoreType.DMA((6,))],
        cost_estimate=pl.CostEstimate(flops=1 << 20, bytes_accessed=18 << 20, transcendentals=0),
        compiler_params=vmem(16),
        name="expert_ready",
    )(*blocks, gain, own, far)


def lower(h_s, w2, outs, shifts):
    def some_rows(i, carry):
        at = pl.ds(pl.multiple_of(i * BLK, BLK), BLK)
        for out, shift in zip(outs, shifts):
            out[at, :] = jnp.dot(
                h_s[at, :], w2[:, target_cols(*shift)], preferred_element_type=F32
            ).astype(BF16)
        return carry

    lax.fori_loop(0, h_s.shape[0] // BLK, some_rows, 0)


def hidden_kernel(*refs):
    blocks = refs[:5]
    gain, w1, w2, early, square, h_s, o0, o1, o2, n_s, r_s = refs[5:]
    for j, shift in enumerate(NEAR[:EARLY]):
        n_s[:, source_rows(*shift)] = early[:, j * BLK : (j + 1) * BLK]
    shifts = NEAR[EARLY:] + FAR
    prepare(blocks, shifts, [source_rows(*shift) for shift in shifts], gain, n_s, r_s)
    factor = lax.rsqrt((square[...] + r_s[...]) * (1.0 / 2048) + NORM_EPS)

    def tile(j, carry):
        cols = pl.ds(pl.multiple_of(j * BLK, BLK), BLK)
        later = pl.ds(pl.multiple_of(WIDE + j * BLK, BLK), BLK)
        g = nt_dot(n_s[...], w1[cols, :]) * factor
        u = nt_dot(n_s[...], w1[later, :]) * factor
        h_s[:, cols] = (g / (1.0 + jnp.exp(-g)) * u).astype(BF16)
        return carry

    lax.fori_loop(0, WIDE // BLK, tile, 0)
    lower(h_s, w2, (o0, o1, o2), FIRST_OUT)


def expert_hidden(blocks, gain, w1, w2, early, square):
    rows = blocks[0].shape[0]
    piece = jax.ShapeDtypeStruct((rows, BLK), BF16)
    return pl.pallas_call(
        hidden_kernel,
        out_shape=(jax.ShapeDtypeStruct((rows, WIDE), BF16), piece, piece, piece),
        in_specs=[VMEM] * 10,
        out_specs=(VMEM,) * 4,
        scratch_shapes=[pltpu.VMEM((rows, 2048), BF16), pltpu.VMEM((rows, 1), F32)],
        cost_estimate=pl.CostEstimate(
            flops=5 * rows * 2048 * WIDE, bytes_accessed=13 << 20, transcendentals=rows * WIDE
        ),
        compiler_params=vmem(16),
        name="expert_hidden",
    )(*blocks, gain, w1, w2, early, square)


def lower_kernel(h_s, w2, *outs):
    lower(h_s, w2, outs, NEXT_OUT)


def expert_lower(h, w2):
    rows = h.shape[0]
    return pl.pallas_call(
        lower_kernel,
        out_shape=(jax.ShapeDtypeStruct((rows, BLK), BF16),) * 5,
        in_specs=[VMEM] * 2,
        out_specs=(VMEM,) * 5,
        cost_estimate=pl.CostEstimate(
            flops=2 * rows * 1536 * WIDE, bytes_accessed=6 << 20, transcendentals=0
        ),
        compiler_params=vmem(16),
        name="expert_lower",
    )(h, w2)


def finish_kernel(mixed, rows, slot, out):
    ids = lax.broadcasted_iota(jnp.int32, (EXPERTS * CAP, BLK), 0)
    pick = jnp.where(ids == slot[...], 1.0, 0.0).astype(BF16)
    out[...] = (mixed[...].astype(F32) + tn_dot(pick, rows[...])).astype(BF16)


def finish(mixed, rows, slot):
    return pl.pallas_call(
        finish_kernel,
        out_shape=jax.ShapeDtypeStruct((BLK, BLK), BF16),
        in_specs=[VMEM] * 3,
        out_specs=VMEM,
        cost_estimate=pl.CostEstimate(
            flops=2 * 512 * BLK * BLK, bytes_accessed=1 << 20, transcendentals=0
        ),
        compiler_params=vmem(8),
        name="finish",
    )(mixed, rows, slot)


def tp_shift(a, dx, dy):
    pairs = [(i * 2 + j, ((i + dx) % 4) * 2 + (j + dy) % 2) for i in range(4) for j in range(2)]
    return lax.ppermute(a, TP, pairs)


def tp_gather(a):
    near = [a] + [tp_shift(a, *s) for s in NEAR[1:]]
    return near + [tp_shift(near[1], 1, 0), tp_shift(near[2], 3, 0)]


def tp_scatter(pieces, waves):
    got = tp_shift(pieces[6], 1, 0), tp_shift(pieces[7], 3, 0)
    beside = tp_shift(pieces[3], *NEAR[3])
    if waves:
        *got, beside = lax.optimization_barrier((*got, beside))
    sums = add_pairs(pieces[1], got[0], pieces[2], got[1])
    straight = [tp_shift(p, *s) for p, s in zip(pieces[4:6], NEAR[4:6])]
    return [pieces[0], beside] + straight + [tp_shift(p, *s) for p, s in zip(sums, NEAR[1:3])]


def swap(a, dy, dc):
    pairs = [(i * 2 + j, (i ^ dy) * 2 + (j ^ dc)) for i in range(2) for j in range(2)]
    return lax.ppermute(a, ("yh", "c"), pairs)


def ring(a, step):
    return lax.ppermute(a, "z", [(i, (i + step) % 8) for i in range(8)])


def attention(blocks, wq, wk, wv, frames, weights):
    acc, rest = project_near(blocks[:6], jnp.concatenate([wk, wv, wq], axis=1))
    own, other = project_far(acc, rest, *blocks[6:], frames)
    kv, q = join(own, swap(other, 0, 1))
    f, b = ring(kv, 1), ring(kv, -1)
    theirs = swap(q, 1, 0)
    f, b, theirs = lax.optimization_barrier((f, b, theirs))
    state = None
    for k in range(1, 4):
        if k == 2:
            f, b, *held = lax.optimization_barrier((f, b, *state, *weights))
            state, weights = held[:5], held[5:]
            weights = jnp.concatenate(weights, axis=0)
        if k == 3:
            f, b, weights, *state = lax.optimization_barrier((f, b, weights, *state))
        here = f, b
        if k < 3:
            f, b = ring(f, 1), ring(b, -1)
        else:
            way = jnp.where(lax.axis_index("c") == 0, f, b)
            hops = [(i * 2 + c, (i + (-1 if c else 1)) % 8 * 2 + c) for i in range(8) for c in range(2)]
            far = lax.ppermute(way, ("z", "c"), hops)
        state = step(k, state, *here) if state else first(q, theirs, kv, *here)
    far_weights = lax.ppermute(weights, "c", [(0, 1), (1, 0)])
    mine, theirs = last(state, far)
    theirs, far_weights = lax.optimization_barrier((swap(theirs, 1, 0), far_weights))
    mine, other = merge(mine, theirs)
    return mine, swap(other, 0, 1), weights, far_weights


def shards(stream, frames, fidelity, wq, wk, wv, wo, gain, gate, up, down):
    route = fidelity[:, 0]
    spot = lax.iota(jnp.int32, BLK)
    same = (route[:, None] == route[None, :]) & (spot[None, :] < spot[:, None])
    slot = (route * CAP + jnp.sum(same.astype(jnp.int32), axis=1))[None, :]
    gain = gain[None, :]

    expert_weights = (gate[0].T, up[0].T, down[0])
    mine, other, own, far = attention(tp_gather(stream), wq, wk, wv, frames[None, :], expert_weights)
    mixed, rows = to_slots(tp_scatter(output(mine, other, wo), False), stream, slot)

    sent = lax.all_to_all(rows.reshape(EXPERTS, CAP, BLK), CHIPS, 0, 0, tiled=True)
    blocks = tp_gather(sent.reshape(EXPERTS * CAP, BLK))
    w1, w2, *early = expert_ready(blocks[:EARLY], gain, own, far)
    h, *lowered = expert_hidden(blocks[EARLY:], gain, w1, w2, *early)
    lowered = dict(zip(FIRST_OUT + NEXT_OUT, [*lowered, *expert_lower(h, w2)]))
    summed = sum_all(tp_scatter([lowered[shift] for shift in NEAR + FAR], True))
    back = lax.all_to_all(summed.reshape(EXPERTS, CAP, BLK), CHIPS, 0, 0, tiled=True)
    return finish(mixed, back.reshape(EXPERTS * CAP, BLK), slot)


def solution(mesh):
    axes = ("z", "yh", "c", "x", "yl")
    fine = Mesh(np.asarray(mesh.devices).reshape(8, 2, 2, 4, 2), axes)
    return jax.shard_map(
        shards,
        mesh=fine,
        in_specs=(
            P(SEQ, TP),
            P(SEQ),
            P(SEQ, None),
            P(None, TP),
            P(None, TP),
            P(None, TP),
            P(TP, None),
            P(),
            P(SEQ, None, TP),
            P(SEQ, None, TP),
            P(SEQ, TP, None),
        ),
        out_specs=P(SEQ, TP),
        check_vma=False,
    )
```

```python
import functools
import math

import jax
import jax.numpy as jnp
import numpy as np
from jax import lax
from jax.experimental import pallas as pl
from jax.experimental.pallas import tpu as pltpu
from jax.sharding import Mesh, PartitionSpec as P

HEAD = 128
EXPERTS = 16
CAP = 32
BLK = 256
NEG = -1e30
NORM_EPS = 1e-05
SEQ = ("z", "yh", "c")
CHIPS = ("z", "yh")
TP = ("x", "yl")
NEAR = ((0, 0), (1, 0), (3, 1), (0, 1), (3, 0), (1, 1))
FAR = ((2, 0), (2, 1))
F32 = jnp.float32
BF16 = jnp.bfloat16

VMEM = pl.BlockSpec(memory_space=pltpu.VMEM)
HBM = pl.BlockSpec(memory_space=pltpu.HBM)


def nt_dot(a, b):
    return lax.dot_general(a, b, (((1,), (1,)), ((), ())), preferred_element_type=F32)


def tn_dot(a, b):
    return lax.dot_general(a, b, (((0,), (0,)), ((), ())), preferred_element_type=F32)


def vmem(mib):
    return pltpu.CompilerParams(vmem_limit_bytes=mib << 20)


def source_rows(dx, dy):
    x, yl = lax.axis_index("x"), lax.axis_index("yl")
    source = ((x + 4 - dx) % 4) * 2 + (yl + dy) % 2
    return pl.ds(pl.multiple_of(source * BLK, BLK), BLK)


def near_kernel(*refs):
    blocks = refs[:6]
    weights, acc, rest = refs[6:]

    def some(i, carry):
        cols = pl.ds(pl.multiple_of(i * BLK, BLK), BLK)
        total = None
        for block, shift in zip(blocks, NEAR):
            term = jnp.dot(block[...], weights[source_rows(*shift), cols], preferred_element_type=F32)
            total = term if total is None else total + term
        acc[:, cols] = total
        for j, shift in enumerate(FAR):
            rest[j * BLK : (j + 1) * BLK, cols] = weights[source_rows(*shift), cols]
        return carry

    lax.fori_loop(0, 3, some, 0)


def project_near(blocks, weights):
    return pl.pallas_call(
        near_kernel,
        out_shape=(
            jax.ShapeDtypeStruct((BLK, 3 * BLK), F32),
            jax.ShapeDtypeStruct((2 * BLK, 3 * BLK), BF16),
        ),
        in_specs=[VMEM] * 7,
        out_specs=(VMEM,) * 2,
        cost_estimate=pl.CostEstimate(
            flops=2 * BLK * 1536 * 768, bytes_accessed=5 << 20, transcendentals=0
        ),
        compiler_params=vmem(20),
        name="project_near",
    )(*blocks, weights)


def far_kernel(acc, rest, b0, b1, frames, own, other):
    first = lax.axis_index("c") == 0

    def some(i, carry):
        cols = pl.ds(pl.multiple_of(i * BLK, BLK), BLK)
        total = acc[:, cols]
        for j, block in enumerate((b0, b1)):
            total = total + jnp.dot(
                block[...], rest[j * BLK : (j + 1) * BLK, cols], preferred_element_type=F32
            )
        left, right = total[:, :HEAD], total[:, HEAD:]
        cols = pl.ds(pl.multiple_of(i * HEAD, HEAD), HEAD)
        own[:BLK, cols] = jnp.where(first, left, right).astype(BF16)
        other[:BLK, cols] = jnp.where(first, right, left).astype(BF16)
        return carry

    lax.fori_loop(0, 3, some, 0)
    tail = jnp.broadcast_to(frames[...], (16, BLK)).astype(BF16)
    for out in (own, other):
        out[BLK:, : 2 * HEAD] = tail
        out[BLK:, 2 * HEAD :] = tail[:, :HEAD]


def project_far(acc, rest, b0, b1, frames):
    packet = jax.ShapeDtypeStruct((BLK + 16, 3 * HEAD), BF16)
    return pl.pallas_call(
        far_kernel,
        out_shape=(packet, packet),
        in_specs=[VMEM] * 5,
        out_specs=(VMEM,) * 2,
        cost_estimate=pl.CostEstimate(
            flops=2 * BLK * 512 * 768, bytes_accessed=2 << 20, transcendentals=0
        ),
        compiler_params=vmem(16),
        name="project_far",
    )(acc, rest, b0, b1, frames)


def join_kernel(own, got, kv, q):
    row = lax.broadcasted_iota(jnp.int32, (16, BLK), 0)
    both = [ref[BLK:, : 2 * HEAD].astype(F32) for ref in (own, got)]
    tail = jnp.where(row == 0, both[0], both[1])
    for i, ref in enumerate((own, got)):
        rows = slice(i * BLK, (i + 1) * BLK)
        kv[rows, :] = ref[:BLK, : 2 * HEAD]
        q[rows, :] = ref[:BLK, 2 * HEAD :]
    kv[2 * BLK :, :] = tail.astype(BF16)
    row = lax.broadcasted_iota(jnp.int32, (16, HEAD), 0)
    parts = [b[:, h * HEAD : (h + 1) * HEAD] for b in both for h in range(2)]
    lines = jnp.where(row == 0, parts[0], jnp.where(row == 1, parts[1], jnp.where(row == 2, parts[2], parts[3])))
    q[2 * BLK :, :] = lines.astype(BF16)


def join(own, got):
    return pl.pallas_call(
        join_kernel,
        out_shape=(
            jax.ShapeDtypeStruct((2 * BLK + 16, 2 * HEAD), BF16),
            jax.ShapeDtypeStruct((2 * BLK + 16, HEAD), BF16),
        ),
        in_specs=[VMEM] * 2,
        out_specs=(VMEM,) * 2,
        cost_estimate=pl.CostEstimate(flops=BLK * BLK, bytes_accessed=1 << 19, transcendentals=0),
        compiler_params=vmem(8),
        name="join",
    )(own, got)


def visit(q_s, f_s, m_s, l_s, acc_s, kv, masked, wide):
    scale = 1.0 / math.sqrt(HEAD)
    if masked:
        lines = [jnp.broadcast_to(kv[r : r + 1, :].astype(F32), (HEAD, BLK)) for r in (2 * BLK, 2 * BLK + 1)]
        frames = jnp.concatenate([jnp.transpose(line)[:, :1] for line in lines], axis=0)

    def part(i, carry):
        lanes = pl.ds(pl.multiple_of(i * wide, wide), wide)
        s = nt_dot(kv[: 2 * BLK, :HEAD], q_s[lanes, :]) * scale
        if masked:
            allowed = frames <= f_s[:, lanes]
            s = jnp.where(allowed, s, NEG)
        old = m_s[:, lanes]
        top = jnp.maximum(old, jnp.max(s, axis=0, keepdims=True))
        decay = jnp.exp(old - top)
        p = jnp.exp(s - top)
        if masked:
            p = jnp.where(allowed, p, 0.0)
        m_s[:, lanes] = top
        l_s[:, lanes] = l_s[:, lanes] * decay + jnp.sum(p, axis=0, keepdims=True)
        acc_s[:, lanes] = acc_s[:, lanes] * decay + tn_dot(kv[: 2 * BLK, HEAD:], p.astype(BF16))
        return carry

    lax.fori_loop(0, 4 * BLK // wide, part, 0)


def first_kernel(mine, theirs, own, f, b, q_s, f_s, m_s, l_s, acc_s, kv):
    for g, q in enumerate((mine, theirs)):
        q_s[g * 2 * BLK : (g + 1) * 2 * BLK, :] = q[: 2 * BLK, :]
        for i in range(4):
            lanes = slice((g * 4 + i) * HEAD, (g * 4 + i + 1) * HEAD)
            f_s[:, lanes] = q[2 * BLK + i : 2 * BLK + i + 1, :].astype(F32)
    m_s[...] = jnp.full_like(m_s, NEG)
    l_s[...] = jnp.zeros_like(l_s)
    acc_s[...] = jnp.zeros_like(acc_s)
    z = lax.axis_index("z")
    wanted = (z >= 0, z >= 1, (z == 7) | (lax.axis_index("yh") == 0))

    def side(j, carry):
        need = z < 0
        for i, (block, want) in enumerate(zip((own, f, b), wanted)):

            @pl.when((j == i) & want)
            def _():
                kv[...] = block[...]

            need = need | ((j == i) & want)

        @pl.when(need)
        def _():
            visit(q_s, f_s, m_s, l_s, acc_s, kv, True, 2 * BLK)

        return carry

    lax.fori_loop(0, 3, side, 0)


STATE = (
    jax.ShapeDtypeStruct((4 * BLK, HEAD), BF16),
    jax.ShapeDtypeStruct((1, 4 * BLK), F32),
    jax.ShapeDtypeStruct((1, 4 * BLK), F32),
    jax.ShapeDtypeStruct((1, 4 * BLK), F32),
    jax.ShapeDtypeStruct((HEAD, 4 * BLK), F32),
)


def visit_cost(blocks):
    work = 1024 * BLK * blocks
    return pl.CostEstimate(flops=4 * work * HEAD, bytes_accessed=2 << 20, transcendentals=work)


def first(mine, theirs, own, f, b):
    return pl.pallas_call(
        first_kernel,
        out_shape=STATE,
        in_specs=[VMEM] * 5,
        out_specs=(VMEM,) * 5,
        scratch_shapes=[pltpu.VMEM(f.shape, BF16)],
        cost_estimate=visit_cost(6),
        compiler_params=vmem(24),
        name="first",
    )(mine, theirs, own, f, b)


def step_kernel(k, q_s, f_s, m_i, l_i, acc_i, f, b, m_s, l_s, acc_s, kv):
    z = lax.axis_index("z")
    m_s[...] = m_i[...]
    l_s[...] = l_i[...]
    acc_s[...] = acc_i[...]

    def side(j, carry):
        @pl.when((j == 0) & (z >= k))
        def _():
            kv[...] = f[...]

        @pl.when((j == 1) & (z + k >= 8))
        def _():
            kv[...] = b[...]

        @pl.when(((j == 0) & (z >= k)) | ((j == 1) & (z + k >= 8)))
        def _():
            visit(q_s, f_s, m_s, l_s, acc_s, kv, False, BLK)

        return carry

    lax.fori_loop(0, 2, side, 0)


def step(k, state, f, b):
    m, l, acc = pl.pallas_call(
        functools.partial(step_kernel, k),
        out_shape=STATE[2:],
        in_specs=[VMEM] * 7,
        out_specs=(VMEM,) * 3,
        scratch_shapes=[pltpu.VMEM(f.shape, BF16)],
        cost_estimate=visit_cost(4),
        compiler_params=vmem(24),
        name="step",
    )(*state, f, b)
    return state[0], state[1], m, l, acc


def last_kernel(q_s, f_s, m_i, l_i, acc_i, kv, mine, theirs, m_s, l_s, acc_s):
    m_s[...] = m_i[...]
    l_s[...] = l_i[...]
    acc_s[...] = acc_i[...]

    @pl.when(lax.axis_index("z") >= 4)
    def _():
        visit(q_s, f_s, m_s, l_s, acc_s, kv, False, 2 * BLK)

    for g, out in enumerate((mine, theirs)):
        lanes = slice(g * 2 * BLK, (g + 1) * 2 * BLK)
        total = l_s[:, lanes]
        some = total > 0.0
        safe = jnp.where(some, total, 1.0)
        out[:HEAD, :] = (acc_s[:, lanes] * (1.0 / safe)).astype(BF16)
        log = jnp.where(some, m_s[:, lanes] + jnp.log(safe), NEG)
        row = lax.broadcasted_iota(jnp.int32, (16, 2 * BLK), 0)
        high = log.astype(BF16).astype(F32)
        middle = (log - high).astype(BF16).astype(F32)
        low = log - high - middle
        terms = jnp.where(row == 0, high, jnp.where(row == 1, middle, jnp.where(row == 2, low, 0.0)))
        out[HEAD:, :] = terms.astype(BF16)


def last(state, kv):
    return pl.pallas_call(
        last_kernel,
        out_shape=(jax.ShapeDtypeStruct((HEAD + 16, 2 * BLK), BF16),) * 2,
        in_specs=[VMEM] * 6,
        out_specs=(VMEM,) * 2,
        scratch_shapes=[pltpu.VMEM(s.shape, s.dtype) for s in STATE[2:]],
        cost_estimate=visit_cost(2),
        compiler_params=vmem(24),
        name="last",
    )(*state, kv)


def merge_kernel(a, b, mine, other):
    la = jnp.sum(a[HEAD:, :].astype(F32), axis=0, keepdims=True)
    lb = jnp.sum(b[HEAD:, :].astype(F32), axis=0, keepdims=True)
    top = jnp.maximum(la, lb)
    wa, wb = jnp.exp(la - top), jnp.exp(lb - top)
    inv = 1.0 / (wa + wb)
    total = (a[:HEAD, :].astype(F32) * (wa * inv) + b[:HEAD, :].astype(F32) * (wb * inv)).astype(BF16)
    mine[...] = total[:, :BLK]
    other[...] = total[:, BLK:]


def merge(a, b):
    half = jax.ShapeDtypeStruct((HEAD, BLK), BF16)
    return pl.pallas_call(
        merge_kernel,
        out_shape=(half, half),
        in_specs=[VMEM] * 2,
        out_specs=(VMEM,) * 2,
        cost_estimate=pl.CostEstimate(flops=1 << 18, bytes_accessed=1 << 19, transcendentals=1024),
        compiler_params=vmem(8),
        name="merge",
    )(a, b)


def output_kernel(mine, other, w, *outs):
    first = lax.axis_index("c") == 0
    a, b = (jnp.transpose(ref[...].astype(F32)) for ref in (mine, other))
    rows = jnp.concatenate([jnp.where(first, a, b), jnp.where(first, b, a)], axis=1).astype(BF16)
    for out, shift in zip(outs, NEAR + FAR):
        out[...] = jnp.dot(rows, w[:, target_cols(*shift)], preferred_element_type=F32).astype(BF16)


def target_cols(dx, dy):
    x, yl = lax.axis_index("x"), lax.axis_index("yl")
    target = ((x + dx) % 4) * 2 + (yl + dy) % 2
    return pl.ds(pl.multiple_of(target * BLK, BLK), BLK)


def output(mine, other, w):
    return pl.pallas_call(
        output_kernel,
        out_shape=(jax.ShapeDtypeStruct((BLK, BLK), BF16),) * 8,
        in_specs=[VMEM] * 3,
        out_specs=(VMEM,) * 8,
        cost_estimate=pl.CostEstimate(
            flops=2 * BLK * BLK * 2048, bytes_accessed=3 << 20, transcendentals=0
        ),
        compiler_params=vmem(16),
        name="output",
    )(mine, other, w)


def add_kernel(a0, b0, a1, b1, out0, out1):
    out0[...] = (a0[...].astype(F32) + b0[...].astype(F32)).astype(BF16)
    out1[...] = (a1[...].astype(F32) + b1[...].astype(F32)).astype(BF16)


def add_pairs(a0, b0, a1, b1):
    return pl.pallas_call(
        add_kernel,
        out_shape=(jax.ShapeDtypeStruct(a0.shape, BF16),) * 2,
        in_specs=[VMEM] * 4,
        out_specs=(VMEM,) * 2,
        cost_estimate=pl.CostEstimate(flops=a0.size, bytes_accessed=12 * a0.size, transcendentals=0),
        compiler_params=vmem(8),
        name="add_pairs",
    )(a0, b0, a1, b1)


def sum_kernel(*refs):
    total = refs[0][...].astype(F32)
    for ref in refs[1:-1]:
        total = total + ref[...].astype(F32)
    refs[-1][...] = total.astype(BF16)


def sum_all(terms):
    return pl.pallas_call(
        sum_kernel,
        out_shape=jax.ShapeDtypeStruct(terms[0].shape, BF16),
        in_specs=[VMEM] * len(terms),
        out_specs=VMEM,
        cost_estimate=pl.CostEstimate(
            flops=6 * terms[0].size, bytes_accessed=14 * terms[0].size, transcendentals=0
        ),
        compiler_params=vmem(8),
        name="sum_all",
    )(*terms)


def slots_kernel(*refs):
    terms = refs[:6]
    stream, slot, mixed, rows = refs[6:]
    total = stream[...].astype(F32)
    for term in terms:
        total = total + term[...].astype(F32)
    kept = total.astype(BF16)
    mixed[...] = kept
    ids = lax.broadcasted_iota(jnp.int32, (EXPERTS * CAP, BLK), 0)
    pick = jnp.where(ids == slot[...], 1.0, 0.0).astype(BF16)
    rows[...] = jnp.dot(pick, kept, preferred_element_type=F32).astype(BF16)


def to_slots(terms, stream, slot):
    return pl.pallas_call(
        slots_kernel,
        out_shape=(
            jax.ShapeDtypeStruct((BLK, BLK), BF16),
            jax.ShapeDtypeStruct((EXPERTS * CAP, BLK), BF16),
        ),
        in_specs=[VMEM] * 8,
        out_specs=(VMEM, VMEM),
        cost_estimate=pl.CostEstimate(
            flops=2 * 512 * BLK * BLK, bytes_accessed=2 << 20, transcendentals=0
        ),
        compiler_params=vmem(16),
        name="slots",
    )(*terms, stream, slot)


UNITS = 704
WIDE = 768
SOME = 64


def prepare(blocks, shifts, places, gain, n_s, square):
    def some_rows(i, carry):
        at = pl.ds(pl.multiple_of(i * SOME, SOME), SOME)
        total = None
        for block, shift, cols in zip(blocks, shifts, places):
            v = block[at, :].astype(F32)
            n_s[at, cols] = (v * gain[:, source_rows(*shift)]).astype(BF16)
            total = v * v if total is None else total + v * v
        square[at, :] = jnp.sum(total, axis=1, keepdims=True)
        return carry

    lax.fori_loop(0, blocks[0].shape[0] // SOME, some_rows, 0)


FIRST_OUT = FAR + ((0, 1),)
NEXT_OUT = ((0, 0), (1, 0), (3, 1), (1, 1), (3, 0))
EARLY = 3


def ready_kernel(b0, b1, b2, gain, own, far, w1, w2, n_s, square, sem):
    half = UNITS // 2
    copies = [
        pltpu.make_async_copy(
            src.at[pl.ds(i * half, half), :], dst.at[pl.ds(at + j * half, half), :], sem.at[3 * j + i]
        )
        for i, (dst, at) in enumerate([(w1, 0), (w1, WIDE), (w2, 0)])
        for j, src in enumerate((own, far))
    ]
    for copy in copies:
        copy.start()
    pad = jnp.zeros((WIDE - UNITS, 2048), BF16)
    w1[UNITS:WIDE, :] = pad
    w1[WIDE + UNITS :, :] = pad
    w2[UNITS:, :] = pad
    places = [slice(j * BLK, (j + 1) * BLK) for j in range(EARLY)]
    prepare((b0, b1, b2), NEAR[:EARLY], places, gain, n_s, square)
    for copy in copies:
        copy.wait()


def expert_ready(blocks, gain, own, far):
    rows = blocks[0].shape[0]
    return pl.pallas_call(
        ready_kernel,
        out_shape=(
            jax.ShapeDtypeStruct((2 * WIDE, 2048), BF16),
            jax.ShapeDtypeStruct((WIDE, 2048), BF16),
            jax.ShapeDtypeStruct((rows, EARLY * BLK), BF16),
            jax.ShapeDtypeStruct((rows, 1), F32),
        ),
        in_specs=[VMEM] * 4 + [HBM] * 2,
        out_specs=(VMEM,) * 4,
        scratch_shapes=[pltpu.SemaphoreType.DMA((6,))],
        cost_estimate=pl.CostEstimate(flops=1 << 20, bytes_accessed=18 << 20, transcendentals=0),
        compiler_params=vmem(16),
        name="expert_ready",
    )(*blocks, gain, own, far)


def lower(h_s, w2, outs, shifts):
    def some_rows(i, carry):
        at = pl.ds(pl.multiple_of(i * BLK, BLK), BLK)
        for out, shift in zip(outs, shifts):
            out[at, :] = jnp.dot(
                h_s[at, :], w2[:, target_cols(*shift)], preferred_element_type=F32
            ).astype(BF16)
        return carry

    lax.fori_loop(0, h_s.shape[0] // BLK, some_rows, 0)


def hidden_kernel(*refs):
    blocks = refs[:5]
    gain, w1, w2, early, square, h_s, o0, o1, o2, n_s, r_s = refs[5:]
    for j, shift in enumerate(NEAR[:EARLY]):
        n_s[:, source_rows(*shift)] = early[:, j * BLK : (j + 1) * BLK]
    shifts = NEAR[EARLY:] + FAR
    prepare(blocks, shifts, [source_rows(*shift) for shift in shifts], gain, n_s, r_s)
    factor = lax.rsqrt((square[...] + r_s[...]) * (1.0 / 2048) + NORM_EPS)

    def tile(j, carry):
        cols = pl.ds(pl.multiple_of(j * BLK, BLK), BLK)
        later = pl.ds(pl.multiple_of(WIDE + j * BLK, BLK), BLK)
        g = nt_dot(n_s[...], w1[cols, :]) * factor
        u = nt_dot(n_s[...], w1[later, :]) * factor
        h_s[:, cols] = (g / (1.0 + jnp.exp(-g)) * u).astype(BF16)
        return carry

    lax.fori_loop(0, WIDE // BLK, tile, 0)
    lower(h_s, w2, (o0, o1, o2), FIRST_OUT)


def expert_hidden(blocks, gain, w1, w2, early, square):
    rows = blocks[0].shape[0]
    piece = jax.ShapeDtypeStruct((rows, BLK), BF16)
    return pl.pallas_call(
        hidden_kernel,
        out_shape=(jax.ShapeDtypeStruct((rows, WIDE), BF16), piece, piece, piece),
        in_specs=[VMEM] * 10,
        out_specs=(VMEM,) * 4,
        scratch_shapes=[pltpu.VMEM((rows, 2048), BF16), pltpu.VMEM((rows, 1), F32)],
        cost_estimate=pl.CostEstimate(
            flops=5 * rows * 2048 * WIDE, bytes_accessed=13 << 20, transcendentals=rows * WIDE
        ),
        compiler_params=vmem(16),
        name="expert_hidden",
    )(*blocks, gain, w1, w2, early, square)


def lower_kernel(h_s, w2, *outs):
    lower(h_s, w2, outs, NEXT_OUT)


def expert_lower(h, w2):
    rows = h.shape[0]
    return pl.pallas_call(
        lower_kernel,
        out_shape=(jax.ShapeDtypeStruct((rows, BLK), BF16),) * 5,
        in_specs=[VMEM] * 2,
        out_specs=(VMEM,) * 5,
        cost_estimate=pl.CostEstimate(
            flops=2 * rows * 1536 * WIDE, bytes_accessed=6 << 20, transcendentals=0
        ),
        compiler_params=vmem(16),
        name="expert_lower",
    )(h, w2)


def finish_kernel(mixed, rows, slot, out):
    ids = lax.broadcasted_iota(jnp.int32, (EXPERTS * CAP, BLK), 0)
    pick = jnp.where(ids == slot[...], 1.0, 0.0).astype(BF16)
    out[...] = (mixed[...].astype(F32) + tn_dot(pick, rows[...])).astype(BF16)


def finish(mixed, rows, slot):
    return pl.pallas_call(
        finish_kernel,
        out_shape=jax.ShapeDtypeStruct((BLK, BLK), BF16),
        in_specs=[VMEM] * 3,
        out_specs=VMEM,
        cost_estimate=pl.CostEstimate(
            flops=2 * 512 * BLK * BLK, bytes_accessed=1 << 20, transcendentals=0
        ),
        compiler_params=vmem(8),
        name="finish",
    )(mixed, rows, slot)


def tp_shift(a, dx, dy):
    pairs = [(i * 2 + j, ((i + dx) % 4) * 2 + (j + dy) % 2) for i in range(4) for j in range(2)]
    return lax.ppermute(a, TP, pairs)


def tp_gather(a):
    near = [a] + [tp_shift(a, *s) for s in NEAR[1:]]
    return near + [tp_shift(near[1], 1, 0), tp_shift(near[2], 3, 0)]


def tp_scatter(pieces, waves):
    got = tp_shift(pieces[6], 1, 0), tp_shift(pieces[7], 3, 0)
    beside = tp_shift(pieces[3], *NEAR[3])
    if waves:
        *got, beside = lax.optimization_barrier((*got, beside))
    sums = add_pairs(pieces[1], got[0], pieces[2], got[1])
    straight = [tp_shift(p, *s) for p, s in zip(pieces[4:6], NEAR[4:6])]
    return [pieces[0], beside] + straight + [tp_shift(p, *s) for p, s in zip(sums, NEAR[1:3])]


def swap(a, dy, dc):
    pairs = [(i * 2 + j, (i ^ dy) * 2 + (j ^ dc)) for i in range(2) for j in range(2)]
    return lax.ppermute(a, ("yh", "c"), pairs)


def ring(a, step):
    return lax.ppermute(a, "z", [(i, (i + step) % 8) for i in range(8)])


def attention(blocks, wq, wk, wv, frames, weights):
    acc, rest = project_near(blocks[:6], jnp.concatenate([wk, wv, wq], axis=1))
    own, other = project_far(acc, rest, *blocks[6:], frames)
    kv, q = join(own, swap(other, 0, 1))
    f, b = ring(kv, 1), ring(kv, -1)
    theirs = swap(q, 1, 0)
    weights, kv = lax.optimization_barrier((weights, kv))
    weights = jnp.concatenate(weights, axis=0)
    f, b, theirs, weights = lax.optimization_barrier((f, b, theirs, weights))
    state = None
    for k in range(1, 4):
        if k > 1:
            f, b, weights, *state = lax.optimization_barrier((f, b, weights, *state))
        here = f, b
        if k < 3:
            f, b = ring(f, 1), ring(b, -1)
        else:
            way = jnp.where(lax.axis_index("c") == 0, f, b)
            hops = [(i * 2 + c, (i + (-1 if c else 1)) % 8 * 2 + c) for i in range(8) for c in range(2)]
            far = lax.ppermute(way, ("z", "c"), hops)
        state = step(k, state, *here) if state else first(q, theirs, kv, *here)
    far_weights = lax.ppermute(weights, "c", [(0, 1), (1, 0)])
    mine, theirs = last(state, far)
    theirs, far_weights = lax.optimization_barrier((swap(theirs, 1, 0), far_weights))
    mine, other = merge(mine, theirs)
    return mine, swap(other, 0, 1), weights, far_weights


def shards(stream, frames, fidelity, wq, wk, wv, wo, gain, gate, up, down):
    route = fidelity[:, 0]
    spot = lax.iota(jnp.int32, BLK)
    same = (route[:, None] == route[None, :]) & (spot[None, :] < spot[:, None])
    slot = (route * CAP + jnp.sum(same.astype(jnp.int32), axis=1))[None, :]
    gain = gain[None, :]

    expert_weights = (gate[0].T, up[0].T, down[0])
    mine, other, own, far = attention(tp_gather(stream), wq, wk, wv, frames[None, :], expert_weights)
    mixed, rows = to_slots(tp_scatter(output(mine, other, wo), False), stream, slot)

    sent = lax.all_to_all(rows.reshape(EXPERTS, CAP, BLK), CHIPS, 0, 0, tiled=True)
    blocks = tp_gather(sent.reshape(EXPERTS * CAP, BLK))
    w1, w2, *early = expert_ready(blocks[:EARLY], gain, own, far)
    h, *lowered = expert_hidden(blocks[EARLY:], gain, w1, w2, *early)
    lowered = dict(zip(FIRST_OUT + NEXT_OUT, [*lowered, *expert_lower(h, w2)]))
    summed = sum_all(tp_scatter([lowered[shift] for shift in NEAR + FAR], True))
    back = lax.all_to_all(summed.reshape(EXPERTS, CAP, BLK), CHIPS, 0, 0, tiled=True)
    return finish(mixed, back.reshape(EXPERTS * CAP, BLK), slot)


def solution(mesh):
    axes = ("z", "yh", "c", "x", "yl")
    fine = Mesh(np.asarray(mesh.devices).reshape(8, 2, 2, 4, 2), axes)
    return jax.shard_map(
        shards,
        mesh=fine,
        in_specs=(
            P(SEQ, TP),
            P(SEQ),
            P(SEQ, None),
            P(None, TP),
            P(None, TP),
            P(None, TP),
            P(TP, None),
            P(),
            P(SEQ, None, TP),
            P(SEQ, None, TP),
            P(SEQ, TP, None),
        ),
        out_specs=P(SEQ, TP),
        check_vma=False,
    )
```

```python
import functools
import math

import jax
import jax.numpy as jnp
import numpy as np
from jax import lax
from jax.experimental import pallas as pl
from jax.experimental.pallas import tpu as pltpu
from jax.sharding import Mesh, PartitionSpec as P

HEAD = 128
EXPERTS = 16
CAP = 32
BLK = 256
NEG = -1e30
NORM_EPS = 1e-05
SEQ = ("z", "yh", "c")
CHIPS = ("z", "yh")
TP = ("x", "yl")
NEAR = ((0, 0), (1, 0), (3, 1), (0, 1), (3, 0), (1, 1))
FAR = ((2, 0), (2, 1))
F32 = jnp.float32
BF16 = jnp.bfloat16

VMEM = pl.BlockSpec(memory_space=pltpu.VMEM)
HBM = pl.BlockSpec(memory_space=pltpu.HBM)


def nt_dot(a, b):
    return lax.dot_general(a, b, (((1,), (1,)), ((), ())), preferred_element_type=F32)


def tn_dot(a, b):
    return lax.dot_general(a, b, (((0,), (0,)), ((), ())), preferred_element_type=F32)


def vmem(mib):
    return pltpu.CompilerParams(vmem_limit_bytes=mib << 20)


def source_rows(dx, dy):
    x, yl = lax.axis_index("x"), lax.axis_index("yl")
    source = ((x + 4 - dx) % 4) * 2 + (yl + dy) % 2
    return pl.ds(pl.multiple_of(source * BLK, BLK), BLK)


def near_kernel(*refs):
    blocks = refs[:6]
    weights, acc, rest = refs[6:]

    def some(i, carry):
        cols = pl.ds(pl.multiple_of(i * BLK, BLK), BLK)
        total = None
        for block, shift in zip(blocks, NEAR):
            term = jnp.dot(block[...], weights[source_rows(*shift), cols], preferred_element_type=F32)
            total = term if total is None else total + term
        acc[:, cols] = total
        for j, shift in enumerate(FAR):
            rest[j * BLK : (j + 1) * BLK, cols] = weights[source_rows(*shift), cols]
        return carry

    lax.fori_loop(0, 3, some, 0)


def project_near(blocks, weights):
    return pl.pallas_call(
        near_kernel,
        out_shape=(
            jax.ShapeDtypeStruct((BLK, 3 * BLK), F32),
            jax.ShapeDtypeStruct((2 * BLK, 3 * BLK), BF16),
        ),
        in_specs=[VMEM] * 7,
        out_specs=(VMEM,) * 2,
        cost_estimate=pl.CostEstimate(
            flops=2 * BLK * 1536 * 768, bytes_accessed=5 << 20, transcendentals=0
        ),
        compiler_params=vmem(20),
        name="project_near",
    )(*blocks, weights)


def far_kernel(acc, rest, b0, b1, frames, own, other):
    first = lax.axis_index("c") == 0

    def some(i, carry):
        cols = pl.ds(pl.multiple_of(i * BLK, BLK), BLK)
        total = acc[:, cols]
        for j, block in enumerate((b0, b1)):
            total = total + jnp.dot(
                block[...], rest[j * BLK : (j + 1) * BLK, cols], preferred_element_type=F32
            )
        left, right = total[:, :HEAD], total[:, HEAD:]
        cols = pl.ds(pl.multiple_of(i * HEAD, HEAD), HEAD)
        own[:BLK, cols] = jnp.where(first, left, right).astype(BF16)
        other[:BLK, cols] = jnp.where(first, right, left).astype(BF16)
        return carry

    lax.fori_loop(0, 3, some, 0)
    tail = jnp.broadcast_to(frames[...], (16, BLK)).astype(BF16)
    for out in (own, other):
        out[BLK:, : 2 * HEAD] = tail
        out[BLK:, 2 * HEAD :] = tail[:, :HEAD]


def project_far(acc, rest, b0, b1, frames):
    packet = jax.ShapeDtypeStruct((BLK + 16, 3 * HEAD), BF16)
    return pl.pallas_call(
        far_kernel,
        out_shape=(packet, packet),
        in_specs=[VMEM] * 5,
        out_specs=(VMEM,) * 2,
        cost_estimate=pl.CostEstimate(
            flops=2 * BLK * 512 * 768, bytes_accessed=2 << 20, transcendentals=0
        ),
        compiler_params=vmem(16),
        name="project_far",
    )(acc, rest, b0, b1, frames)


def join_kernel(own, got, kv, q):
    row = lax.broadcasted_iota(jnp.int32, (16, BLK), 0)
    both = [ref[BLK:, : 2 * HEAD].astype(F32) for ref in (own, got)]
    tail = jnp.where(row == 0, both[0], both[1])
    for i, ref in enumerate((own, got)):
        rows = slice(i * BLK, (i + 1) * BLK)
        kv[rows, :] = ref[:BLK, : 2 * HEAD]
        q[rows, :] = ref[:BLK, 2 * HEAD :]
    kv[2 * BLK :, :] = tail.astype(BF16)
    row = lax.broadcasted_iota(jnp.int32, (16, HEAD), 0)
    parts = [b[:, h * HEAD : (h + 1) * HEAD] for b in both for h in range(2)]
    lines = jnp.where(row == 0, parts[0], jnp.where(row == 1, parts[1], jnp.where(row == 2, parts[2], parts[3])))
    q[2 * BLK :, :] = lines.astype(BF16)


def join(own, got):
    return pl.pallas_call(
        join_kernel,
        out_shape=(
            jax.ShapeDtypeStruct((2 * BLK + 16, 2 * HEAD), BF16),
            jax.ShapeDtypeStruct((2 * BLK + 16, HEAD), BF16),
        ),
        in_specs=[VMEM] * 2,
        out_specs=(VMEM,) * 2,
        cost_estimate=pl.CostEstimate(flops=BLK * BLK, bytes_accessed=1 << 19, transcendentals=0),
        compiler_params=vmem(8),
        name="join",
    )(own, got)


def visit(q_s, f_s, m_s, l_s, acc_s, kv, masked, wide):
    scale = 1.0 / math.sqrt(HEAD)
    if masked:
        lines = [jnp.broadcast_to(kv[r : r + 1, :].astype(F32), (HEAD, BLK)) for r in (2 * BLK, 2 * BLK + 1)]
        frames = jnp.concatenate([jnp.transpose(line)[:, :1] for line in lines], axis=0)

    def part(i, carry):
        lanes = pl.ds(pl.multiple_of(i * wide, wide), wide)
        s = nt_dot(kv[: 2 * BLK, :HEAD], q_s[lanes, :]) * scale
        if masked:
            allowed = frames <= f_s[:, lanes]
            s = jnp.where(allowed, s, NEG)
        old = m_s[:, lanes]
        top = jnp.maximum(old, jnp.max(s, axis=0, keepdims=True))
        decay = jnp.exp(old - top)
        p = jnp.exp(s - top)
        if masked:
            p = jnp.where(allowed, p, 0.0)
        m_s[:, lanes] = top
        l_s[:, lanes] = l_s[:, lanes] * decay + jnp.sum(p, axis=0, keepdims=True)
        acc_s[:, lanes] = acc_s[:, lanes] * decay + tn_dot(kv[: 2 * BLK, HEAD:], p.astype(BF16))
        return carry

    lax.fori_loop(0, 4 * BLK // wide, part, 0)


def first_kernel(mine, theirs, own, f, b, q_s, f_s, m_s, l_s, acc_s, kv):
    for g, q in enumerate((mine, theirs)):
        q_s[g * 2 * BLK : (g + 1) * 2 * BLK, :] = q[: 2 * BLK, :]
        for i in range(4):
            lanes = slice((g * 4 + i) * HEAD, (g * 4 + i + 1) * HEAD)
            f_s[:, lanes] = q[2 * BLK + i : 2 * BLK + i + 1, :].astype(F32)
    m_s[...] = jnp.full_like(m_s, NEG)
    l_s[...] = jnp.zeros_like(l_s)
    acc_s[...] = jnp.zeros_like(acc_s)
    z = lax.axis_index("z")
    wanted = (z >= 0, z >= 1, (z == 7) | (lax.axis_index("yh") == 0))

    def side(j, carry):
        need = z < 0
        for i, (block, want) in enumerate(zip((own, f, b), wanted)):

            @pl.when((j == i) & want)
            def _():
                kv[...] = block[...]

            need = need | ((j == i) & want)

        @pl.when(need)
        def _():
            visit(q_s, f_s, m_s, l_s, acc_s, kv, True, 2 * BLK)

        return carry

    lax.fori_loop(0, 3, side, 0)


STATE = (
    jax.ShapeDtypeStruct((4 * BLK, HEAD), BF16),
    jax.ShapeDtypeStruct((1, 4 * BLK), F32),
    jax.ShapeDtypeStruct((1, 4 * BLK), F32),
    jax.ShapeDtypeStruct((1, 4 * BLK), F32),
    jax.ShapeDtypeStruct((HEAD, 4 * BLK), F32),
)


def visit_cost(blocks):
    work = 1024 * BLK * blocks
    return pl.CostEstimate(flops=4 * work * HEAD, bytes_accessed=2 << 20, transcendentals=work)


def first(mine, theirs, own, f, b):
    return pl.pallas_call(
        first_kernel,
        out_shape=STATE,
        in_specs=[VMEM] * 5,
        out_specs=(VMEM,) * 5,
        scratch_shapes=[pltpu.VMEM(f.shape, BF16)],
        cost_estimate=visit_cost(6),
        compiler_params=vmem(24),
        name="first",
    )(mine, theirs, own, f, b)


def step_kernel(k, q_s, f_s, m_i, l_i, acc_i, f, b, m_s, l_s, acc_s, kv):
    z = lax.axis_index("z")
    m_s[...] = m_i[...]
    l_s[...] = l_i[...]
    acc_s[...] = acc_i[...]

    def side(j, carry):
        @pl.when((j == 0) & (z >= k))
        def _():
            kv[...] = f[...]

        @pl.when((j == 1) & (z + k >= 8))
        def _():
            kv[...] = b[...]

        @pl.when(((j == 0) & (z >= k)) | ((j == 1) & (z + k >= 8)))
        def _():
            visit(q_s, f_s, m_s, l_s, acc_s, kv, False, BLK)

        return carry

    lax.fori_loop(0, 2, side, 0)


def step(k, state, f, b):
    m, l, acc = pl.pallas_call(
        functools.partial(step_kernel, k),
        out_shape=STATE[2:],
        in_specs=[VMEM] * 7,
        out_specs=(VMEM,) * 3,
        scratch_shapes=[pltpu.VMEM(f.shape, BF16)],
        cost_estimate=visit_cost(4),
        compiler_params=vmem(24),
        name="step",
    )(*state, f, b)
    return state[0], state[1], m, l, acc


def last_kernel(q_s, f_s, m_i, l_i, acc_i, kv, mine, theirs, m_s, l_s, acc_s):
    m_s[...] = m_i[...]
    l_s[...] = l_i[...]
    acc_s[...] = acc_i[...]

    @pl.when(lax.axis_index("z") >= 4)
    def _():
        visit(q_s, f_s, m_s, l_s, acc_s, kv, False, 2 * BLK)

    for g, out in enumerate((mine, theirs)):
        lanes = slice(g * 2 * BLK, (g + 1) * 2 * BLK)
        total = l_s[:, lanes]
        some = total > 0.0
        safe = jnp.where(some, total, 1.0)
        out[:HEAD, :] = (acc_s[:, lanes] * (1.0 / safe)).astype(BF16)
        log = jnp.where(some, m_s[:, lanes] + jnp.log(safe), NEG)
        row = lax.broadcasted_iota(jnp.int32, (16, 2 * BLK), 0)
        high = log.astype(BF16).astype(F32)
        middle = (log - high).astype(BF16).astype(F32)
        low = log - high - middle
        terms = jnp.where(row == 0, high, jnp.where(row == 1, middle, jnp.where(row == 2, low, 0.0)))
        out[HEAD:, :] = terms.astype(BF16)


def last(state, kv):
    return pl.pallas_call(
        last_kernel,
        out_shape=(jax.ShapeDtypeStruct((HEAD + 16, 2 * BLK), BF16),) * 2,
        in_specs=[VMEM] * 6,
        out_specs=(VMEM,) * 2,
        scratch_shapes=[pltpu.VMEM(s.shape, s.dtype) for s in STATE[2:]],
        cost_estimate=visit_cost(2),
        compiler_params=vmem(24),
        name="last",
    )(*state, kv)


def merge_kernel(a, b, mine, other):
    la = jnp.sum(a[HEAD:, :].astype(F32), axis=0, keepdims=True)
    lb = jnp.sum(b[HEAD:, :].astype(F32), axis=0, keepdims=True)
    top = jnp.maximum(la, lb)
    wa, wb = jnp.exp(la - top), jnp.exp(lb - top)
    inv = 1.0 / (wa + wb)
    total = (a[:HEAD, :].astype(F32) * (wa * inv) + b[:HEAD, :].astype(F32) * (wb * inv)).astype(BF16)
    mine[...] = total[:, :BLK]
    other[...] = total[:, BLK:]


def merge(a, b):
    half = jax.ShapeDtypeStruct((HEAD, BLK), BF16)
    return pl.pallas_call(
        merge_kernel,
        out_shape=(half, half),
        in_specs=[VMEM] * 2,
        out_specs=(VMEM,) * 2,
        cost_estimate=pl.CostEstimate(flops=1 << 18, bytes_accessed=1 << 19, transcendentals=1024),
        compiler_params=vmem(8),
        name="merge",
    )(a, b)


def output_kernel(mine, other, w, *outs):
    first = lax.axis_index("c") == 0
    a, b = (jnp.transpose(ref[...].astype(F32)) for ref in (mine, other))
    rows = jnp.concatenate([jnp.where(first, a, b), jnp.where(first, b, a)], axis=1).astype(BF16)
    for out, shift in zip(outs, NEAR + FAR):
        out[...] = jnp.dot(rows, w[:, target_cols(*shift)], preferred_element_type=F32).astype(BF16)


def target_cols(dx, dy):
    x, yl = lax.axis_index("x"), lax.axis_index("yl")
    target = ((x + dx) % 4) * 2 + (yl + dy) % 2
    return pl.ds(pl.multiple_of(target * BLK, BLK), BLK)


def output(mine, other, w):
    return pl.pallas_call(
        output_kernel,
        out_shape=(jax.ShapeDtypeStruct((BLK, BLK), BF16),) * 8,
        in_specs=[VMEM] * 3,
        out_specs=(VMEM,) * 8,
        cost_estimate=pl.CostEstimate(
            flops=2 * BLK * BLK * 2048, bytes_accessed=3 << 20, transcendentals=0
        ),
        compiler_params=vmem(16),
        name="output",
    )(mine, other, w)


def add_kernel(a0, b0, a1, b1, out0, out1):
    out0[...] = (a0[...].astype(F32) + b0[...].astype(F32)).astype(BF16)
    out1[...] = (a1[...].astype(F32) + b1[...].astype(F32)).astype(BF16)


def add_pairs(a0, b0, a1, b1):
    return pl.pallas_call(
        add_kernel,
        out_shape=(jax.ShapeDtypeStruct(a0.shape, BF16),) * 2,
        in_specs=[VMEM] * 4,
        out_specs=(VMEM,) * 2,
        cost_estimate=pl.CostEstimate(flops=a0.size, bytes_accessed=12 * a0.size, transcendentals=0),
        compiler_params=vmem(8),
        name="add_pairs",
    )(a0, b0, a1, b1)


def sum_kernel(*refs):
    total = refs[0][...].astype(F32)
    for ref in refs[1:-1]:
        total = total + ref[...].astype(F32)
    refs[-1][...] = total.astype(BF16)


def sum_all(terms):
    return pl.pallas_call(
        sum_kernel,
        out_shape=jax.ShapeDtypeStruct(terms[0].shape, BF16),
        in_specs=[VMEM] * len(terms),
        out_specs=VMEM,
        cost_estimate=pl.CostEstimate(
            flops=6 * terms[0].size, bytes_accessed=14 * terms[0].size, transcendentals=0
        ),
        compiler_params=vmem(8),
        name="sum_all",
    )(*terms)


def slots_kernel(*refs):
    terms = refs[:6]
    stream, slot, mixed, rows = refs[6:]
    total = stream[...].astype(F32)
    for term in terms:
        total = total + term[...].astype(F32)
    kept = total.astype(BF16)
    mixed[...] = kept
    ids = lax.broadcasted_iota(jnp.int32, (EXPERTS * CAP, BLK), 0)
    pick = jnp.where(ids == slot[...], 1.0, 0.0).astype(BF16)
    rows[...] = jnp.dot(pick, kept, preferred_element_type=F32).astype(BF16)


def to_slots(terms, stream, slot):
    return pl.pallas_call(
        slots_kernel,
        out_shape=(
            jax.ShapeDtypeStruct((BLK, BLK), BF16),
            jax.ShapeDtypeStruct((EXPERTS * CAP, BLK), BF16),
        ),
        in_specs=[VMEM] * 8,
        out_specs=(VMEM, VMEM),
        cost_estimate=pl.CostEstimate(
            flops=2 * 512 * BLK * BLK, bytes_accessed=2 << 20, transcendentals=0
        ),
        compiler_params=vmem(16),
        name="slots",
    )(*terms, stream, slot)


UNITS = 704
WIDE = 768
SOME = 64


def prepare(blocks, shifts, places, gain, n_s, square):
    def some_rows(i, carry):
        at = pl.ds(pl.multiple_of(i * SOME, SOME), SOME)
        total = None
        for block, shift, cols in zip(blocks, shifts, places):
            v = block[at, :].astype(F32)
            n_s[at, cols] = (v * gain[:, source_rows(*shift)]).astype(BF16)
            total = v * v if total is None else total + v * v
        square[at, :] = jnp.sum(total, axis=1, keepdims=True)
        return carry

    lax.fori_loop(0, blocks[0].shape[0] // SOME, some_rows, 0)


FIRST_OUT = FAR + ((0, 1),)
NEXT_OUT = ((0, 0), (1, 0), (3, 1), (1, 1), (3, 0))
EARLY = 3


def ready_kernel(b0, b1, b2, gain, own, far, w1, w2, n_s, square, sem):
    half = UNITS // 2
    copies = [
        pltpu.make_async_copy(
            src.at[pl.ds(i * half, half), :], dst.at[pl.ds(at + j * half, half), :], sem.at[3 * j + i]
        )
        for i, (dst, at) in enumerate([(w1, 0), (w1, WIDE), (w2, 0)])
        for j, src in enumerate((own, far))
    ]
    for copy in copies:
        copy.start()
    pad = jnp.zeros((WIDE - UNITS, 2048), BF16)
    w1[UNITS:WIDE, :] = pad
    w1[WIDE + UNITS :, :] = pad
    w2[UNITS:, :] = pad
    places = [slice(j * BLK, (j + 1) * BLK) for j in range(EARLY)]
    prepare((b0, b1, b2), NEAR[:EARLY], places, gain, n_s, square)
    for copy in copies:
        copy.wait()


def expert_ready(blocks, gain, own, far):
    rows = blocks[0].shape[0]
    return pl.pallas_call(
        ready_kernel,
        out_shape=(
            jax.ShapeDtypeStruct((2 * WIDE, 2048), BF16),
            jax.ShapeDtypeStruct((WIDE, 2048), BF16),
            jax.ShapeDtypeStruct((rows, EARLY * BLK), BF16),
            jax.ShapeDtypeStruct((rows, 1), F32),
        ),
        in_specs=[VMEM] * 4 + [HBM] * 2,
        out_specs=(VMEM,) * 4,
        scratch_shapes=[pltpu.SemaphoreType.DMA((6,))],
        cost_estimate=pl.CostEstimate(flops=1 << 20, bytes_accessed=18 << 20, transcendentals=0),
        compiler_params=vmem(16),
        name="expert_ready",
    )(*blocks, gain, own, far)


def lower(h_s, w2, outs, shifts):
    def some_rows(i, carry):
        at = pl.ds(pl.multiple_of(i * BLK, BLK), BLK)
        for out, shift in zip(outs, shifts):
            out[at, :] = jnp.dot(
                h_s[at, :], w2[:, target_cols(*shift)], preferred_element_type=F32
            ).astype(BF16)
        return carry

    lax.fori_loop(0, h_s.shape[0] // BLK, some_rows, 0)


def hidden_kernel(*refs):
    blocks = refs[:5]
    gain, w1, w2, early, square, h_s, o0, o1, o2, n_s, r_s = refs[5:]
    for j, shift in enumerate(NEAR[:EARLY]):
        n_s[:, source_rows(*shift)] = early[:, j * BLK : (j + 1) * BLK]
    shifts = NEAR[EARLY:] + FAR
    prepare(blocks, shifts, [source_rows(*shift) for shift in shifts], gain, n_s, r_s)
    factor = lax.rsqrt((square[...] + r_s[...]) * (1.0 / 2048) + NORM_EPS)

    def tile(j, carry):
        cols = pl.ds(pl.multiple_of(j * BLK, BLK), BLK)
        later = pl.ds(pl.multiple_of(WIDE + j * BLK, BLK), BLK)
        g = nt_dot(n_s[...], w1[cols, :]) * factor
        u = nt_dot(n_s[...], w1[later, :]) * factor
        h_s[:, cols] = (g / (1.0 + jnp.exp(-g)) * u).astype(BF16)
        return carry

    lax.fori_loop(0, WIDE // BLK, tile, 0)
    lower(h_s, w2, (o0, o1, o2), FIRST_OUT)


def expert_hidden(blocks, gain, w1, w2, early, square):
    rows = blocks[0].shape[0]
    piece = jax.ShapeDtypeStruct((rows, BLK), BF16)
    return pl.pallas_call(
        hidden_kernel,
        out_shape=(jax.ShapeDtypeStruct((rows, WIDE), BF16), piece, piece, piece),
        in_specs=[VMEM] * 10,
        out_specs=(VMEM,) * 4,
        scratch_shapes=[pltpu.VMEM((rows, 2048), BF16), pltpu.VMEM((rows, 1), F32)],
        cost_estimate=pl.CostEstimate(
            flops=5 * rows * 2048 * WIDE, bytes_accessed=13 << 20, transcendentals=rows * WIDE
        ),
        compiler_params=vmem(16),
        name="expert_hidden",
    )(*blocks, gain, w1, w2, early, square)


def lower_kernel(h_s, w2, *outs):
    lower(h_s, w2, outs, NEXT_OUT)


def expert_lower(h, w2):
    rows = h.shape[0]
    return pl.pallas_call(
        lower_kernel,
        out_shape=(jax.ShapeDtypeStruct((rows, BLK), BF16),) * 5,
        in_specs=[VMEM] * 2,
        out_specs=(VMEM,) * 5,
        cost_estimate=pl.CostEstimate(
            flops=2 * rows * 1536 * WIDE, bytes_accessed=6 << 20, transcendentals=0
        ),
        compiler_params=vmem(16),
        name="expert_lower",
    )(h, w2)


def finish_kernel(mixed, rows, slot, out):
    ids = lax.broadcasted_iota(jnp.int32, (EXPERTS * CAP, BLK), 0)
    pick = jnp.where(ids == slot[...], 1.0, 0.0).astype(BF16)
    out[...] = (mixed[...].astype(F32) + tn_dot(pick, rows[...])).astype(BF16)


def finish(mixed, rows, slot):
    return pl.pallas_call(
        finish_kernel,
        out_shape=jax.ShapeDtypeStruct((BLK, BLK), BF16),
        in_specs=[VMEM] * 3,
        out_specs=VMEM,
        cost_estimate=pl.CostEstimate(
            flops=2 * 512 * BLK * BLK, bytes_accessed=1 << 20, transcendentals=0
        ),
        compiler_params=vmem(8),
        name="finish",
    )(mixed, rows, slot)


def tp_shift(a, dx, dy):
    pairs = [(i * 2 + j, ((i + dx) % 4) * 2 + (j + dy) % 2) for i in range(4) for j in range(2)]
    return lax.ppermute(a, TP, pairs)


def tp_gather(a):
    near = [a] + [tp_shift(a, *s) for s in NEAR[1:]]
    return near + [tp_shift(near[1], 1, 0), tp_shift(near[2], 3, 0)]


def tp_scatter(pieces, waves):
    got = tp_shift(pieces[6], 1, 0), tp_shift(pieces[7], 3, 0)
    beside = tp_shift(pieces[3], *NEAR[3])
    if waves:
        beside, *got = lax.optimization_barrier((beside, *got))
    sums = add_pairs(pieces[1], got[0], pieces[2], got[1])
    straight = [tp_shift(p, *s) for p, s in zip(pieces[4:6], NEAR[4:6])]
    return [pieces[0], beside] + straight + [tp_shift(p, *s) for p, s in zip(sums, NEAR[1:3])]


def swap(a, dy, dc):
    pairs = [(i * 2 + j, (i ^ dy) * 2 + (j ^ dc)) for i in range(2) for j in range(2)]
    return lax.ppermute(a, ("yh", "c"), pairs)


def ring(a, step):
    return lax.ppermute(a, "z", [(i, (i + step) % 8) for i in range(8)])


def attention(blocks, wq, wk, wv, frames, weights):
    acc, rest = project_near(blocks[:6], jnp.concatenate([wk, wv, wq], axis=1))
    own, other = project_far(acc, rest, *blocks[6:], frames)
    kv, q = join(own, swap(other, 0, 1))
    f, b = ring(kv, 1), ring(kv, -1)
    theirs = swap(q, 1, 0)
    weights, kv = lax.optimization_barrier((weights, kv))
    weights = jnp.concatenate(weights, axis=0)
    f, b, theirs, weights = lax.optimization_barrier((f, b, theirs, weights))
    state = None
    for k in range(1, 4):
        if k > 1:
            f, b, weights, *state = lax.optimization_barrier((f, b, weights, *state))
        here = f, b
        if k < 3:
            f, b = ring(f, 1), ring(b, -1)
        else:
            way = jnp.where(lax.axis_index("c") == 0, f, b)
            hops = [(i * 2 + c, (i + (-1 if c else 1)) % 8 * 2 + c) for i in range(8) for c in range(2)]
            far = lax.ppermute(way, ("z", "c"), hops)
        state = step(k, state, *here) if state else first(q, theirs, kv, *here)
    far_weights = lax.ppermute(weights, "c", [(0, 1), (1, 0)])
    mine, theirs = last(state, far)
    theirs, far_weights = lax.optimization_barrier((swap(theirs, 1, 0), far_weights))
    mine, other = merge(mine, theirs)
    return mine, swap(other, 0, 1), weights, far_weights


def shards(stream, frames, fidelity, wq, wk, wv, wo, gain, gate, up, down):
    route = fidelity[:, 0]
    spot = lax.iota(jnp.int32, BLK)
    same = (route[:, None] == route[None, :]) & (spot[None, :] < spot[:, None])
    slot = (route * CAP + jnp.sum(same.astype(jnp.int32), axis=1))[None, :]
    gain = gain[None, :]

    expert_weights = (gate[0].T, up[0].T, down[0])
    mine, other, own, far = attention(tp_gather(stream), wq, wk, wv, frames[None, :], expert_weights)
    mixed, rows = to_slots(tp_scatter(output(mine, other, wo), False), stream, slot)

    sent = lax.all_to_all(rows.reshape(EXPERTS, CAP, BLK), CHIPS, 0, 0, tiled=True)
    blocks = tp_gather(sent.reshape(EXPERTS * CAP, BLK))
    w1, w2, *early = expert_ready(blocks[:EARLY], gain, own, far)
    h, *lowered = expert_hidden(blocks[EARLY:], gain, w1, w2, *early)
    lowered = dict(zip(FIRST_OUT + NEXT_OUT, [*lowered, *expert_lower(h, w2)]))
    summed = sum_all(tp_scatter([lowered[shift] for shift in NEAR + FAR], True))
    back = lax.all_to_all(summed.reshape(EXPERTS, CAP, BLK), CHIPS, 0, 0, tiled=True)
    return finish(mixed, back.reshape(EXPERTS * CAP, BLK), slot)


def solution(mesh):
    axes = ("z", "yh", "c", "x", "yl")
    fine = Mesh(np.asarray(mesh.devices).reshape(8, 2, 2, 4, 2), axes)
    return jax.shard_map(
        shards,
        mesh=fine,
        in_specs=(
            P(SEQ, TP),
            P(SEQ),
            P(SEQ, None),
            P(None, TP),
            P(None, TP),
            P(None, TP),
            P(TP, None),
            P(),
            P(SEQ, None, TP),
            P(SEQ, None, TP),
            P(SEQ, TP, None),
        ),
        out_specs=P(SEQ, TP),
        check_vma=False,
    )
```
